256 devices in a mesh: seq: 16 (over z, x_lo), head: 8 (over y, x_hi), pair: 2 (over core).
Axes of the slice: x: 4 (x_hi: 2, x_lo: 2; x = x_hi * 2 + x_lo), y: 4, z: 8, core: 2. Of those that a mesh axis runs over, the one named last changes fastest.
Arguments:
- queries: bfloat16 [12288, 5120], P(('pair', 'seq'), 'head'), parts along dimension 0, may hold values from -12 to 12
- keys: bfloat16 [12288, 5120], P(('pair', 'seq'), 'head'), parts along dimension 0, may hold values from -12 to 12
- values: bfloat16 [12288, 5120], P(('pair', 'seq'), 'head'), parts along dimension 0, may hold values from -6 to 6
- cross_query: bfloat16 [12288, 5120], P(('pair', 'seq'), 'head'), parts along dimension 0, may hold values from -12 to 12
- text_keys: bfloat16 [1024, 5120], P('pair', 'head'), parts along dimension 0, may hold values from -12 to 12
- text_values: bfloat16 [1024, 5120], P('pair', 'head'), parts along dimension 0, may hold values from -6 to 6
- out_weight: bfloat16 [5120, 5120], P('head'), may hold values from -0.078125 to 0.078125
- block_list: int32 [48, 18], replicated, may hold values from 0 to 47, as said below
- block_count: int32 [48], replicated, may hold values from 6 to 18, as said below
Outputs:
- block_stream: bfloat16 [12288, 5120], P(('pair', 'seq'), 'head'), parts along dimension 0
- cross_heads: bfloat16 [12288, 5120], P(('pair', 'seq'), 'head'), parts along dimension 0
The draws below stay inside these ranges and needn't reach their ends.
There are 2 independent parts, one for each index of `pair`. The reference program is written for one: setup_inputs(seed, part) draws one part's arguments, and reference() takes and returns one part's arrays. A program takes and returns all parts, laid end to end along the dimension named above; an argument that names none is the same for every part. Nothing has to cross between parts.
Inputs may be any that keep to these rules, and one draw needn't show every extreme that they name: `block_list`: each row holds 18 distinct key blocks; its first block_count entries include every block of frame groups f - 1, f and f + 1 (those that exist) and of group 0, with f = row // 3 and a frame group being 3 consecutive blocks. `block_count`: some row uses all 18 entries.
All inputs are finite; a program needn't handle non-finite values.
Results may differ from the reference program's by a relative error of at most 0.029.
Values may be sent and summed in bfloat16 or wider, within the bound.
No kernel may reach another device: no remote copies, remote signals or barrier semaphores. Data moves between devices by JAX's collectives and lax.ppermute only.
A program may use at most 128 MiB of HBM per device.

```python
import jax
import jax.numpy as jnp
from jax import lax

D = 5120
HEADS = 40
DH = 128
TEXT = 512
BLK = 128
FB = 3
KB = 48
NB = 18
S = 6144
HD = 5120
N_HEAD = 8


def base_draw(key, salt, count):
    return jax.random.normal(jax.random.fold_in(key, salt), (count, HEADS * DH))


def draw_queries(key, part):
    field = base_draw(key, 10, S)
    return field.astype(jnp.bfloat16)


def draw_keys(key, part):
    field = base_draw(key, 11, S)
    return field.astype(jnp.bfloat16)


def draw_cross_query(key, part):
    field = base_draw(key, 12, S)
    return field.astype(jnp.bfloat16)


def draw_text_keys(key, part):
    field = base_draw(key, 13, TEXT)
    return field.astype(jnp.bfloat16)


def mask_parts(key):
    blocks = jnp.arange(KB, dtype=jnp.int32)
    frame = blocks // FB
    needed = (jnp.abs(frame[:, None] - frame[None, :]) <= 1) | (frame[None, :] == 0)
    noise = jax.random.randint(jax.random.fold_in(key, 21), (KB, KB), 0, 4096)
    scored = (noise + 8192 * needed.astype(jnp.int32)) * KB + blocks[None, :]
    unused, picked = lax.top_k(scored, NB)
    needed_count = jnp.sum(needed.astype(jnp.int32), axis=1)
    extra = jax.random.randint(jax.random.fold_in(key, 22), (KB,), 0, NB + 1 - needed_count)
    count = needed_count + extra
    fullest = jax.random.randint(jax.random.fold_in(key, 23), (), 0, KB)
    count = jnp.where(blocks == fullest, NB, count)
    return (picked.astype(jnp.int32), count.astype(jnp.int32))


def draw_block_list(key, part):
    return mask_parts(key)[0]


def draw_block_count(key, part):
    return mask_parts(key)[1]


def levels(rng, shape, pieces, smallest, top_value):
    loudness, own = 1.0, jax.random.fold_in(rng, 6)
    for position, shards_of in pieces:
        draws = jnp.exp(jax.random.uniform(jax.random.fold_in(own, position), (shards_of,), jnp.float32, smallest / len(pieces), top_value / len(pieces)))
        loudness = loudness * jnp.repeat(draws, shape[position] // shards_of).reshape([-1 if axis == position else 1 for axis in range(len(shape))])
    return loudness


def gaussian(own_key, dims, spread, bound, cuts=(), kind=jnp.bfloat16):
    level = levels(own_key, dims, cuts, -0.22, 0.18) if cuts else 1.0
    drawn = jax.random.normal(own_key, dims, jnp.float32) * spread * level
    return jnp.minimum(jnp.maximum(drawn, -bound), bound).astype(kind)


def setup_inputs(seed: int = 0, part: int = 0) -> dict:
    streams_of = jax.random.split(jax.random.key(seed), 10)
    own_keys = jax.random.split(jax.random.fold_in(streams_of[9], part), 10)
    queries = draw_queries(jax.random.fold_in(jax.random.fold_in(streams_of[9], part), 71), part)
    keys = draw_keys(jax.random.fold_in(jax.random.fold_in(streams_of[9], part), 71), part)
    values = gaussian(own_keys[2], (S, HD), 1.0, 6.0, ((0, 16), (1, 8)))
    cross_query = draw_cross_query(jax.random.fold_in(jax.random.fold_in(streams_of[9], part), 71), part)
    text_keys = draw_text_keys(jax.random.fold_in(jax.random.fold_in(streams_of[9], part), 71), part)
    text_values = gaussian(own_keys[5], (TEXT, HD), 1.0, 6.0, ((1, 8),))
    out_weight = gaussian(streams_of[6], (HD, D), HD ** -0.5, 0.078125, ((0, 8),))
    block_list = draw_block_list(jax.random.fold_in(streams_of[9], 71), part)
    block_count = draw_block_count(jax.random.fold_in(streams_of[9], 71), part)
    return {"queries": queries, "keys": keys, "values": values, "cross_query": cross_query, "text_keys": text_keys, "text_values": text_values, "out_weight": out_weight, "block_list": block_list, "block_count": block_count}


def allowed_table(block_list, block_count):
    slots = jnp.arange(block_list.shape[1], dtype=jnp.int32)
    targets = jnp.arange(block_list.shape[0], dtype=jnp.int32)
    hit = (block_list[:, :, None] == targets[None, None, :]) & (slots[None, :, None] < block_count[:, None, None])
    return jnp.any(hit, axis=1).astype(jnp.int32)


def attend_head(query_head, key_head, value_head, token_mask, scale):
    score = jnp.dot(query_head, key_head.T, preferred_element_type=jnp.float32) * scale
    score = jnp.where(token_mask, score, -1e30)
    row_max = jnp.max(score, axis=1, keepdims=True)
    weight = jnp.where(token_mask, jnp.exp(score - row_max), 0.0)
    total = jnp.sum(weight, axis=1, keepdims=True)
    summed = jnp.dot(weight.astype(jnp.bfloat16), value_head, preferred_element_type=jnp.float32)
    return summed / total


def split_heads(array):
    return array.reshape(array.shape[0], HEADS, DH).transpose(1, 0, 2)


def reference(queries, keys, values, cross_query, text_keys, text_values, out_weight, block_list, block_count):
    scale = DH ** -0.5
    allowed = allowed_table(block_list, block_count) > 0
    token_mask = jnp.repeat(jnp.repeat(allowed, BLK, axis=0), BLK, axis=1)

    def self_head(items):
        return attend_head(items[0], items[1], items[2], token_mask, scale)

    self_out = lax.map(self_head, (split_heads(queries), split_heads(keys), split_heads(values)))
    self_heads = self_out.transpose(1, 0, 2).reshape(S, HD).astype(jnp.bfloat16)

    text_mask = jnp.ones((S, TEXT), dtype=bool)

    def cross_head(items):
        return attend_head(items[0], items[1], items[2], text_mask, scale)

    cross_out = lax.map(cross_head, (split_heads(cross_query), split_heads(text_keys), split_heads(text_values)))
    cross_heads = cross_out.transpose(1, 0, 2).reshape(S, HD).astype(jnp.bfloat16)

    group = HD // N_HEAD
    stream = jnp.zeros((S, D), jnp.float32)
    for index in range(N_HEAD):
        partial_sum = jnp.dot(self_heads[:, index * group:(index + 1) * group], out_weight[index * group:(index + 1) * group], preferred_element_type=jnp.float32)
        partial_sum = lax.optimization_barrier(partial_sum.astype(jnp.bfloat16)).astype(jnp.float32)
        stream = stream + partial_sum
    return stream.astype(jnp.bfloat16), cross_heads
```

```python
import functools
import math

import jax
import jax.numpy as jnp
from jax import lax
from jax.experimental import pallas as pl
from jax.experimental.pallas import tpu as pltpu
from jax.sharding import PartitionSpec as P

DH = 128
BLK = 128
FB = 3
ROWS = FB * BLK
MAX_EXTRA = 12
IN_FLIGHT = 3
NEG = -1e30
TO_EXP2 = DH ** (-0.5) * math.log2(math.e)
NT = (((1,), (1,)), ((), ()))


def extra_blocks(block_list, block_count):
    slots = block_list.shape[1]
    row_frame = (jnp.arange(block_list.shape[0], dtype=jnp.int32) // FB)[:, None]
    frame = block_list // FB
    near = (jnp.abs(frame - row_frame) <= 1) | (frame == 0)
    listed = jnp.arange(slots, dtype=jnp.int32)[None, :] < block_count[:, None]
    extra = (listed & ~near).astype(jnp.int32)
    before = jnp.tril(jnp.ones((slots, slots), jnp.int32), -1)
    place = jnp.sum(extra[:, None, :] * before[None], axis=2)
    wanted = jnp.arange(MAX_EXTRA, dtype=jnp.int32)
    hit = (place[:, :, None] == wanted[None, None, :]) & (extra[:, :, None] > 0)
    blocks = jnp.sum(jnp.where(hit, block_list[:, :, None], 0), axis=1)
    return blocks.astype(jnp.int32), jnp.sum(extra, axis=1).astype(jnp.int32)


def pack_kernel(side_ref, q_ref, k_ref, v_ref, qa, qb, qc, qpa, qpb, kva, kvb, kvc, kvpa, kvpb):
    side = side_ref[0]
    mine = side * 2 * DH
    theirs = (1 - side) * 2 * DH
    heads = ((mine, qa, kva), (mine + DH, qb, kvb), (4 * DH, qc, kvc), (theirs, qpa, kvpa), (theirs + DH, qpb, kvpb))
    for offset, q_out, kv_out in heads:
        columns = pl.ds(pl.multiple_of(offset, DH), DH)
        q_out[...] = q_ref[:, columns]
        kv_out[0:ROWS, :] = k_ref[:, columns]
        kv_out[ROWS : 2 * ROWS, :] = v_ref[:, columns]


def pack(side, queries, keys, values):
    smem = pl.BlockSpec(memory_space=pltpu.SMEM)
    vmem = pl.BlockSpec(memory_space=pltpu.VMEM)
    small = jax.ShapeDtypeStruct((ROWS, DH), jnp.bfloat16)
    pair = jax.ShapeDtypeStruct((2 * ROWS, DH), jnp.bfloat16)
    return pl.pallas_call(
        pack_kernel,
        out_shape=[small] * 5 + [pair] * 5,
        in_specs=[smem, vmem, vmem, vmem],
        out_specs=[vmem] * 10,
        cost_estimate=pl.CostEstimate(flops=0, bytes_accessed=6 * ROWS * 5 * DH * 2, transcendentals=0),
        name="pack",
    )(side, queries, keys, values)


def attend_frame(frame, last, blocks_ref, count_ref, q_ref, o_ref, k_s, v_s, near_s, far_s, top_s, total_s, sum_s):
    low = jnp.maximum(frame - 1, 1)
    nears = jnp.minimum(frame + 1, last) - low + 2
    first_row = frame * FB
    counts = [count_ref[first_row + r] for r in range(FB)]
    pairs = (jnp.maximum(jnp.maximum(counts[0], counts[1]), counts[2]) + 1) // 2

    def near_rows(w):
        key_frame = jnp.where(w == 0, 0, low + w - 1)
        return pl.ds(pl.multiple_of(key_frame * ROWS, ROWS), ROWS)

    def far_rows(r, e):
        return pl.ds(pl.multiple_of(blocks_ref[first_row + r, e] * BLK, BLK), BLK)

    top_s[...] = jnp.full_like(top_s, NEG)

    def near_scores(w, carry):
        score = lax.dot_general(q_ref[...], k_s[near_rows(w), :], NT, preferred_element_type=jnp.float32)
        near_s[w] = score
        best = jnp.maximum(jnp.maximum(score[:, :BLK], score[:, BLK : 2 * BLK]), score[:, 2 * BLK :])
        top_s[...] = jnp.maximum(top_s[...], best)
        return carry

    lax.fori_loop(0, nears, near_scores, 0)

    def far_scores(i, carry):
        for r in range(FB):
            rows = slice(r * BLK, (r + 1) * BLK)
            best = top_s[rows, :]
            for j in range(2):
                e = 2 * i + j
                score = lax.dot_general(
                    q_ref[rows, :], k_s[far_rows(r, e), :], NT, preferred_element_type=jnp.float32
                )
                score = jnp.where(e < counts[r], score, NEG)
                far_s[r, e] = score
                best = jnp.maximum(best, score)
            top_s[rows, :] = best
        return carry

    lax.fori_loop(0, pairs, far_scores, 0)
    top_s[...] = jnp.broadcast_to(jnp.max(top_s[...], axis=1, keepdims=True) * TO_EXP2, top_s.shape)
    total_s[...] = jnp.zeros_like(total_s)
    sum_s[...] = jnp.zeros_like(sum_s)

    def near_weights(w, carry):
        top = top_s[...]
        weights = [jnp.exp2(near_s[w, :, c * BLK : (c + 1) * BLK] * TO_EXP2 - top) for c in range(FB)]
        total_s[...] += weights[0] + weights[1] + weights[2]
        weight = jnp.concatenate([p.astype(jnp.bfloat16) for p in weights], axis=1)
        sum_s[...] += jnp.dot(weight, v_s[near_rows(w), :], preferred_element_type=jnp.float32)
        return carry

    lax.fori_loop(0, nears, near_weights, 0)

    def far_weights(i, carry):
        for r in range(FB):
            rows = slice(r * BLK, (r + 1) * BLK)
            top = top_s[rows, :]
            weights = [jnp.exp2(far_s[r, 2 * i + j] * TO_EXP2 - top) for j in range(2)]
            total_s[rows, :] += weights[0] + weights[1]
            part = jnp.dot(
                weights[0].astype(jnp.bfloat16), v_s[far_rows(r, 2 * i), :], preferred_element_type=jnp.float32
            )
            part += jnp.dot(
                weights[1].astype(jnp.bfloat16), v_s[far_rows(r, 2 * i + 1), :], preferred_element_type=jnp.float32
            )
            sum_s[rows, :] += part
        return carry

    lax.fori_loop(0, pairs, far_weights, 0)
    o_ref[...] = (sum_s[...] / jnp.sum(total_s[...], axis=1, keepdims=True)).astype(o_ref.dtype)


def attend_kernel(frames_in, pieces_in, place_ref, query_frame_ref, blocks_ref, count_ref, *refs):
    q_refs = refs[:frames_in]
    piece_refs = refs[frames_in : frames_in + pieces_in]
    o_refs = refs[frames_in + pieces_in : 2 * frames_in + pieces_in]
    k_s, v_s, near_s, far_s, top_s, total_s, sum_s, sems = refs[2 * frames_in + pieces_in :]
    copies = []
    for n, piece in enumerate(piece_refs):
        rows = pl.ds(pl.multiple_of(place_ref[n] * ROWS, ROWS), ROWS)
        copies.append(pltpu.make_async_copy(piece.at[0:ROWS, :], k_s.at[rows, :], sems.at[0, n]))
        copies.append(pltpu.make_async_copy(piece.at[ROWS : 2 * ROWS, :], v_s.at[rows, :], sems.at[1, n]))
    for copy in copies:
        copy.start()
    for copy in copies:
        copy.wait()
    for q_ref, o_ref, n in zip(q_refs, o_refs, range(frames_in)):
        attend_frame(
            query_frame_ref[n], pieces_in - 1, blocks_ref, count_ref, q_ref, o_ref,
            k_s, v_s, near_s, far_s, top_s, total_s, sum_s,
        )


def attend(queries, pieces, place, query_frames, blocks, counts):
    frames_in, pieces_in = len(queries), len(pieces)
    smem = pl.BlockSpec(memory_space=pltpu.SMEM)
    vmem = pl.BlockSpec(memory_space=pltpu.VMEM)
    stay = pl.BlockSpec(memory_space=pl.ANY)
    tokens = pieces_in * ROWS
    stat = pltpu.VMEM((ROWS, BLK), jnp.float32)
    elements = frames_in * ROWS * 18 * BLK
    return pl.pallas_call(
        functools.partial(attend_kernel, frames_in, pieces_in),
        out_shape=[jax.ShapeDtypeStruct((ROWS, DH), jnp.bfloat16)] * frames_in,
        in_specs=[smem] * 4 + [vmem] * frames_in + [stay] * pieces_in,
        out_specs=[vmem] * frames_in,
        scratch_shapes=[
            pltpu.VMEM((tokens, DH), jnp.bfloat16),
            pltpu.VMEM((tokens, DH), jnp.bfloat16),
            pltpu.VMEM((4, ROWS, ROWS), jnp.float32),
            pltpu.VMEM((FB, MAX_EXTRA, BLK, BLK), jnp.float32),
            stat,
            stat,
            stat,
            pltpu.SemaphoreType.DMA((2, pieces_in)),
        ],
        compiler_params=pltpu.CompilerParams(vmem_limit_bytes=24 << 20),
        cost_estimate=pl.CostEstimate(
            flops=4 * elements * DH, bytes_accessed=tokens * DH * 4, transcendentals=elements
        ),
        name="attend",
    )(place, query_frames, blocks, counts, *queries, *pieces)


def cross_kernel(q_ref, k_ref, v_ref, o_ref):
    for h in range(q_ref.shape[1] // DH):
        columns = slice(h * DH, (h + 1) * DH)
        score = lax.dot_general(q_ref[:, columns], k_ref[:, columns], NT, preferred_element_type=jnp.float32)
        top = jnp.max(score, axis=1, keepdims=True) * TO_EXP2
        weight = jnp.exp2(score * TO_EXP2 - top)
        total = jnp.sum(weight, axis=1, keepdims=True)
        part = jnp.dot(weight.astype(jnp.bfloat16), v_ref[:, columns], preferred_element_type=jnp.float32)
        o_ref[:, columns] = (part / total).astype(o_ref.dtype)


def cross(cross_query, text_keys, text_values):
    vmem = pl.BlockSpec(memory_space=pltpu.VMEM)
    elements = cross_query.shape[0] * cross_query.shape[1] // DH * text_keys.shape[0]
    return pl.pallas_call(
        cross_kernel,
        out_shape=jax.ShapeDtypeStruct(cross_query.shape, jnp.bfloat16),
        in_specs=[vmem] * 3,
        out_specs=vmem,
        compiler_params=pltpu.CompilerParams(vmem_limit_bytes=24 << 20),
        cost_estimate=pl.CostEstimate(
            flops=4 * elements * DH, bytes_accessed=4 * cross_query.size, transcendentals=elements
        ),
        name="cross",
    )(cross_query, text_keys, text_values)


def body(n_seq, n_head, queries, keys, values, cross_query, text_keys, text_values, out_weight, block_list, block_count):
    n_z = n_seq // 2
    half = n_z // 2
    seq = lax.axis_index("seq")
    z, side = seq // 2, seq % 2
    blocks, counts = extra_blocks(block_list, block_count)

    def z_shift(step):
        return [(s, (s // 2 + step) % n_z * 2 + s % 2) for s in range(n_seq)]

    swap = [(s, s ^ 1) for s in range(n_seq)]

    def to_other(array):
        return lax.ppermute(array, "seq", swap)

    sent = {1: [], -1: []}

    def hop(array, way):
        done = sent[way]
        if len(done) >= IN_FLIGHT:
            array, done[-IN_FLIGHT] = lax.optimization_barrier((array, done[-IN_FLIGHT]))
        got = lax.ppermute(array, "seq", z_shift(way))
        done.append(got)
        return got

    def all_planes(starts):
        found = [{0: array} for array, _ in starts]
        for step in range(1, half + 1):
            for place, (_, last_way) in zip(found, starts):
                for way in (1, -1):
                    if step < half or way == last_way:
                        place[way * step % n_z] = hop(place[way * (step - 1) % n_z], way)
        return [[place[d] for d in range(n_z)] for place in found]

    qa, qb, qc, qpa, qpb, kva, kvb, kvc, kvpa, kvpb = pack(side.reshape(1), queries, keys, values)
    kva_other, kvb_other = to_other(kvpa), to_other(kvpb)
    qa_other, qb_other = to_other(qpa), to_other(qpb)

    below = (z - jnp.arange(n_z, dtype=jnp.int32)) % n_z
    place = jnp.concatenate([below * 2 + side, below * 2 + 1 - side])
    query_frames = jnp.stack([seq, seq + 1 - 2 * side])

    (mine_c,) = all_planes([(kvc, 1)])
    other_c = [to_other(piece) for piece in mine_c]
    mine_a, other_a = all_planes([(kva, -1), (kva_other, 1)])
    mine_b, other_b = all_planes([(kvb, -1), (kvb_other, 1)])

    cross_heads = cross(cross_query, text_keys, text_values)

    (oc,) = attend([qc], mine_c + other_c, place, query_frames, blocks, counts)
    oa, oa_send = attend([qa, qa_other], mine_a + other_a, place, query_frames, blocks, counts)
    ob, ob_send = attend([qb, qb_other], mine_b + other_b, place, query_frames, blocks, counts)
    oa_got, ob_got = to_other(oa_send), to_other(ob_send)
    mine = jnp.concatenate([oa, ob], axis=1)
    got = jnp.concatenate([oa_got, ob_got], axis=1)
    first = jnp.where(side == 0, mine, got)
    second = jnp.where(side == 0, got, mine)
    self_heads = jnp.concatenate([first, second, oc], axis=1)

    width = out_weight.shape[1] // n_head
    head = lax.axis_index("head")
    n_y = n_head // 2
    total = None
    for dy in (2, 1, 3, 0):
        for dx in (1, 0):
            target = (head // 2 + dy) % n_y * 2 + (head % 2) ^ dx
            weight = lax.dynamic_slice_in_dim(out_weight, target * width, width, 1)
            term = jnp.dot(self_heads, weight, preferred_element_type=jnp.float32).astype(jnp.bfloat16)
            if dy or dx:
                route = [(g, ((g // 2 + dy) % n_y * 2 + (g % 2)) ^ dx) for g in range(n_head)]
                term = lax.ppermute(term, "head", route)
            term = term.astype(jnp.float32)
            total = term if total is None else total + term
    return total.astype(jnp.bfloat16), cross_heads


def solution(mesh):
    rows = P(("pair", "seq"), "head")
    text = P("pair", "head")
    return jax.shard_map(
        functools.partial(body, mesh.shape["seq"], mesh.shape["head"]),
        mesh=mesh,
        in_specs=(rows, rows, rows, rows, text, text, P("head", None), P(), P()),
        out_specs=(rows, rows),
        check_vma=False,
    )
```

```python
import functools
import math

import jax
import jax.numpy as jnp
from jax import lax
from jax.experimental import pallas as pl
from jax.experimental.pallas import tpu as pltpu
from jax.sharding import PartitionSpec as P

DH = 128
BLK = 128
FB = 3
ROWS = FB * BLK
MAX_EXTRA = 12
IN_FLIGHT = 3
ATTEND_VMEM = 16 << 20
NEG = -1e30
TO_EXP2 = DH ** (-0.5) * math.log2(math.e)
NT = (((1,), (1,)), ((), ()))


def extra_blocks(block_list, block_count):
    slots = block_list.shape[1]
    row_frame = (jnp.arange(block_list.shape[0], dtype=jnp.int32) // FB)[:, None]
    frame = block_list // FB
    near = (jnp.abs(frame - row_frame) <= 1) | (frame == 0)
    listed = jnp.arange(slots, dtype=jnp.int32)[None, :] < block_count[:, None]
    extra = (listed & ~near).astype(jnp.int32)
    before = jnp.tril(jnp.ones((slots, slots), jnp.int32), -1)
    place = jnp.sum(extra[:, None, :] * before[None], axis=2)
    wanted = jnp.arange(MAX_EXTRA, dtype=jnp.int32)
    hit = (place[:, :, None] == wanted[None, None, :]) & (extra[:, :, None] > 0)
    blocks = jnp.sum(jnp.where(hit, block_list[:, :, None], 0), axis=1)
    return blocks.astype(jnp.int32), jnp.sum(extra, axis=1).astype(jnp.int32)


def pack_kernel(side_ref, q_ref, k_ref, v_ref, qa, qb, qc, qpa, qpb, kva, kvb, kvc, kvpa, kvpb):
    side = side_ref[0]
    mine = side * 2 * DH
    theirs = (1 - side) * 2 * DH
    heads = ((mine, qa, kva), (mine + DH, qb, kvb), (4 * DH, qc, kvc), (theirs, qpa, kvpa), (theirs + DH, qpb, kvpb))
    for offset, q_out, kv_out in heads:
        columns = pl.ds(pl.multiple_of(offset, DH), DH)
        q_out[...] = q_ref[:, columns]
        kv_out[0:ROWS, :] = k_ref[:, columns]
        kv_out[ROWS : 2 * ROWS, :] = v_ref[:, columns]


def pack(side, queries, keys, values):
    smem = pl.BlockSpec(memory_space=pltpu.SMEM)
    vmem = pl.BlockSpec(memory_space=pltpu.VMEM)
    small = jax.ShapeDtypeStruct((ROWS, DH), jnp.bfloat16)
    pair = jax.ShapeDtypeStruct((2 * ROWS, DH), jnp.bfloat16)
    return pl.pallas_call(
        pack_kernel,
        out_shape=[small] * 5 + [pair] * 5,
        in_specs=[smem, vmem, vmem, vmem],
        out_specs=[vmem] * 10,
        cost_estimate=pl.CostEstimate(flops=0, bytes_accessed=6 * ROWS * 5 * DH * 2, transcendentals=0),
        name="pack",
    )(side, queries, keys, values)


def attend_frame(frame, last, blocks_ref, count_ref, q_ref, o_ref, k_s, v_s, near_s, far_s, top_s, total_s, sum_s):
    low = jnp.maximum(frame - 1, 1)
    nears = jnp.minimum(frame + 1, last) - low + 2
    first_row = frame * FB
    counts = [count_ref[first_row + r] for r in range(FB)]
    pairs = (jnp.maximum(jnp.maximum(counts[0], counts[1]), counts[2]) + 1) // 2

    def near_rows(w):
        key_frame = jnp.where(w == 0, 0, low + w - 1)
        return pl.ds(pl.multiple_of(key_frame * ROWS, ROWS), ROWS)

    def far_rows(r, e):
        return pl.ds(pl.multiple_of(blocks_ref[first_row + r, e] * BLK, BLK), BLK)

    top_s[...] = jnp.full_like(top_s, NEG)

    def near_scores(w, carry):
        score = lax.dot_general(q_ref[...], k_s[near_rows(w), :], NT, preferred_element_type=jnp.float32)
        near_s[w] = score
        best = jnp.maximum(jnp.maximum(score[:, :BLK], score[:, BLK : 2 * BLK]), score[:, 2 * BLK :])
        top_s[...] = jnp.maximum(top_s[...], best)
        return carry

    lax.fori_loop(0, nears, near_scores, 0)

    def far_scores(i, carry):
        for r in range(FB):
            rows = slice(r * BLK, (r + 1) * BLK)
            best = top_s[rows, :]
            for j in range(2):
                e = 2 * i + j
                score = lax.dot_general(
                    q_ref[rows, :], k_s[far_rows(r, e), :], NT, preferred_element_type=jnp.float32
                )
                score = jnp.where(e < counts[r], score, NEG)
                far_s[r, e] = score
                best = jnp.maximum(best, score)
            top_s[rows, :] = best
        return carry

    lax.fori_loop(0, pairs, far_scores, 0)
    top_s[...] = jnp.broadcast_to(jnp.max(top_s[...], axis=1, keepdims=True) * TO_EXP2, top_s.shape)
    total_s[...] = jnp.zeros_like(total_s)
    sum_s[...] = jnp.zeros_like(sum_s)

    def near_weights(w, carry):
        top = top_s[...]
        weights = [jnp.exp2(near_s[w, :, c * BLK : (c + 1) * BLK] * TO_EXP2 - top) for c in range(FB)]
        total_s[...] += weights[0] + weights[1] + weights[2]
        weight = jnp.concatenate([p.astype(jnp.bfloat16) for p in weights], axis=1)
        sum_s[...] += jnp.dot(weight, v_s[near_rows(w), :], preferred_element_type=jnp.float32)
        return carry

    lax.fori_loop(0, nears, near_weights, 0)

    def far_weights(i, carry):
        for r in range(FB):
            rows = slice(r * BLK, (r + 1) * BLK)
            top = top_s[rows, :]
            weights = [jnp.exp2(far_s[r, 2 * i + j] * TO_EXP2 - top) for j in range(2)]
            total_s[rows, :] += weights[0] + weights[1]
            part = jnp.dot(
                weights[0].astype(jnp.bfloat16), v_s[far_rows(r, 2 * i), :], preferred_element_type=jnp.float32
            )
            part += jnp.dot(
                weights[1].astype(jnp.bfloat16), v_s[far_rows(r, 2 * i + 1), :], preferred_element_type=jnp.float32
            )
            sum_s[rows, :] += part
        return carry

    lax.fori_loop(0, pairs, far_weights, 0)
    o_ref[...] = (sum_s[...] / jnp.sum(total_s[...], axis=1, keepdims=True)).astype(o_ref.dtype)


def attend_kernel(frames_in, pieces_in, place_ref, query_frame_ref, blocks_ref, count_ref, *refs):
    q_refs = refs[:frames_in]
    piece_refs = refs[frames_in : frames_in + pieces_in]
    o_refs = refs[frames_in + pieces_in : 2 * frames_in + pieces_in]
    q_s, o_s, k_s, v_s, near_s, far_s, top_s, total_s, sum_s = refs[2 * frames_in + pieces_in :]
    for n, piece in enumerate(piece_refs):
        rows = pl.ds(pl.multiple_of(place_ref[n] * ROWS, ROWS), ROWS)
        k_s[rows, :] = piece[0:ROWS, :]
        v_s[rows, :] = piece[ROWS : 2 * ROWS, :]
    for n in range(frames_in):
        q_s[n] = q_refs[n][...]

    def one(n, carry):
        attend_frame(
            query_frame_ref[n], pieces_in - 1, blocks_ref, count_ref, q_s.at[n], o_s.at[n],
            k_s, v_s, near_s, far_s, top_s, total_s, sum_s,
        )
        return carry

    lax.fori_loop(0, frames_in, one, 0)
    for n in range(frames_in):
        o_refs[n][...] = o_s[n]


def attend(queries, pieces, place, query_frames, blocks, counts):
    frames_in, pieces_in = len(queries), len(pieces)
    smem = pl.BlockSpec(memory_space=pltpu.SMEM)
    vmem = pl.BlockSpec(memory_space=pltpu.VMEM)
    tokens = pieces_in * ROWS
    stat = pltpu.VMEM((ROWS, BLK), jnp.float32)
    elements = frames_in * ROWS * 18 * BLK
    return pl.pallas_call(
        functools.partial(attend_kernel, frames_in, pieces_in),
        out_shape=[jax.ShapeDtypeStruct((ROWS, DH), jnp.bfloat16)] * frames_in,
        in_specs=[smem] * 4 + [vmem] * (frames_in + pieces_in),
        out_specs=[vmem] * frames_in,
        scratch_shapes=[
            pltpu.VMEM((frames_in, ROWS, DH), jnp.bfloat16),
            pltpu.VMEM((frames_in, ROWS, DH), jnp.bfloat16),
            pltpu.VMEM((tokens, DH), jnp.bfloat16),
            pltpu.VMEM((tokens, DH), jnp.bfloat16),
            pltpu.VMEM((4, ROWS, ROWS), jnp.float32),
            pltpu.VMEM((FB, MAX_EXTRA, BLK, BLK), jnp.float32),
            stat,
            stat,
            stat,
        ],
        compiler_params=pltpu.CompilerParams(vmem_limit_bytes=ATTEND_VMEM),
        cost_estimate=pl.CostEstimate(
            flops=20 * elements * DH, bytes_accessed=tokens * DH * 4, transcendentals=elements
        ),
        name="attend",
    )(place, query_frames, blocks, counts, *queries, *pieces)


def cross_kernel(q_ref, k_ref, v_ref, o_ref):
    def one(h, carry):
        columns = pl.ds(pl.multiple_of(h * DH, DH), DH)
        score = lax.dot_general(q_ref[:, columns], k_ref[:, columns], NT, preferred_element_type=jnp.float32)
        top = jnp.max(score, axis=1, keepdims=True) * TO_EXP2
        weight = jnp.exp2(score * TO_EXP2 - top)
        total = jnp.sum(weight, axis=1, keepdims=True)
        part = jnp.dot(weight.astype(jnp.bfloat16), v_ref[:, columns], preferred_element_type=jnp.float32)
        o_ref[:, columns] = (part / total).astype(o_ref.dtype)
        return carry

    lax.fori_loop(0, q_ref.shape[1] // DH, one, 0)


def cross(cross_query, text_keys, text_values):
    vmem = pl.BlockSpec(memory_space=pltpu.VMEM)
    elements = cross_query.shape[0] * cross_query.shape[1] // DH * text_keys.shape[0]
    return pl.pallas_call(
        cross_kernel,
        out_shape=jax.ShapeDtypeStruct(cross_query.shape, jnp.bfloat16),
        in_specs=[vmem] * 3,
        out_specs=vmem,
        compiler_params=pltpu.CompilerParams(vmem_limit_bytes=8 << 20),
        cost_estimate=pl.CostEstimate(
            flops=4 * elements * DH, bytes_accessed=4 * cross_query.size, transcendentals=elements
        ),
        name="cross",
    )(cross_query, text_keys, text_values)


def body(n_seq, n_head, queries, keys, values, cross_query, text_keys, text_values, out_weight, block_list, block_count):
    n_z = n_seq // 2
    half = n_z // 2
    seq = lax.axis_index("seq")
    z, side = seq // 2, seq % 2
    blocks, counts = extra_blocks(block_list, block_count)

    def z_shift(step):
        return [(s, (s // 2 + step) % n_z * 2 + s % 2) for s in range(n_seq)]

    swap = [(s, s ^ 1) for s in range(n_seq)]

    def to_other(array):
        return lax.ppermute(array, "seq", swap)

    sent = {1: [], -1: []}

    def hop(array, way):
        done = sent[way]
        if len(done) >= IN_FLIGHT:
            array, done[-IN_FLIGHT] = lax.optimization_barrier((array, done[-IN_FLIGHT]))
        got = lax.ppermute(array, "seq", z_shift(way))
        done.append(got)
        return got

    def all_planes(starts):
        found = [{0: array} for array, _ in starts]
        for step in range(1, half + 1):
            for place, (_, last_way) in zip(found, starts):
                for way in (1, -1):
                    if step < half or way == last_way:
                        place[way * step % n_z] = hop(place[way * (step - 1) % n_z], way)
        return [[place[d] for d in range(n_z)] for place in found]

    qa, qb, qc, qpa, qpb, kva, kvb, kvc, kvpa, kvpb = pack(side.reshape(1), queries, keys, values)
    kva_other, kvb_other = to_other(kvpa), to_other(kvpb)
    qa_other, qb_other = to_other(qpa), to_other(qpb)

    below = (z - jnp.arange(n_z, dtype=jnp.int32)) % n_z
    place = jnp.concatenate([below * 2 + side, below * 2 + 1 - side])
    query_frames = jnp.stack([seq, seq + 1 - 2 * side])

    (mine_c,) = all_planes([(kvc, 1)])
    other_c = [to_other(piece) for piece in mine_c]
    mine_a, other_a = all_planes([(kva, -1), (kva_other, 1)])
    mine_b, other_b = all_planes([(kvb, -1), (kvb_other, 1)])

    cross_heads = cross(cross_query, text_keys, text_values)

    (oc,) = attend([qc], mine_c + other_c, place, query_frames, blocks, counts)
    oa, oa_send = attend([qa, qa_other], mine_a + other_a, place, query_frames, blocks, counts)
    ob, ob_send = attend([qb, qb_other], mine_b + other_b, place, query_frames, blocks, counts)
    oa_got, ob_got = to_other(oa_send), to_other(ob_send)
    mine = jnp.concatenate([oa, ob], axis=1)
    got = jnp.concatenate([oa_got, ob_got], axis=1)
    first = jnp.where(side == 0, mine, got)
    second = jnp.where(side == 0, got, mine)
    self_heads = jnp.concatenate([first, second, oc], axis=1)

    width = out_weight.shape[1] // n_head
    head = lax.axis_index("head")
    n_y = n_head // 2
    total = None
    for dy in (2, 1, 3, 0):
        for dx in (1, 0):
            target = (head // 2 + dy) % n_y * 2 + (head % 2) ^ dx
            weight = lax.dynamic_slice_in_dim(out_weight, target * width, width, 1)
            term = jnp.dot(self_heads, weight, preferred_element_type=jnp.float32).astype(jnp.bfloat16)
            if dy or dx:
                route = [(g, ((g // 2 + dy) % n_y * 2 + (g % 2)) ^ dx) for g in range(n_head)]
                term = lax.ppermute(term, "head", route)
            term = term.astype(jnp.float32)
            total = term if total is None else total + term
    return total.astype(jnp.bfloat16), cross_heads


def solution(mesh):
    rows = P(("pair", "seq"), "head")
    text = P("pair", "head")
    return jax.shard_map(
        functools.partial(body, mesh.shape["seq"], mesh.shape["head"]),
        mesh=mesh,
        in_specs=(rows, rows, rows, rows, text, text, P("head", None), P(), P()),
        out_specs=(rows, rows),
        check_vma=False,
    )
```

```python
import functools
import math

import jax
import jax.numpy as jnp
from jax import lax
from jax.experimental import pallas as pl
from jax.experimental.pallas import tpu as pltpu
from jax.sharding import PartitionSpec as P

DH = 128
BLK = 128
FB = 3
ROWS = FB * BLK
MAX_EXTRA = 12
MAX_NEAR = 3
GROUPS = ((0, 1), (2, 3), (4,))
IN_FLIGHT = 2
NEG = -1e30
LOG2E = math.log2(math.e)
TO_EXP2 = DH ** (-0.5) * LOG2E
NT = (((1,), (1,)), ((), ()))
SMEM = pl.BlockSpec(memory_space=pltpu.SMEM)
VMEM = pl.BlockSpec(memory_space=pltpu.VMEM)


def plan_kernel(last, seq_ref, list_ref, count_ref, blocks_out, count_out, near_out):
    side = seq_ref[0] % 2
    for which in range(2):
        frame = seq_ref[0] + which * (1 - 2 * side)
        found = jnp.int32(0)
        for key_frame in (frame - 1, frame, frame + 1, 0):
            here = (key_frame % 2 == side) & (key_frame >= 0) & (key_frame <= last)
            if isinstance(key_frame, int):
                here &= frame > 1
            near_out[which * (MAX_NEAR + 1) + found] = key_frame // 2
            found += here.astype(jnp.int32)
        near_out[which * (MAX_NEAR + 1) + MAX_NEAR] = found
        for r in range(FB):
            row, out = frame * FB + r, which * FB + r
            for e in range(MAX_EXTRA + 1):
                blocks_out[out, e] = 0

            def one(j, extras, row=row, out=out, frame=frame):
                block = list_ref[row, j]
                key_frame = lax.div(block, FB)
                far = (jnp.abs(key_frame - frame) > 1) & (key_frame > 0) & (key_frame % 2 == side)
                blocks_out[out, extras] = jnp.where(
                    far, lax.div(key_frame, 2) * FB + block - key_frame * FB, 0
                )
                return extras + far.astype(jnp.int32)

            extras = lax.fori_loop(0, count_ref[row], one, jnp.int32(0))
            count_out[out] = extras


def plan(frames, seq, block_list, block_count):
    return pl.pallas_call(
        functools.partial(plan_kernel, frames - 1),
        out_shape=[
            jax.ShapeDtypeStruct((2 * FB, MAX_EXTRA + 1), jnp.int32),
            jax.ShapeDtypeStruct((2 * FB,), jnp.int32),
            jax.ShapeDtypeStruct((2 * (MAX_NEAR + 1),), jnp.int32),
        ],
        in_specs=[SMEM] * 3,
        out_specs=[SMEM] * 3,
        compiler_params=pltpu.CompilerParams(vmem_limit_bytes=1 << 20),
        cost_estimate=pl.CostEstimate(flops=1000, bytes_accessed=8000, transcendentals=0),
        name="plan",
    )(seq, block_list, block_count)


def pack_kernel(k_ref, v_ref, *outs):
    for heads, out in zip(GROUPS, outs):
        for n, head in enumerate(heads):
            columns = slice(head * DH, (head + 1) * DH)
            out[2 * n * ROWS : (2 * n + 1) * ROWS, :] = k_ref[:, columns]
            out[(2 * n + 1) * ROWS : (2 * n + 2) * ROWS, :] = v_ref[:, columns]


def pack(keys, values):
    return pl.pallas_call(
        pack_kernel,
        out_shape=[jax.ShapeDtypeStruct((2 * ROWS * len(heads), DH), jnp.bfloat16) for heads in GROUPS],
        in_specs=[VMEM, VMEM],
        out_specs=[VMEM] * len(GROUPS),
        compiler_params=pltpu.CompilerParams(vmem_limit_bytes=6 << 20),
        cost_estimate=pl.CostEstimate(flops=0, bytes_accessed=4 * keys.size * 2, transcendentals=0),
        name="pack",
    )(keys, values)


def attend_frame(which, near_ref, blocks_ref, count_ref, q_ref, o_ref, lse_ref, k_s, v_s, near_s, far_s, top_s, total_s, sum_s):
    nears = near_ref[which * (MAX_NEAR + 1) + MAX_NEAR]
    counts = [count_ref[which * FB + r] for r in range(FB)]
    pairs = (jnp.maximum(jnp.maximum(counts[0], counts[1]), counts[2]) + 1) // 2

    def near_rows(w):
        return pl.ds(pl.multiple_of(near_ref[which * (MAX_NEAR + 1) + w] * ROWS, ROWS), ROWS)

    def far_rows(r, e):
        return pl.ds(pl.multiple_of(blocks_ref[which * FB + r, e] * BLK, BLK), BLK)

    top_s[...] = jnp.full_like(top_s, NEG)

    def near_scores(w, carry):
        score = lax.dot_general(q_ref[...], k_s[near_rows(w), :], NT, preferred_element_type=jnp.float32)
        near_s[w] = score
        best = jnp.maximum(jnp.maximum(score[:, :BLK], score[:, BLK : 2 * BLK]), score[:, 2 * BLK :])
        top_s[...] = jnp.maximum(top_s[...], best)
        return carry

    lax.fori_loop(0, nears, near_scores, 0)

    def far_scores(i, carry):
        for r in range(FB):
            rows = slice(r * BLK, (r + 1) * BLK)
            best = top_s[rows, :]
            for j in range(2):
                e = 2 * i + j
                score = lax.dot_general(
                    q_ref[rows, :], k_s[far_rows(r, e), :], NT, preferred_element_type=jnp.float32
                )
                score = jnp.where(e < counts[r], score, NEG)
                far_s[r, e] = score
                best = jnp.maximum(best, score)
            top_s[rows, :] = best
        return carry

    lax.fori_loop(0, pairs, far_scores, 0)
    top_s[...] = jnp.broadcast_to(jnp.max(top_s[...], axis=1, keepdims=True) * TO_EXP2, top_s.shape)
    total_s[...] = jnp.zeros_like(total_s)
    sum_s[...] = jnp.zeros_like(sum_s)

    def near_weights(w, carry):
        top = top_s[...]
        weights = [jnp.exp2(near_s[w, :, c * BLK : (c + 1) * BLK] * TO_EXP2 - top) for c in range(FB)]
        total_s[...] += weights[0] + weights[1] + weights[2]
        weight = jnp.concatenate([p.astype(jnp.bfloat16) for p in weights], axis=1)
        sum_s[...] += jnp.dot(weight, v_s[near_rows(w), :], preferred_element_type=jnp.float32)
        return carry

    lax.fori_loop(0, nears, near_weights, 0)

    def far_weights(i, carry):
        for r in range(FB):
            rows = slice(r * BLK, (r + 1) * BLK)
            top = top_s[rows, :]
            weights = [jnp.exp2(far_s[r, 2 * i + j] * TO_EXP2 - top) for j in range(2)]
            total_s[rows, :] += weights[0] + weights[1]
            part = jnp.dot(
                weights[0].astype(jnp.bfloat16), v_s[far_rows(r, 2 * i), :], preferred_element_type=jnp.float32
            )
            part += jnp.dot(
                weights[1].astype(jnp.bfloat16), v_s[far_rows(r, 2 * i + 1), :], preferred_element_type=jnp.float32
            )
            sum_s[rows, :] += part
        return carry

    lax.fori_loop(0, pairs, far_weights, 0)
    total = jnp.sum(total_s[...], axis=1, keepdims=True)
    o_ref[...] = sum_s[...] / total
    lse_ref[...] = top_s[...] + jnp.log(total) * LOG2E


def attend_kernel(heads, planes, seq_ref, near_ref, blocks_ref, count_ref, q_ref, q_other_ref, *refs):
    piece_refs = refs[:planes]
    keep_o, keep_lse, send = refs[planes : planes + 3]
    q_s, o_s, lse_s, k_s, v_s, near_s, far_s, top_s, total_s, sum_s = refs[planes + 3 :]
    z = lax.div(seq_ref[0], 2)
    for d, piece in enumerate(piece_refs):
        rows = pl.ds(pl.multiple_of(lax.rem(z + planes - d, planes) * ROWS, ROWS), ROWS)
        for n in range(len(heads)):
            k_s[n, rows, :] = piece[2 * n * ROWS : (2 * n + 1) * ROWS, :]
            v_s[n, rows, :] = piece[(2 * n + 1) * ROWS : (2 * n + 2) * ROWS, :]
    for n, head in enumerate(heads):
        columns = slice(head * DH, (head + 1) * DH)
        q_s[2 * n] = q_ref[:, columns]
        q_s[2 * n + 1] = q_other_ref[:, columns]

    def one(i, carry):
        head, which = lax.div(i, 2), lax.rem(i, 2)
        attend_frame(
            which, near_ref, blocks_ref, count_ref, q_s.at[i], o_s.at[i], lse_s.at[i],
            k_s.at[head], v_s.at[head], near_s, far_s, top_s, total_s, sum_s,
        )
        return carry

    lax.fori_loop(0, 2 * len(heads), one, 0)
    lane = lax.broadcasted_iota(jnp.int32, (ROWS, DH), 1)
    for n in range(len(heads)):
        rows = slice(n * ROWS, (n + 1) * ROWS)
        keep_o[rows, :] = o_s[2 * n]
        keep_lse[rows, :] = lse_s[2 * n]
        send[2 * n * ROWS : (2 * n + 1) * ROWS, :] = o_s[2 * n + 1].astype(jnp.bfloat16)
        left = lse_s[2 * n + 1]
        packed = jnp.zeros((ROWS, DH), jnp.float32)
        for term in range(3):
            piece = left.astype(jnp.bfloat16).astype(jnp.float32)
            packed = jnp.where(lane == term, piece, packed)
            left = left - piece
        send[(2 * n + 1) * ROWS : (2 * n + 2) * ROWS, :] = packed.astype(jnp.bfloat16)


def attend(heads, queries, queries_other, pieces, seq, near, blocks, counts):
    planes, held = len(pieces), len(heads)
    tokens = planes * ROWS
    stat = pltpu.VMEM((ROWS, BLK), jnp.float32)
    each = pltpu.VMEM((2 * held, ROWS, DH), jnp.float32)
    elements = held * ROWS * 18 * BLK
    return pl.pallas_call(
        functools.partial(attend_kernel, heads, planes),
        out_shape=[
            jax.ShapeDtypeStruct((held * ROWS, DH), jnp.float32),
            jax.ShapeDtypeStruct((held * ROWS, DH), jnp.float32),
            jax.ShapeDtypeStruct((2 * held * ROWS, DH), jnp.bfloat16),
        ],
        in_specs=[SMEM] * 4 + [VMEM] * (2 + planes),
        out_specs=[VMEM] * 3,
        scratch_shapes=[
            pltpu.VMEM((2 * held, ROWS, DH), jnp.bfloat16),
            each,
            each,
            pltpu.VMEM((held, tokens, DH), jnp.bfloat16),
            pltpu.VMEM((held, tokens, DH), jnp.bfloat16),
            pltpu.VMEM((MAX_NEAR, ROWS, ROWS), jnp.float32),
            pltpu.VMEM((FB, MAX_EXTRA, BLK, BLK), jnp.float32),
            stat,
            stat,
            stat,
        ],
        compiler_params=pltpu.CompilerParams(vmem_limit_bytes=18 << 20),
        cost_estimate=pl.CostEstimate(
            flops=40 * elements * DH, bytes_accessed=4 * held * tokens * DH, transcendentals=elements
        ),
        name="attend",
    )(seq, near, blocks, counts, queries, queries_other, *pieces)


def merge_kernel(*refs):
    out_ref, parts = refs[-1], refs[:-1]
    column = 0
    for o_ref, lse_ref, got_ref in zip(parts[0::3], parts[1::3], parts[2::3]):
        for n in range(o_ref.shape[0] // ROWS):
            rows = slice(n * ROWS, (n + 1) * ROWS)
            other_o = got_ref[2 * n * ROWS : (2 * n + 1) * ROWS, :].astype(jnp.float32)
            packed = got_ref[(2 * n + 1) * ROWS : (2 * n + 2) * ROWS, :].astype(jnp.float32)
            other_lse = jnp.sum(packed, axis=1, keepdims=True)
            lse = lse_ref[rows, :]
            top = jnp.maximum(lse, other_lse)
            mine, other = jnp.exp2(lse - top), jnp.exp2(other_lse - top)
            out = ((o_ref[rows, :] * mine + other_o * other) / (mine + other)).astype(out_ref.dtype)
            for copy in range(out_ref.shape[0]):
                out_ref[copy, :, column : column + DH] = out
            column += DH


def merge(copies, *parts):
    size = sum(part.size for part in parts[0::3])
    return pl.pallas_call(
        merge_kernel,
        out_shape=jax.ShapeDtypeStruct((copies, ROWS, size // ROWS), jnp.bfloat16),
        in_specs=[VMEM] * len(parts),
        out_specs=VMEM,
        compiler_params=pltpu.CompilerParams(vmem_limit_bytes=10 << 20),
        cost_estimate=pl.CostEstimate(flops=8 * size, bytes_accessed=30 * size, transcendentals=2 * size),
        name="merge",
    )(*parts)


def tile_kernel(pair_ref, weight_ref, out_ref):
    out_ref[0] = weight_ref[...]


def tile(pair, weight, count):
    deep, width = weight.shape[0] // 2, weight.shape[1] // count
    return pl.pallas_call(
        tile_kernel,
        out_shape=jax.ShapeDtypeStruct((count, deep, width), weight.dtype),
        grid_spec=pltpu.PrefetchScalarGridSpec(
            num_scalar_prefetch=1,
            grid=(count,),
            in_specs=[pl.BlockSpec((deep, width), lambda g, pair: (pair[0], g))],
            out_specs=pl.BlockSpec((1, deep, width), lambda g, pair: (g, 0, 0)),
        ),
        compiler_params=pltpu.CompilerParams(vmem_limit_bytes=4 << 20),
        cost_estimate=pl.CostEstimate(flops=0, bytes_accessed=2 * weight.size, transcendentals=0),
        name="tile",
    )(pair, weight)


def cross_kernel(q_ref, k_ref, v_ref, o_ref):
    def one(h, carry):
        columns = pl.ds(pl.multiple_of(h * DH, DH), DH)
        score = lax.dot_general(q_ref[:, columns], k_ref[:, columns], NT, preferred_element_type=jnp.float32)
        top = jnp.max(score, axis=1, keepdims=True) * TO_EXP2
        weight = jnp.exp2(score * TO_EXP2 - top)
        total = jnp.sum(weight, axis=1, keepdims=True)
        part = jnp.dot(weight.astype(jnp.bfloat16), v_ref[:, columns], preferred_element_type=jnp.float32)
        o_ref[:, columns] = (part / total).astype(o_ref.dtype)
        return carry

    lax.fori_loop(0, q_ref.shape[1] // DH, one, 0)


def cross(cross_query, text_keys, text_values):
    elements = cross_query.shape[0] * cross_query.shape[1] // DH * text_keys.shape[0]
    return pl.pallas_call(
        cross_kernel,
        out_shape=jax.ShapeDtypeStruct(cross_query.shape, jnp.bfloat16),
        in_specs=[VMEM] * 3,
        out_specs=VMEM,
        compiler_params=pltpu.CompilerParams(vmem_limit_bytes=8 << 20),
        cost_estimate=pl.CostEstimate(
            flops=40 * elements * DH, bytes_accessed=4 * cross_query.size, transcendentals=elements
        ),
        name="cross",
    )(cross_query, text_keys, text_values)


def project_kernel(first, pair_ref, heads_ref, mine_ref, got_ref, *refs):
    out_ref, total_s = refs[-2:]
    total_s[...] = refs[0][...] if len(refs) == 3 else jnp.zeros_like(total_s)
    depth, deep = heads_ref.shape[2], mine_ref.shape[1]
    low, high = first * DH, first * DH + depth

    def add(lower_ref, upper_ref):
        def one(g, carry):
            for ref, base in ((lower_ref, 0), (upper_ref, deep)):
                start, stop = max(low, base), min(high, base + deep)
                if start < stop:
                    part = jnp.dot(
                        heads_ref[g, :, start - low : stop - low],
                        ref[g, start - base : stop - base, :],
                        preferred_element_type=jnp.float32,
                    )
                    total_s[...] += part
            return carry

        lax.fori_loop(0, heads_ref.shape[0], one, 0)

    @pl.when(pair_ref[0] == 0)
    def _():
        add(mine_ref, got_ref)

    @pl.when(pair_ref[0] == 1)
    def _():
        add(got_ref, mine_ref)

    out_ref[...] = total_s[...].astype(out_ref.dtype)


def project(first, pair, heads, mine, got, before, dtype):
    groups, rows, depth = heads.shape
    width = mine.shape[2]
    given = [heads, mine, got] + ([] if before is None else [before])
    return pl.pallas_call(
        functools.partial(project_kernel, first),
        out_shape=jax.ShapeDtypeStruct((rows, width), dtype),
        in_specs=[SMEM] + [VMEM] * len(given),
        out_specs=VMEM,
        scratch_shapes=[pltpu.VMEM((rows, width), jnp.float32)],
        compiler_params=pltpu.CompilerParams(vmem_limit_bytes=16 << 20),
        cost_estimate=pl.CostEstimate(
            flops=2 * groups * rows * depth * width, bytes_accessed=2 * heads.size + 2 * groups * depth * width, transcendentals=0
        ),
        name="project",
    )(pair, *given)


def body(n_seq, n_head, queries, keys, values, cross_query, text_keys, text_values, out_weight, block_list, block_count):
    n_z = n_seq // 2
    seq = lax.axis_index("seq").reshape(1)
    pair = lax.axis_index("pair").reshape(1)
    swap = [(s, s ^ 1) for s in range(n_seq)]

    def to_other(array):
        return lax.ppermute(array, "seq", swap)

    def z_shift(step):
        return [(s, (s // 2 + step) % n_z * 2 + s % 2) for s in range(n_seq)]

    held = [{0: array} for array in pack(keys, values)]
    out_weight, held[0][0] = lax.optimization_barrier((out_weight, held[0][0]))
    queries_other = to_other(queries)
    mine = lax.all_to_all(tile(pair, out_weight, n_head), "head", 0, 0, tiled=True)
    got = lax.ppermute(mine, "pair", [(0, 1), (1, 0)])
    blocks, counts, near = plan(n_seq, seq, block_list, block_count)
    cross_heads = cross(cross_query, text_keys, text_values)

    sent = {1: [], -1: []}

    def hop(way, group, step, after=None):
        done = sent[way]
        array = held[group][way * (step - 1) % n_z]
        if len(done) >= IN_FLIGHT:
            at, where = done[-IN_FLIGHT]
            array, held[at][where] = lax.optimization_barrier((array, held[at][where]))
        if after is not None:
            array, after[0] = lax.optimization_barrier((array, after[0]))
        place = way * step % n_z
        held[group][place] = lax.ppermute(array, "seq", z_shift(way))
        done.append((group, place))

    def partial(group):
        pieces = [held[group][d] for d in range(n_z)]
        return attend(GROUPS[group], queries, queries_other, pieces, seq, near, blocks, counts)

    def share(*parts):
        merged = merge(n_head, *(array for part in parts for array in (*part[:2], to_other(part[2]))))
        return lax.all_to_all(merged, "head", 0, 0, tiled=True)

    for group, step in ((0, 1), (0, 2), (1, 1), (0, 3), (1, 2)):
        hop(1, group, step)
        hop(-1, group, step)
    hop(1, 0, 4)
    hop(1, 1, 3)
    hop(-1, 1, 3)
    hop(1, 2, 1)
    hop(-1, 2, 1)
    first = list(partial(0))
    hop(1, 2, 2, first)
    hop(-1, 1, 4, first)
    hop(-1, 2, 2)
    hop(1, 2, 3)
    second = list(partial(1))
    hop(1, 2, 4, second)
    hop(-1, 2, 3, second)
    most = share(first, second)
    before = project(0, pair, most, mine, got, None, jnp.float32)
    last = share(partial(2))
    block_stream = project(GROUPS[2][0], pair, last, mine, got, before, jnp.bfloat16)
    return block_stream, cross_heads


def solution(mesh):
    rows = P(("pair", "seq"), "head")
    text = P("pair", "head")
    return jax.shard_map(
        functools.partial(body, mesh.shape["seq"], mesh.shape["head"]),
        mesh=mesh,
        in_specs=(rows, rows, rows, rows, text, text, P("head", None), P(), P()),
        out_specs=(rows, rows),
        check_vma=False,
    )
```

```python
import functools
import math

import jax
import jax.numpy as jnp
from jax import lax
from jax.experimental import pallas as pl
from jax.experimental.pallas import tpu as pltpu
from jax.sharding import PartitionSpec as P

DH = 128
BLK = 128
FB = 3
ROWS = FB * BLK
MAX_EXTRA = 12
MAX_NEAR = 3
GROUPS = ((0, 1), (2, 3), (4,))
IN_FLIGHT = 2
NEG = -1e30
LOG2E = math.log2(math.e)
TO_EXP2 = DH ** (-0.5) * LOG2E
NT = (((1,), (1,)), ((), ()))
SMEM = pl.BlockSpec(memory_space=pltpu.SMEM)
VMEM = pl.BlockSpec(memory_space=pltpu.VMEM)


def plan_kernel(last, seq_ref, list_ref, count_ref, blocks_out, count_out, near_out):
    side = seq_ref[0] % 2
    for which in range(2):
        frame = seq_ref[0] + which * (1 - 2 * side)
        found = jnp.int32(0)
        for key_frame in (frame - 1, frame, frame + 1, 0):
            here = (key_frame % 2 == side) & (key_frame >= 0) & (key_frame <= last)
            if isinstance(key_frame, int):
                here &= frame > 1
            near_out[which * (MAX_NEAR + 1) + found] = key_frame // 2
            found += here.astype(jnp.int32)
        near_out[which * (MAX_NEAR + 1) + MAX_NEAR] = found
        for r in range(FB):
            row, out = frame * FB + r, which * FB + r
            for e in range(MAX_EXTRA + 1):
                blocks_out[out, e] = 0

            def one(j, extras, row=row, out=out, frame=frame):
                block = list_ref[row, j]
                key_frame = lax.div(block, FB)
                far = (jnp.abs(key_frame - frame) > 1) & (key_frame > 0) & (key_frame % 2 == side)
                blocks_out[out, extras] = jnp.where(
                    far, lax.div(key_frame, 2) * FB + block - key_frame * FB, 0
                )
                return extras + far.astype(jnp.int32)

            extras = lax.fori_loop(0, count_ref[row], one, jnp.int32(0))
            count_out[out] = extras


def plan(frames, seq, block_list, block_count):
    return pl.pallas_call(
        functools.partial(plan_kernel, frames - 1),
        out_shape=[
            jax.ShapeDtypeStruct((2 * FB, MAX_EXTRA + 1), jnp.int32),
            jax.ShapeDtypeStruct((2 * FB,), jnp.int32),
            jax.ShapeDtypeStruct((2 * (MAX_NEAR + 1),), jnp.int32),
        ],
        in_specs=[SMEM] * 3,
        out_specs=[SMEM] * 3,
        compiler_params=pltpu.CompilerParams(vmem_limit_bytes=1 << 20),
        cost_estimate=pl.CostEstimate(flops=1000, bytes_accessed=8000, transcendentals=0),
        name="plan",
    )(seq, block_list, block_count)


def pack_kernel(k_ref, v_ref, *outs):
    for heads, out in zip(GROUPS, outs):
        for n, head in enumerate(heads):
            columns = slice(head * DH, (head + 1) * DH)
            out[2 * n * ROWS : (2 * n + 1) * ROWS, :] = k_ref[:, columns]
            out[(2 * n + 1) * ROWS : (2 * n + 2) * ROWS, :] = v_ref[:, columns]


def pack(keys, values):
    return pl.pallas_call(
        pack_kernel,
        out_shape=[jax.ShapeDtypeStruct((2 * ROWS * len(heads), DH), jnp.bfloat16) for heads in GROUPS],
        in_specs=[VMEM, VMEM],
        out_specs=[VMEM] * len(GROUPS),
        compiler_params=pltpu.CompilerParams(vmem_limit_bytes=6 << 20),
        cost_estimate=pl.CostEstimate(flops=0, bytes_accessed=4 * keys.size * 2, transcendentals=0),
        name="pack",
    )(keys, values)


def attend_frame(which, heads, near_ref, blocks_ref, count_ref, q_s, o_s, lse_s, k_s, v_s, near_s, far_s, top_s, sum_s):
    nears = near_ref[which * (MAX_NEAR + 1) + MAX_NEAR]
    counts = [count_ref[which * FB + r] for r in range(FB)]
    pairs = (jnp.maximum(jnp.maximum(counts[0], counts[1]), counts[2]) + 1) // 2

    def near_rows(w):
        return pl.ds(pl.multiple_of(near_ref[which * (MAX_NEAR + 1) + w] * ROWS, ROWS), ROWS)

    def far_rows(r, e):
        return pl.ds(pl.multiple_of(blocks_ref[which * FB + r, e] * BLK, BLK), BLK)

    top_s[...] = jnp.full_like(top_s, NEG)

    def near_scores(w, carry):
        for n in range(heads):
            score = lax.dot_general(
                q_s[2 * n + which], k_s[n, near_rows(w), :], NT, preferred_element_type=jnp.float32
            )
            near_s[n, w] = score
            best = jnp.maximum(jnp.maximum(score[:, :BLK], score[:, BLK : 2 * BLK]), score[:, 2 * BLK :])
            top_s[n] = jnp.maximum(top_s[n], best)
        return carry

    lax.fori_loop(0, nears, near_scores, 0)

    def far_scores(i, carry):
        for n in range(heads):
            for r in range(FB):
                rows = slice(r * BLK, (r + 1) * BLK)
                best = top_s[n, rows, :]
                for j in range(2):
                    e = 2 * i + j
                    score = lax.dot_general(
                        q_s[2 * n + which, rows, :], k_s[n, far_rows(r, e), :], NT, preferred_element_type=jnp.float32
                    )
                    score = jnp.where(e < counts[r], score, NEG)
                    far_s[n, r, e] = score
                    best = jnp.maximum(best, score)
                top_s[n, rows, :] = best
        return carry

    lax.fori_loop(0, pairs, far_scores, 0)
    for n in range(heads):
        top_s[n] = jnp.broadcast_to(jnp.max(top_s[n], axis=1, keepdims=True) * TO_EXP2, (ROWS, BLK))
    sum_s[...] = jnp.zeros_like(sum_s)

    def near_weights(w, carry):
        for n in range(heads):
            top = top_s[n]
            weights = [jnp.exp2(near_s[n, w, :, c * BLK : (c + 1) * BLK] * TO_EXP2 - top) for c in range(FB)]
            weight = jnp.concatenate([p.astype(jnp.bfloat16) for p in weights], axis=1)
            sum_s[n] += jnp.dot(weight, v_s[n, near_rows(w), :], preferred_element_type=jnp.float32)
        return carry

    lax.fori_loop(0, nears, near_weights, 0)

    def far_weights(i, carry):
        for n in range(heads):
            for r in range(FB):
                rows = slice(r * BLK, (r + 1) * BLK)
                top = top_s[n, rows, :]
                weights = [jnp.exp2(far_s[n, r, 2 * i + j] * TO_EXP2 - top) for j in range(2)]
                part = jnp.dot(
                    weights[0].astype(jnp.bfloat16), v_s[n, far_rows(r, 2 * i), :], preferred_element_type=jnp.float32
                )
                part += jnp.dot(
                    weights[1].astype(jnp.bfloat16), v_s[n, far_rows(r, 2 * i + 1), :], preferred_element_type=jnp.float32
                )
                sum_s[n, rows, :] += part
        return carry

    lax.fori_loop(0, pairs, far_weights, 0)
    for n in range(heads):
        total = sum_s[n, :, DH:]
        o_s[2 * n + which] = sum_s[n, :, :DH] / total
        lse_s[2 * n + which] = top_s[n] + jnp.log(total) * LOG2E


def attend_kernel(heads, planes, seq_ref, near_ref, blocks_ref, count_ref, q_ref, q_other_ref, *refs):
    piece_refs = refs[:planes]
    keep_o, keep_lse, send = refs[planes : planes + 3]
    q_s, o_s, lse_s, k_s, v_s, near_s, far_s, top_s, sum_s = refs[planes + 3 :]
    z = lax.div(seq_ref[0], 2)
    v_s[:, :, DH:] = jnp.ones((len(heads), planes * ROWS, DH), jnp.bfloat16)
    for d, piece in enumerate(piece_refs):
        rows = pl.ds(pl.multiple_of(lax.rem(z + planes - d, planes) * ROWS, ROWS), ROWS)
        for n in range(len(heads)):
            k_s[n, rows, :] = piece[2 * n * ROWS : (2 * n + 1) * ROWS, :]
            v_s[n, rows, 0:DH] = piece[(2 * n + 1) * ROWS : (2 * n + 2) * ROWS, :]
    for n, head in enumerate(heads):
        columns = slice(head * DH, (head + 1) * DH)
        q_s[2 * n] = q_ref[:, columns]
        q_s[2 * n + 1] = q_other_ref[:, columns]

    def one(which, carry):
        attend_frame(
            which, len(heads), near_ref, blocks_ref, count_ref, q_s, o_s, lse_s, k_s, v_s, near_s, far_s, top_s, sum_s
        )
        return carry

    lax.fori_loop(0, 2, one, 0)
    lane = lax.broadcasted_iota(jnp.int32, (ROWS, DH), 1)
    for n in range(len(heads)):
        rows = slice(n * ROWS, (n + 1) * ROWS)
        keep_o[rows, :] = o_s[2 * n]
        keep_lse[rows, :] = lse_s[2 * n]
        send[2 * n * ROWS : (2 * n + 1) * ROWS, :] = o_s[2 * n + 1].astype(jnp.bfloat16)
        left = lse_s[2 * n + 1]
        packed = jnp.zeros((ROWS, DH), jnp.float32)
        for term in range(3):
            piece = left.astype(jnp.bfloat16).astype(jnp.float32)
            packed = jnp.where(lane == term, piece, packed)
            left = left - piece
        send[(2 * n + 1) * ROWS : (2 * n + 2) * ROWS, :] = packed.astype(jnp.bfloat16)


def attend(heads, queries, queries_other, pieces, seq, near, blocks, counts):
    planes, held = len(pieces), len(heads)
    tokens = planes * ROWS
    each = pltpu.VMEM((2 * held, ROWS, DH), jnp.float32)
    elements = held * ROWS * 18 * BLK
    return pl.pallas_call(
        functools.partial(attend_kernel, heads, planes),
        out_shape=[
            jax.ShapeDtypeStruct((held * ROWS, DH), jnp.float32),
            jax.ShapeDtypeStruct((held * ROWS, DH), jnp.float32),
            jax.ShapeDtypeStruct((2 * held * ROWS, DH), jnp.bfloat16),
        ],
        in_specs=[SMEM] * 4 + [VMEM] * (2 + planes),
        out_specs=[VMEM] * 3,
        scratch_shapes=[
            pltpu.VMEM((2 * held, ROWS, DH), jnp.bfloat16),
            each,
            each,
            pltpu.VMEM((held, tokens, DH), jnp.bfloat16),
            pltpu.VMEM((held, tokens, 2 * DH), jnp.bfloat16),
            pltpu.VMEM((held, MAX_NEAR, ROWS, ROWS), jnp.float32),
            pltpu.VMEM((held, FB, MAX_EXTRA, BLK, BLK), jnp.float32),
            pltpu.VMEM((held, ROWS, BLK), jnp.float32),
            pltpu.VMEM((held, ROWS, 2 * DH), jnp.float32),
        ],
        compiler_params=pltpu.CompilerParams(vmem_limit_bytes=28 << 20),
        cost_estimate=pl.CostEstimate(
            flops=40 * elements * DH, bytes_accessed=4 * held * tokens * DH, transcendentals=elements
        ),
        name="attend",
    )(seq, near, blocks, counts, queries, queries_other, *pieces)


def merge_kernel(*refs):
    out_ref, parts = refs[-1], refs[:-1]
    column = 0
    for o_ref, lse_ref, got_ref in zip(parts[0::3], parts[1::3], parts[2::3]):
        for n in range(o_ref.shape[0] // ROWS):
            rows = slice(n * ROWS, (n + 1) * ROWS)
            other_o = got_ref[2 * n * ROWS : (2 * n + 1) * ROWS, :].astype(jnp.float32)
            packed = got_ref[(2 * n + 1) * ROWS : (2 * n + 2) * ROWS, :].astype(jnp.float32)
            other_lse = jnp.sum(packed, axis=1, keepdims=True)
            lse = lse_ref[rows, :]
            top = jnp.maximum(lse, other_lse)
            mine, other = jnp.exp2(lse - top), jnp.exp2(other_lse - top)
            out = ((o_ref[rows, :] * mine + other_o * other) / (mine + other)).astype(out_ref.dtype)
            out_ref[:, column : column + DH] = out
            column += DH


def merge(*parts):
    size = sum(part.size for part in parts[0::3])
    return pl.pallas_call(
        merge_kernel,
        out_shape=jax.ShapeDtypeStruct((ROWS, size // ROWS), jnp.bfloat16),
        in_specs=[VMEM] * len(parts),
        out_specs=VMEM,
        compiler_params=pltpu.CompilerParams(vmem_limit_bytes=10 << 20),
        cost_estimate=pl.CostEstimate(flops=8 * size, bytes_accessed=30 * size, transcendentals=2 * size),
        name="merge",
    )(*parts)


def tile_kernel(y_ref, weight_ref, *refs):
    outs, sems = refs[:-1], refs[-1]
    width = outs[0].shape[1]
    copies = []
    for dy, out in enumerate(outs):
        start = pl.multiple_of(lax.rem(y_ref[0] + dy, len(outs)) * width, width)
        copies.append(pltpu.make_async_copy(weight_ref.at[:, pl.ds(start, width)], out, sems.at[dy]))
    for copy in copies:
        copy.start()
    for copy in copies:
        copy.wait()


def tile(y, weight, count):
    stay = pl.BlockSpec(memory_space=pl.ANY)
    return pl.pallas_call(
        tile_kernel,
        out_shape=[jax.ShapeDtypeStruct((weight.shape[0], weight.shape[1] // count), weight.dtype)] * count,
        in_specs=[SMEM, stay],
        out_specs=[stay] * count,
        scratch_shapes=[pltpu.SemaphoreType.DMA((count,))],
        compiler_params=pltpu.CompilerParams(vmem_limit_bytes=1 << 20),
        cost_estimate=pl.CostEstimate(flops=0, bytes_accessed=4 * weight.size, transcendentals=0),
        name="tile",
    )(y, weight)


def cross_kernel(q_ref, k_ref, v_ref, o_ref):
    def one(h, carry):
        columns = pl.ds(pl.multiple_of(h * DH, DH), DH)
        score = lax.dot_general(q_ref[:, columns], k_ref[:, columns], NT, preferred_element_type=jnp.float32)
        top = jnp.max(score, axis=1, keepdims=True) * TO_EXP2
        weight = jnp.exp2(score * TO_EXP2 - top)
        total = jnp.sum(weight, axis=1, keepdims=True)
        part = jnp.dot(weight.astype(jnp.bfloat16), v_ref[:, columns], preferred_element_type=jnp.float32)
        o_ref[:, columns] = (part / total).astype(o_ref.dtype)
        return carry

    lax.fori_loop(0, q_ref.shape[1] // DH, one, 0)


def cross(cross_query, text_keys, text_values):
    elements = cross_query.shape[0] * cross_query.shape[1] // DH * text_keys.shape[0]
    return pl.pallas_call(
        cross_kernel,
        out_shape=jax.ShapeDtypeStruct(cross_query.shape, jnp.bfloat16),
        in_specs=[VMEM] * 3,
        out_specs=VMEM,
        compiler_params=pltpu.CompilerParams(vmem_limit_bytes=8 << 20),
        cost_estimate=pl.CostEstimate(
            flops=40 * elements * DH, bytes_accessed=4 * cross_query.size, transcendentals=elements
        ),
        name="cross",
    )(cross_query, text_keys, text_values)


def project_kernel(first, sources, *refs):
    heads, weights, total_ref = refs[:sources], refs[sources : 2 * sources], refs[-1]
    depth = heads[0].shape[1]
    total = None if len(refs) == 2 * sources + 1 else refs[2 * sources][...]
    for head_ref, weight_ref in zip(heads, weights):
        weight = weight_ref[first * DH : first * DH + depth, :]
        part = jnp.dot(head_ref[...], weight, preferred_element_type=jnp.float32)
        total = part if total is None else total + part
    total_ref[...] = total


def project_last_kernel(first, sources, x_ref, *refs):
    heads, weights, before_ref = refs[:sources], refs[sources : 2 * sources], refs[2 * sources]
    keep_ref, send_ref = refs[2 * sources + 1 : 2 * sources + 3]
    depth = heads[0].shape[1]
    width = keep_ref.shape[1]
    rows = slice(first * DH, first * DH + depth)
    for where, out_ref in ((1 - x_ref[0], send_ref), (x_ref[0], keep_ref)):
        columns = pl.ds(pl.multiple_of(where * width, width), width)
        total = before_ref[:, columns]
        for head_ref, weight_ref in zip(heads, weights):
            total += jnp.dot(head_ref[...], weight_ref[rows, columns], preferred_element_type=jnp.float32)
        out_ref[...] = total.astype(out_ref.dtype)


def project(first, heads, weights, before=None, x=None):
    rows, depth = heads[0].shape
    width = weights[0].shape[1]
    given = [*heads, *weights] + ([] if before is None else [before])
    if x is None:
        kernel, lead, out = project_kernel, [], jax.ShapeDtypeStruct((rows, width), jnp.float32)
    else:
        kernel, lead = project_last_kernel, [x]
        out = [jax.ShapeDtypeStruct((rows, width // 2), dtype) for dtype in (jnp.float32, jnp.bfloat16)]
    return pl.pallas_call(
        functools.partial(kernel, first, len(heads)),
        out_shape=out,
        in_specs=[SMEM] * len(lead) + [VMEM] * len(given),
        out_specs=VMEM if x is None else [VMEM] * 2,
        compiler_params=pltpu.CompilerParams(vmem_limit_bytes=20 << 20),
        cost_estimate=pl.CostEstimate(
            flops=2 * len(heads) * rows * depth * width,
            bytes_accessed=2 * len(heads) * depth * (rows + width),
            transcendentals=0,
        ),
        name="project",
    )(*lead, *given)


def body(n_seq, n_head, queries, keys, values, cross_query, text_keys, text_values, out_weight, block_list, block_count):
    n_z, n_y = n_seq // 2, n_head // 2
    seq = lax.axis_index("seq").reshape(1)
    head = lax.axis_index("head").reshape(1)
    swap = [(s, s ^ 1) for s in range(n_seq)]

    def to_other(array):
        return lax.ppermute(array, "seq", swap)

    def z_shift(step):
        return [(s, (s // 2 + step) % n_z * 2 + s % 2) for s in range(n_seq)]

    def y_shift(step):
        return [(g, (g // 2 + step) % n_y * 2 + g % 2) for g in range(n_head)]

    held = [{0: array} for array in pack(keys, values)]
    sent = {1: [], -1: []}

    def hop(way, group, step, after=None):
        done = sent[way]
        array = held[group][way * (step - 1) % n_z]
        if len(done) >= IN_FLIGHT:
            at, where = done[-IN_FLIGHT]
            array, held[at][where] = lax.optimization_barrier((array, held[at][where]))
        if after is not None:
            array, after[0] = lax.optimization_barrier((array, after[0]))
        place = way * step % n_z
        held[group][place] = lax.ppermute(array, "seq", z_shift(way))
        done.append((group, place))

    def partial(group):
        pieces = [held[group][d] for d in range(n_z)]
        return attend(GROUPS[group], queries, queries_other, pieces, seq, near, blocks, counts)

    def join(*parts):
        return merge(*(array for part in parts for array in (*part[:2], to_other(part[2]))))

    def along_y(array):
        return [array] + [lax.ppermute(array, "head", y_shift(-dy)) for dy in range(1, n_y)]

    for group in (0, 1):
        hop(1, group, 1)
        hop(-1, group, 1)
    queries_other = to_other(queries)
    early = list(plan(n_seq, seq, block_list, block_count))
    cross_early = [cross(cross_query, text_keys, text_values)]
    tiles = list(tile(lax.div(head, 2), out_weight, n_y))
    early[0], tiles[0] = lax.optimization_barrier((early[0], tiles[0]))
    hop(1, 0, 2, early)
    hop(-1, 0, 2, cross_early)
    blocks, counts, near = early
    (cross_heads,) = cross_early
    arrived = {dy: lax.ppermute(tiles[dy], "head", y_shift(dy)) for dy in (1, n_y - 1)}
    for group, step in ((0, 3), (1, 2)):
        hop(1, group, step)
        hop(-1, group, step)
    near_tiles = [arrived[1], arrived[n_y - 1]]
    near_tiles[0], near_tiles[1], tiles[2] = lax.optimization_barrier((*near_tiles, tiles[2]))
    hop(1, 0, 4, near_tiles)
    arrived[1], arrived[n_y - 1] = near_tiles
    arrived[2] = lax.ppermute(tiles[2], "head", y_shift(2))
    weights = [tiles[0]] + [arrived[n_y - dy] for dy in range(1, n_y)]
    hop(1, 1, 3)
    hop(-1, 1, 3)
    hop(1, 2, 1)
    hop(-1, 2, 1)
    first = list(partial(0))
    hop(1, 2, 2, first)
    hop(-1, 1, 4, first)
    hop(-1, 2, 2)
    hop(1, 2, 3)
    second = list(partial(1))
    hop(1, 2, 4, second)
    hop(-1, 2, 3, second)
    before = project(0, along_y(join(first)), weights)
    before = project(2, along_y(join(second)), weights, before)
    keep, send = project(GROUPS[2][0], along_y(join(partial(2))), weights, before, lax.rem(head, 2))
    got = lax.ppermute(send, "head", [(g, g ^ 1) for g in range(n_head)])
    return (keep + got.astype(jnp.float32)).astype(jnp.bfloat16), cross_heads


def solution(mesh):
    rows = P(("pair", "seq"), "head")
    text = P("pair", "head")
    return jax.shard_map(
        functools.partial(body, mesh.shape["seq"], mesh.shape["head"]),
        mesh=mesh,
        in_specs=(rows, rows, rows, rows, text, text, P("head", None), P(), P()),
        out_specs=(rows, rows),
        check_vma=False,
    )
```

```python
import functools
import math

import jax
import jax.numpy as jnp
from jax import lax
from jax.experimental import pallas as pl
from jax.experimental.pallas import tpu as pltpu
from jax.sharding import PartitionSpec as P

DH = 128
BLK = 128
FB = 3
ROWS = FB * BLK
MAX_EXTRA = 12
MAX_NEAR = 3
GROUPS = ((0, 1, 2), (3, 4))
IN_FLIGHT = 2
NEG = -1e30
LOG2E = math.log2(math.e)
TO_EXP2 = DH ** (-0.5) * LOG2E
NT = (((1,), (1,)), ((), ()))
SMEM = pl.BlockSpec(memory_space=pltpu.SMEM)
VMEM = pl.BlockSpec(memory_space=pltpu.VMEM)


def plan_kernel(last, seq_ref, list_ref, count_ref, blocks_out, count_out, near_out):
    side = seq_ref[0] % 2
    for which in range(2):
        frame = seq_ref[0] + which * (1 - 2 * side)
        found = jnp.int32(0)
        for w in range(MAX_NEAR):
            near_out[which * (MAX_NEAR + 1) + w] = 0
        for key_frame in (frame - 1, frame, frame + 1, 0):
            here = (key_frame % 2 == side) & (key_frame >= 0) & (key_frame <= last)
            if isinstance(key_frame, int):
                here &= frame > 1
            near_out[which * (MAX_NEAR + 1) + found] = jnp.where(here, key_frame // 2, 0)
            found += here.astype(jnp.int32)
        near_out[which * (MAX_NEAR + 1) + MAX_NEAR] = found
        for r in range(FB):
            row, out = frame * FB + r, which * FB + r
            for e in range(MAX_EXTRA + 1):
                blocks_out[out, e] = 0

            def one(j, extras, row=row, out=out, frame=frame):
                block = list_ref[row, j]
                key_frame = lax.div(block, FB)
                far = (jnp.abs(key_frame - frame) > 1) & (key_frame > 0) & (key_frame % 2 == side)
                blocks_out[out, extras] = jnp.where(
                    far, lax.div(key_frame, 2) * FB + block - key_frame * FB, 0
                )
                return extras + far.astype(jnp.int32)

            extras = lax.fori_loop(0, count_ref[row], one, jnp.int32(0))
            count_out[out] = extras


def plan(frames, seq, block_list, block_count):
    return pl.pallas_call(
        functools.partial(plan_kernel, frames - 1),
        out_shape=[
            jax.ShapeDtypeStruct((2 * FB, MAX_EXTRA + 1), jnp.int32),
            jax.ShapeDtypeStruct((2 * FB,), jnp.int32),
            jax.ShapeDtypeStruct((2 * (MAX_NEAR + 1),), jnp.int32),
        ],
        in_specs=[SMEM] * 3,
        out_specs=[SMEM] * 3,
        compiler_params=pltpu.CompilerParams(vmem_limit_bytes=1 << 20),
        cost_estimate=pl.CostEstimate(flops=1000, bytes_accessed=8000, transcendentals=0),
        name="plan",
    )(seq, block_list, block_count)


def pack_kernel(k_ref, v_ref, *outs):
    for heads, out in zip(GROUPS, outs):
        for n, head in enumerate(heads):
            columns = slice(head * DH, (head + 1) * DH)
            out[2 * n * ROWS : (2 * n + 1) * ROWS, :] = k_ref[:, columns]
            out[(2 * n + 1) * ROWS : (2 * n + 2) * ROWS, :] = v_ref[:, columns]


def pack(keys, values):
    return pl.pallas_call(
        pack_kernel,
        out_shape=[jax.ShapeDtypeStruct((2 * ROWS * len(heads), DH), jnp.bfloat16) for heads in GROUPS],
        in_specs=[VMEM, VMEM],
        out_specs=[VMEM] * len(GROUPS),
        compiler_params=pltpu.CompilerParams(vmem_limit_bytes=6 << 20),
        cost_estimate=pl.CostEstimate(flops=0, bytes_accessed=4 * keys.size * 2, transcendentals=0),
        name="pack",
    )(keys, values)


def attend_lanes(lanes, near_ref, blocks_ref, count_ref, q_s, o_s, lse_s, k_s, v_s, near_s, far_s, top_s, sum_s):
    frames = sorted({which for _, which in lanes}, key=str) if all(isinstance(w, int) for _, w in lanes) else [lanes[0][1]]
    nears = near_ref[frames[0] * (MAX_NEAR + 1) + MAX_NEAR]
    most = count_ref[frames[0] * FB]
    for which in frames:
        nears = jnp.maximum(nears, near_ref[which * (MAX_NEAR + 1) + MAX_NEAR])
        for r in range(FB):
            most = jnp.maximum(most, count_ref[which * FB + r])
    pairs = lax.div(most + 1, 2)

    def near_rows(which, w):
        return pl.ds(pl.multiple_of(near_ref[which * (MAX_NEAR + 1) + w] * ROWS, ROWS), ROWS)

    def far_rows(which, r, e):
        return pl.ds(pl.multiple_of(blocks_ref[which * FB + r, e] * BLK, BLK), BLK)

    top_s[...] = jnp.full_like(top_s, NEG)

    def near_scores(w, carry):
        for lane, (n, which) in enumerate(lanes):
            score = lax.dot_general(
                q_s[2 * n + which], k_s[n, near_rows(which, w), :], NT, preferred_element_type=jnp.float32
            )
            if len(frames) > 1:
                score = jnp.where(w < near_ref[which * (MAX_NEAR + 1) + MAX_NEAR], score, NEG)
            near_s[lane, w] = score
            best = jnp.maximum(jnp.maximum(score[:, :BLK], score[:, BLK : 2 * BLK]), score[:, 2 * BLK :])
            top_s[lane] = jnp.maximum(top_s[lane], best)
        return carry

    lax.fori_loop(0, nears, near_scores, 0)

    def far_scores(i, carry):
        for lane, (n, which) in enumerate(lanes):
            for r in range(FB):
                rows = slice(r * BLK, (r + 1) * BLK)
                best = top_s[lane, rows, :]
                for j in range(2):
                    e = 2 * i + j
                    score = lax.dot_general(
                        q_s[2 * n + which, rows, :], k_s[n, far_rows(which, r, e), :], NT, preferred_element_type=jnp.float32
                    )
                    score = jnp.where(e < count_ref[which * FB + r], score, NEG)
                    far_s[lane, r, e] = score
                    best = jnp.maximum(best, score)
                top_s[lane, rows, :] = best
        return carry

    lax.fori_loop(0, pairs, far_scores, 0)
    for lane in range(len(lanes)):
        top_s[lane] = jnp.broadcast_to(jnp.max(top_s[lane], axis=1, keepdims=True) * TO_EXP2, (ROWS, BLK))
    sum_s[...] = jnp.zeros_like(sum_s)

    def near_weights(w, carry):
        for lane, (n, which) in enumerate(lanes):
            top = top_s[lane]
            weights = [jnp.exp2(near_s[lane, w, :, c * BLK : (c + 1) * BLK] * TO_EXP2 - top) for c in range(FB)]
            weight = jnp.concatenate([p.astype(jnp.bfloat16) for p in weights], axis=1)
            sum_s[lane] += jnp.dot(weight, v_s[n, near_rows(which, w), :], preferred_element_type=jnp.float32)
        return carry

    lax.fori_loop(0, nears, near_weights, 0)

    def far_weights(i, carry):
        for lane, (n, which) in enumerate(lanes):
            for r in range(FB):
                rows = slice(r * BLK, (r + 1) * BLK)
                top = top_s[lane, rows, :]
                part = None
                for j in range(2):
                    weight = jnp.exp2(far_s[lane, r, 2 * i + j] * TO_EXP2 - top).astype(jnp.bfloat16)
                    value = v_s[n, far_rows(which, r, 2 * i + j), :]
                    added = jnp.dot(weight, value, preferred_element_type=jnp.float32)
                    part = added if part is None else part + added
                sum_s[lane, rows, :] += part
        return carry

    lax.fori_loop(0, pairs, far_weights, 0)
    for lane, (n, which) in enumerate(lanes):
        total = sum_s[lane, :, DH:]
        o_s[2 * n + which] = sum_s[lane, :, :DH] / total
        lse_s[2 * n + which] = top_s[lane] + jnp.log(total) * LOG2E


def attend_kernel(heads, first, planes, seq_ref, near_ref, blocks_ref, count_ref, q_ref, q_other_ref, *refs):
    piece_refs = refs[:planes]
    keep_o, keep_lse, send = refs[planes : planes + 3]
    q_s, o_s, lse_s, k_s, v_s, near_s, far_s, top_s, sum_s = refs[planes + 3 :]
    z = lax.div(seq_ref[0], 2)
    v_s[:, :, DH:] = jnp.ones((len(heads), planes * ROWS, DH), jnp.bfloat16)
    for d, piece in enumerate(piece_refs):
        rows = pl.ds(pl.multiple_of(lax.rem(z + planes - d, planes) * ROWS, ROWS), ROWS)
        for n in range(len(heads)):
            at = 2 * (first + n) * ROWS
            k_s[n, rows, :] = piece[at : at + ROWS, :]
            v_s[n, rows, 0:DH] = piece[at + ROWS : at + 2 * ROWS, :]
    for n, head in enumerate(heads):
        columns = slice(head * DH, (head + 1) * DH)
        q_s[2 * n] = q_ref[:, columns]
        q_s[2 * n + 1] = q_other_ref[:, columns]
    tables = (near_ref, blocks_ref, count_ref, q_s, o_s, lse_s, k_s, v_s, near_s, far_s, top_s, sum_s)
    if len(heads) == 1:
        attend_lanes([(0, 0), (0, 1)], *tables)
    else:

        def one(which, carry):
            attend_lanes([(n, which) for n in range(len(heads))], *tables)
            return carry

        lax.fori_loop(0, 2, one, 0)
    lane = lax.broadcasted_iota(jnp.int32, (ROWS, DH), 1)
    for n in range(len(heads)):
        rows = slice(n * ROWS, (n + 1) * ROWS)
        keep_o[rows, :] = o_s[2 * n]
        keep_lse[rows, :] = lse_s[2 * n]
        send[2 * n * ROWS : (2 * n + 1) * ROWS, :] = o_s[2 * n + 1].astype(jnp.bfloat16)
        left = lse_s[2 * n + 1]
        packed = jnp.zeros((ROWS, DH), jnp.float32)
        for term in range(3):
            piece = left.astype(jnp.bfloat16).astype(jnp.float32)
            packed = jnp.where(lane == term, piece, packed)
            left = left - piece
        send[(2 * n + 1) * ROWS : (2 * n + 2) * ROWS, :] = packed.astype(jnp.bfloat16)


def attend(heads, first, queries, queries_other, pieces, seq, near, blocks, counts):
    planes, held = len(pieces), len(heads)
    lanes = max(held, 2)
    tokens = planes * ROWS
    each = pltpu.VMEM((2 * held, ROWS, DH), jnp.float32)
    elements = held * ROWS * 18 * BLK
    return pl.pallas_call(
        functools.partial(attend_kernel, heads, first, planes),
        out_shape=[
            jax.ShapeDtypeStruct((held * ROWS, DH), jnp.float32),
            jax.ShapeDtypeStruct((held * ROWS, DH), jnp.float32),
            jax.ShapeDtypeStruct((2 * held * ROWS, DH), jnp.bfloat16),
        ],
        in_specs=[SMEM] * 4 + [VMEM] * (2 + planes),
        out_specs=[VMEM] * 3,
        scratch_shapes=[
            pltpu.VMEM((2 * held, ROWS, DH), jnp.bfloat16),
            each,
            each,
            pltpu.VMEM((held, tokens, DH), jnp.bfloat16),
            pltpu.VMEM((held, tokens, 2 * DH), jnp.bfloat16),
            pltpu.VMEM((lanes, MAX_NEAR, ROWS, ROWS), jnp.float32),
            pltpu.VMEM((lanes, FB, MAX_EXTRA, BLK, BLK), jnp.float32),
            pltpu.VMEM((lanes, ROWS, BLK), jnp.float32),
            pltpu.VMEM((lanes, ROWS, 2 * DH), jnp.float32),
        ],
        compiler_params=pltpu.CompilerParams(vmem_limit_bytes=(36 if held > 2 else 24) << 20),
        cost_estimate=pl.CostEstimate(
            flops=40 * elements * DH, bytes_accessed=4 * held * tokens * DH, transcendentals=elements
        ),
        name="attend",
    )(seq, near, blocks, counts, queries, queries_other, *pieces)


def merge_kernel(*refs):
    out_ref, parts = refs[-1], refs[:-1]
    column = 0
    for o_ref, lse_ref, got_ref in zip(parts[0::3], parts[1::3], parts[2::3]):
        for n in range(o_ref.shape[0] // ROWS):
            rows = slice(n * ROWS, (n + 1) * ROWS)
            other_o = got_ref[2 * n * ROWS : (2 * n + 1) * ROWS, :].astype(jnp.float32)
            packed = got_ref[(2 * n + 1) * ROWS : (2 * n + 2) * ROWS, :].astype(jnp.float32)
            other_lse = jnp.sum(packed, axis=1, keepdims=True)
            lse = lse_ref[rows, :]
            top = jnp.maximum(lse, other_lse)
            mine, other = jnp.exp2(lse - top), jnp.exp2(other_lse - top)
            out = ((o_ref[rows, :] * mine + other_o * other) / (mine + other)).astype(out_ref.dtype)
            out_ref[:, column : column + DH] = out
            column += DH


def merge(*parts):
    size = sum(part.size for part in parts[0::3])
    return pl.pallas_call(
        merge_kernel,
        out_shape=jax.ShapeDtypeStruct((ROWS, size // ROWS), jnp.bfloat16),
        in_specs=[VMEM] * len(parts),
        out_specs=VMEM,
        compiler_params=pltpu.CompilerParams(vmem_limit_bytes=10 << 20),
        cost_estimate=pl.CostEstimate(flops=8 * size, bytes_accessed=30 * size, transcendentals=2 * size),
        name="merge",
    )(*parts)


def tile_kernel(count, y_ref, pair_ref, weight_ref, *refs):
    outs, sems = refs[:-1], refs[-1]
    width = outs[0].shape[1]
    copies = []
    for n, out in enumerate(outs):
        block = pair_ref[0] if n < count else 1 - pair_ref[0]
        start = pl.multiple_of((lax.rem(y_ref[0] + n, count) * 2 + block) * width, width)
        copies.append(pltpu.make_async_copy(weight_ref.at[:, pl.ds(start, width)], out, sems.at[n]))
    for copy in copies:
        copy.start()
    for copy in copies:
        copy.wait()


def tile(y, pair, weight, count):
    stay = pl.BlockSpec(memory_space=pl.ANY)
    shape = (weight.shape[0], weight.shape[1] // (2 * count))
    return pl.pallas_call(
        functools.partial(tile_kernel, count),
        out_shape=[jax.ShapeDtypeStruct(shape, weight.dtype)] * (count + 1),
        in_specs=[SMEM, SMEM, stay],
        out_specs=[stay] * (count + 1),
        scratch_shapes=[pltpu.SemaphoreType.DMA((count + 1,))],
        compiler_params=pltpu.CompilerParams(vmem_limit_bytes=1 << 20),
        cost_estimate=pl.CostEstimate(flops=0, bytes_accessed=4 * weight.size, transcendentals=0),
        name="tile",
    )(y, pair, weight)


def cross_kernel(q_ref, k_ref, v_ref, o_ref):
    def one(h, carry):
        columns = pl.ds(pl.multiple_of(h * DH, DH), DH)
        score = lax.dot_general(q_ref[:, columns], k_ref[:, columns], NT, preferred_element_type=jnp.float32)
        top = jnp.max(score, axis=1, keepdims=True) * TO_EXP2
        weight = jnp.exp2(score * TO_EXP2 - top)
        total = jnp.sum(weight, axis=1, keepdims=True)
        part = jnp.dot(weight.astype(jnp.bfloat16), v_ref[:, columns], preferred_element_type=jnp.float32)
        o_ref[:, columns] = (part / total).astype(o_ref.dtype)
        return carry

    lax.fori_loop(0, q_ref.shape[1] // DH, one, 0)


def cross(cross_query, text_keys, text_values):
    elements = cross_query.shape[0] * cross_query.shape[1] // DH * text_keys.shape[0]
    return pl.pallas_call(
        cross_kernel,
        out_shape=jax.ShapeDtypeStruct(cross_query.shape, jnp.bfloat16),
        in_specs=[VMEM] * 3,
        out_specs=VMEM,
        compiler_params=pltpu.CompilerParams(vmem_limit_bytes=8 << 20),
        cost_estimate=pl.CostEstimate(
            flops=40 * elements * DH, bytes_accessed=4 * cross_query.size, transcendentals=elements
        ),
        name="cross",
    )(cross_query, text_keys, text_values)


def project_kernel(first, sources, last, *refs):
    keep_ref = refs[0] if last else None
    refs = refs[1:] if last else refs
    heads, weights, refs = refs[:sources], refs[sources : 3 * sources], refs[3 * sources :]
    depth = heads[0].shape[1]
    rows = slice(first * DH, first * DH + depth)
    total_ref = refs[-1]
    for block in range(2):
        total = refs[0][block] if len(refs) > 1 + 2 * last else None
        for head_ref, weight_ref in zip(heads, weights[block::2]):
            part = jnp.dot(head_ref[...], weight_ref[rows, :], preferred_element_type=jnp.float32)
            total = part if total is None else total + part
        total_ref[block] = total
    if last:
        refs[-3][...] = total_ref[keep_ref[0]]
        refs[-2][...] = total_ref[1 - keep_ref[0]].astype(jnp.bfloat16)


def project(first, heads, weights, before=None, keep=None):
    rows, depth = heads[0].shape
    width = weights[0].shape[1]
    given = [*heads, *weights] + ([] if before is None else [before])
    both = jax.ShapeDtypeStruct((2, rows, width), jnp.float32)
    split = [jax.ShapeDtypeStruct((rows, width), dtype) for dtype in (jnp.float32, jnp.bfloat16)]
    last = keep is not None
    return pl.pallas_call(
        functools.partial(project_kernel, first, len(heads), last),
        out_shape=split if last else both,
        in_specs=[SMEM] * last + [VMEM] * len(given),
        out_specs=[VMEM] * 2 if last else VMEM,
        scratch_shapes=[pltpu.VMEM(both.shape, both.dtype)] if last else [],
        compiler_params=pltpu.CompilerParams(vmem_limit_bytes=22 << 20),
        cost_estimate=pl.CostEstimate(
            flops=4 * len(heads) * rows * depth * width,
            bytes_accessed=2 * len(heads) * depth * (rows + 2 * width),
            transcendentals=0,
        ),
        name="project",
    )(*([keep] if last else []), *given)


def body(n_seq, n_head, queries, keys, values, cross_query, text_keys, text_values, out_weight, block_list, block_count):
    n_z, n_y = n_seq // 2, n_head // 2
    seq = lax.axis_index("seq").reshape(1)
    head = lax.axis_index("head").reshape(1)
    pair = lax.axis_index("pair").reshape(1)
    cross_heads = cross(cross_query, text_keys, text_values)
    swap = [(s, s ^ 1) for s in range(n_seq)]

    def to_other(array):
        return lax.ppermute(array, "seq", swap)

    def z_shift(step):
        return [(s, (s // 2 + step) % n_z * 2 + s % 2) for s in range(n_seq)]

    def y_shift(step):
        return [(g, (g // 2 + step) % n_y * 2 + g % 2) for g in range(n_head)]

    held = [{0: array} for array in pack(keys, values)]
    sent = {1: [], -1: []}

    def hop(way, group, step, after=None):
        done = sent[way]
        array = held[group][way * (step - 1) % n_z]
        if len(done) >= IN_FLIGHT:
            at, where = done[-IN_FLIGHT]
            array, held[at][where] = lax.optimization_barrier((array, held[at][where]))
        if after is not None:
            array, after[0] = lax.optimization_barrier((array, after[0]))
        place = way * step % n_z
        held[group][place] = lax.ppermute(array, "seq", z_shift(way))
        done.append((group, place))

    def partial(group, start, stop):
        pieces = [held[group][d] for d in range(n_z)]
        return list(attend(GROUPS[group][start:stop], start, queries, queries_other, pieces, seq, near, blocks, counts))

    def join(part):
        return merge(*part[:2], to_other(part[2]))

    def along_y(array):
        return [array] + [lax.ppermute(array, "head", y_shift(-dy)) for dy in range(1, n_y)]

    for group in (0, 1):
        hop(1, group, 1)
        hop(-1, group, 1)
    queries_other = to_other(queries)
    early = list(plan(n_seq, seq, block_list, block_count))
    tiles = list(tile(lax.div(head, 2), pair, out_weight, n_y))
    early[0], tiles[0] = lax.optimization_barrier((early[0], tiles[0]))
    hop(1, 0, 2, early)
    hop(-1, 0, 2)
    blocks, counts, near = early
    tiles[1:n_y] = [lax.ppermute(tiles[dy], "head", y_shift(dy)) for dy in range(1, n_y)][::-1]
    hop(1, 0, 3)
    hop(-1, 0, 3)
    far_tiles = [lax.optimization_barrier(tuple(tiles[1:n_y]))]
    hop(1, 0, 4, far_tiles)
    hop(-1, 1, 2)
    weights = [tiles[0], tiles[n_y]]
    for mine in far_tiles[0]:
        weights += [mine, lax.ppermute(mine, "pair", [(0, 1), (1, 0)])]
    hop(1, 1, 2)
    hop(-1, 1, 3)
    most = partial(0, 0, 3)
    hop(1, 1, 3, most)
    hop(-1, 1, 4, most)
    before = project(GROUPS[0][0], along_y(join(most)), weights)
    one, two = partial(1, 0, 1), partial(1, 1, 2)
    before = project(GROUPS[1][0], along_y(join(one)), weights, before)
    keep_block = (lax.rem(head, 2) != pair).astype(jnp.int32)
    keep, send = project(GROUPS[1][1], along_y(join(two)), weights, before, keep_block)
    got = lax.ppermute(send, "head", [(g, g ^ 1) for g in range(n_head)])
    return (keep + got.astype(jnp.float32)).astype(jnp.bfloat16), cross_heads


def solution(mesh):
    rows = P(("pair", "seq"), "head")
    text = P("pair", "head")
    return jax.shard_map(
        functools.partial(body, mesh.shape["seq"], mesh.shape["head"]),
        mesh=mesh,
        in_specs=(rows, rows, rows, rows, text, text, P("head", None), P(), P()),
        out_specs=(rows, rows),
        check_vma=False,
    )
```

```python
import functools
import math

import jax
import jax.numpy as jnp
from jax import lax
from jax.experimental import pallas as pl
from jax.experimental.pallas import tpu as pltpu
from jax.sharding import PartitionSpec as P

DH = 128
BLK = 128
FB = 3
ROWS = FB * BLK
MAX_EXTRA = 12
MAX_NEAR = 3
GROUPS = ((0, 1, 2), (3, 4))
IN_FLIGHT = 2
NEG = -1e30
LOG2E = math.log2(math.e)
TO_EXP2 = DH ** (-0.5) * LOG2E
NT = (((1,), (1,)), ((), ()))
SMEM = pl.BlockSpec(memory_space=pltpu.SMEM)
VMEM = pl.BlockSpec(memory_space=pltpu.VMEM)


def plan_kernel(last, seq_ref, list_ref, count_ref, blocks_out, count_out, near_out):
    side = seq_ref[0] % 2
    for which in range(2):
        frame = seq_ref[0] + which * (1 - 2 * side)
        found = jnp.int32(0)
        for w in range(MAX_NEAR):
            near_out[which * (MAX_NEAR + 1) + w] = 0
        for key_frame in (frame - 1, frame, frame + 1, 0):
            here = (key_frame % 2 == side) & (key_frame >= 0) & (key_frame <= last)
            if isinstance(key_frame, int):
                here &= frame > 1
            near_out[which * (MAX_NEAR + 1) + found] = jnp.where(here, key_frame // 2, 0)
            found += here.astype(jnp.int32)
        near_out[which * (MAX_NEAR + 1) + MAX_NEAR] = found
        for r in range(FB):
            row, out = frame * FB + r, which * FB + r
            for e in range(MAX_EXTRA + 1):
                blocks_out[out, e] = 0

            def one(j, extras, row=row, out=out, frame=frame):
                block = list_ref[row, j]
                key_frame = lax.div(block, FB)
                far = (jnp.abs(key_frame - frame) > 1) & (key_frame > 0) & (key_frame % 2 == side)
                blocks_out[out, extras] = jnp.where(
                    far, lax.div(key_frame, 2) * FB + block - key_frame * FB, 0
                )
                return extras + far.astype(jnp.int32)

            extras = lax.fori_loop(0, count_ref[row], one, jnp.int32(0))
            count_out[out] = extras


def plan(frames, seq, block_list, block_count):
    return pl.pallas_call(
        functools.partial(plan_kernel, frames - 1),
        out_shape=[
            jax.ShapeDtypeStruct((2 * FB, MAX_EXTRA + 1), jnp.int32),
            jax.ShapeDtypeStruct((2 * FB,), jnp.int32),
            jax.ShapeDtypeStruct((2 * (MAX_NEAR + 1),), jnp.int32),
        ],
        in_specs=[SMEM] * 3,
        out_specs=[SMEM] * 3,
        compiler_params=pltpu.CompilerParams(vmem_limit_bytes=1 << 20),
        cost_estimate=pl.CostEstimate(flops=1000, bytes_accessed=8000, transcendentals=0),
        name="plan",
    )(seq, block_list, block_count)


def pack_kernel(k_ref, v_ref, *outs):
    for heads, out in zip(GROUPS, outs):
        for n, head in enumerate(heads):
            columns = slice(head * DH, (head + 1) * DH)
            out[2 * n * ROWS : (2 * n + 1) * ROWS, :] = k_ref[:, columns]
            out[(2 * n + 1) * ROWS : (2 * n + 2) * ROWS, :] = v_ref[:, columns]


def pack(keys, values):
    return pl.pallas_call(
        pack_kernel,
        out_shape=[jax.ShapeDtypeStruct((2 * ROWS * len(heads), DH), jnp.bfloat16) for heads in GROUPS],
        in_specs=[VMEM, VMEM],
        out_specs=[VMEM] * len(GROUPS),
        compiler_params=pltpu.CompilerParams(vmem_limit_bytes=6 << 20),
        cost_estimate=pl.CostEstimate(flops=0, bytes_accessed=4 * keys.size * 2, transcendentals=0),
        name="pack",
    )(keys, values)


def attend_lanes(lanes, near_ref, blocks_ref, count_ref, q_s, o_s, lse_s, k_s, v_s, near_s, far_s, top_s, sum_s):
    frames = sorted({which for _, which in lanes}, key=str) if all(isinstance(w, int) for _, w in lanes) else [lanes[0][1]]
    nears = near_ref[frames[0] * (MAX_NEAR + 1) + MAX_NEAR]
    most = count_ref[frames[0] * FB]
    for which in frames:
        nears = jnp.maximum(nears, near_ref[which * (MAX_NEAR + 1) + MAX_NEAR])
        for r in range(FB):
            most = jnp.maximum(most, count_ref[which * FB + r])
    pairs = lax.div(most + 1, 2)

    def near_rows(which, w):
        return pl.ds(pl.multiple_of(near_ref[which * (MAX_NEAR + 1) + w] * ROWS, ROWS), ROWS)

    def far_rows(which, r, e):
        return pl.ds(pl.multiple_of(blocks_ref[which * FB + r, e] * BLK, BLK), BLK)

    top_s[...] = jnp.full_like(top_s, NEG)

    def near_scores(w, carry):
        for lane, (n, which) in enumerate(lanes):
            score = lax.dot_general(
                q_s[2 * n + which], k_s[n, near_rows(which, w), :], NT, preferred_element_type=jnp.float32
            )
            if len(frames) > 1:
                score = jnp.where(w < near_ref[which * (MAX_NEAR + 1) + MAX_NEAR], score, NEG)
            near_s[lane, w] = score
            best = jnp.maximum(jnp.maximum(score[:, :BLK], score[:, BLK : 2 * BLK]), score[:, 2 * BLK :])
            top_s[lane] = jnp.maximum(top_s[lane], best)
        return carry

    lax.fori_loop(0, nears, near_scores, 0)

    def far_scores(i, carry):
        for lane, (n, which) in enumerate(lanes):
            for r in range(FB):
                rows = slice(r * BLK, (r + 1) * BLK)
                best = top_s[lane, rows, :]
                for j in range(2):
                    e = 2 * i + j
                    score = lax.dot_general(
                        q_s[2 * n + which, rows, :], k_s[n, far_rows(which, r, e), :], NT, preferred_element_type=jnp.float32
                    )
                    score = jnp.where(e < count_ref[which * FB + r], score, NEG)
                    far_s[lane, r, e] = score
                    best = jnp.maximum(best, score)
                top_s[lane, rows, :] = best
        return carry

    lax.fori_loop(0, pairs, far_scores, 0)
    for lane in range(len(lanes)):
        top_s[lane] = jnp.broadcast_to(jnp.max(top_s[lane], axis=1, keepdims=True) * TO_EXP2, (ROWS, BLK))
    sum_s[...] = jnp.zeros_like(sum_s)

    def near_weights(w, carry):
        for lane, (n, which) in enumerate(lanes):
            top = top_s[lane]
            weights = [jnp.exp2(near_s[lane, w, :, c * BLK : (c + 1) * BLK] * TO_EXP2 - top) for c in range(FB)]
            weight = jnp.concatenate([p.astype(jnp.bfloat16) for p in weights], axis=1)
            sum_s[lane] += jnp.dot(weight, v_s[n, near_rows(which, w), :], preferred_element_type=jnp.float32)
        return carry

    lax.fori_loop(0, nears, near_weights, 0)

    def far_weights(i, carry):
        for lane, (n, which) in enumerate(lanes):
            for r in range(FB):
                rows = slice(r * BLK, (r + 1) * BLK)
                top = top_s[lane, rows, :]
                part = None
                for j in range(2):
                    weight = jnp.exp2(far_s[lane, r, 2 * i + j] * TO_EXP2 - top).astype(jnp.bfloat16)
                    value = v_s[n, far_rows(which, r, 2 * i + j), :]
                    added = jnp.dot(weight, value, preferred_element_type=jnp.float32)
                    part = added if part is None else part + added
                sum_s[lane, rows, :] += part
        return carry

    lax.fori_loop(0, pairs, far_weights, 0)
    for lane, (n, which) in enumerate(lanes):
        total = sum_s[lane, :, DH:]
        o_s[2 * n + which] = sum_s[lane, :, :DH] / total
        lse_s[2 * n + which] = top_s[lane] + jnp.log(total) * LOG2E


def attend_kernel(heads, first, planes, seq_ref, near_ref, blocks_ref, count_ref, q_ref, q_other_ref, *refs):
    piece_refs = refs[:planes]
    keep_o, keep_lse, send = refs[planes : planes + 3]
    q_s, o_s, lse_s, k_s, v_s, near_s, far_s, top_s, sum_s = refs[planes + 3 :]
    z = lax.div(seq_ref[0], 2)
    v_s[:, :, DH:] = jnp.ones((len(heads), planes * ROWS, DH), jnp.bfloat16)
    for d, piece in enumerate(piece_refs):
        rows = pl.ds(pl.multiple_of(lax.rem(z + planes - d, planes) * ROWS, ROWS), ROWS)
        for n in range(len(heads)):
            at = 2 * (first + n) * ROWS
            k_s[n, rows, :] = piece[at : at + ROWS, :]
            v_s[n, rows, 0:DH] = piece[at + ROWS : at + 2 * ROWS, :]
    for n, head in enumerate(heads):
        columns = slice(head * DH, (head + 1) * DH)
        q_s[2 * n] = q_ref[:, columns]
        q_s[2 * n + 1] = q_other_ref[:, columns]
    tables = (near_ref, blocks_ref, count_ref, q_s, o_s, lse_s, k_s, v_s, near_s, far_s, top_s, sum_s)
    if len(heads) == 1:
        attend_lanes([(0, 0), (0, 1)], *tables)
    else:

        def one(which, carry):
            attend_lanes([(n, which) for n in range(len(heads))], *tables)
            return carry

        lax.fori_loop(0, 2, one, 0)
    lane = lax.broadcasted_iota(jnp.int32, (ROWS, DH), 1)
    for n in range(len(heads)):
        rows = slice(n * ROWS, (n + 1) * ROWS)
        keep_o[rows, :] = o_s[2 * n]
        keep_lse[rows, :] = lse_s[2 * n]
        send[2 * n * ROWS : (2 * n + 1) * ROWS, :] = o_s[2 * n + 1].astype(jnp.bfloat16)
        left = lse_s[2 * n + 1]
        packed = jnp.zeros((ROWS, DH), jnp.float32)
        for term in range(3):
            piece = left.astype(jnp.bfloat16).astype(jnp.float32)
            packed = jnp.where(lane == term, piece, packed)
            left = left - piece
        send[(2 * n + 1) * ROWS : (2 * n + 2) * ROWS, :] = packed.astype(jnp.bfloat16)


def attend(heads, first, queries, queries_other, pieces, seq, near, blocks, counts):
    planes, held = len(pieces), len(heads)
    lanes = max(held, 2)
    tokens = planes * ROWS
    each = pltpu.VMEM((2 * held, ROWS, DH), jnp.float32)
    elements = held * ROWS * 18 * BLK
    return pl.pallas_call(
        functools.partial(attend_kernel, heads, first, planes),
        out_shape=[
            jax.ShapeDtypeStruct((held * ROWS, DH), jnp.float32),
            jax.ShapeDtypeStruct((held * ROWS, DH), jnp.float32),
            jax.ShapeDtypeStruct((2 * held * ROWS, DH), jnp.bfloat16),
        ],
        in_specs=[SMEM] * 4 + [VMEM] * (2 + planes),
        out_specs=[VMEM] * 3,
        scratch_shapes=[
            pltpu.VMEM((2 * held, ROWS, DH), jnp.bfloat16),
            each,
            each,
            pltpu.VMEM((held, tokens, DH), jnp.bfloat16),
            pltpu.VMEM((held, tokens, 2 * DH), jnp.bfloat16),
            pltpu.VMEM((lanes, MAX_NEAR, ROWS, ROWS), jnp.float32),
            pltpu.VMEM((lanes, FB, MAX_EXTRA, BLK, BLK), jnp.float32),
            pltpu.VMEM((lanes, ROWS, BLK), jnp.float32),
            pltpu.VMEM((lanes, ROWS, 2 * DH), jnp.float32),
        ],
        compiler_params=pltpu.CompilerParams(vmem_limit_bytes=(36 if held > 2 else 24) << 20),
        cost_estimate=pl.CostEstimate(
            flops=40 * elements * DH, bytes_accessed=4 * held * tokens * DH, transcendentals=elements
        ),
        name="attend",
    )(seq, near, blocks, counts, queries, queries_other, *pieces)


def merge_kernel(*refs):
    out_ref, parts = refs[-1], refs[:-1]
    column = 0
    for o_ref, lse_ref, got_ref in zip(parts[0::3], parts[1::3], parts[2::3]):
        for n in range(o_ref.shape[0] // ROWS):
            rows = slice(n * ROWS, (n + 1) * ROWS)
            other_o = got_ref[2 * n * ROWS : (2 * n + 1) * ROWS, :].astype(jnp.float32)
            packed = got_ref[(2 * n + 1) * ROWS : (2 * n + 2) * ROWS, :].astype(jnp.float32)
            other_lse = jnp.sum(packed, axis=1, keepdims=True)
            lse = lse_ref[rows, :]
            top = jnp.maximum(lse, other_lse)
            mine, other = jnp.exp2(lse - top), jnp.exp2(other_lse - top)
            out = ((o_ref[rows, :] * mine + other_o * other) / (mine + other)).astype(out_ref.dtype)
            out_ref[:, column : column + DH] = out
            column += DH


def merge(*parts):
    size = sum(part.size for part in parts[0::3])
    return pl.pallas_call(
        merge_kernel,
        out_shape=jax.ShapeDtypeStruct((ROWS, size // ROWS), jnp.bfloat16),
        in_specs=[VMEM] * len(parts),
        out_specs=VMEM,
        compiler_params=pltpu.CompilerParams(vmem_limit_bytes=10 << 20),
        cost_estimate=pl.CostEstimate(flops=8 * size, bytes_accessed=30 * size, transcendentals=2 * size),
        name="merge",
    )(*parts)


def tile_kernel(count, y_ref, pair_ref, weight_ref, *refs):
    outs, sems = refs[:-1], refs[-1]
    width = outs[0].shape[1]
    copies = []
    for n, out in enumerate(outs):
        block = pair_ref[0] if n < count else 1 - pair_ref[0]
        start = pl.multiple_of((lax.rem(y_ref[0] + n, count) * 2 + block) * width, width)
        copies.append(pltpu.make_async_copy(weight_ref.at[:, pl.ds(start, width)], out, sems.at[n]))
    for copy in copies:
        copy.start()
    for copy in copies:
        copy.wait()


def tile(y, pair, weight, count):
    stay = pl.BlockSpec(memory_space=pl.ANY)
    shape = (weight.shape[0], weight.shape[1] // (2 * count))
    return pl.pallas_call(
        functools.partial(tile_kernel, count),
        out_shape=[jax.ShapeDtypeStruct(shape, weight.dtype)] * (count + 1),
        in_specs=[SMEM, SMEM, stay],
        out_specs=[stay] * (count + 1),
        scratch_shapes=[pltpu.SemaphoreType.DMA((count + 1,))],
        compiler_params=pltpu.CompilerParams(vmem_limit_bytes=1 << 20),
        cost_estimate=pl.CostEstimate(flops=0, bytes_accessed=4 * weight.size, transcendentals=0),
        name="tile",
    )(y, pair, weight)


def cross_kernel(q_ref, k_ref, v_ref, o_ref):
    def one(h, carry):
        columns = pl.ds(pl.multiple_of(h * DH, DH), DH)
        score = lax.dot_general(q_ref[:, columns], k_ref[:, columns], NT, preferred_element_type=jnp.float32)
        top = jnp.max(score, axis=1, keepdims=True) * TO_EXP2
        weight = jnp.exp2(score * TO_EXP2 - top)
        total = jnp.sum(weight, axis=1, keepdims=True)
        part = jnp.dot(weight.astype(jnp.bfloat16), v_ref[:, columns], preferred_element_type=jnp.float32)
        o_ref[:, columns] = (part / total).astype(o_ref.dtype)
        return carry

    lax.fori_loop(0, q_ref.shape[1] // DH, one, 0)


def cross(cross_query, text_keys, text_values):
    elements = cross_query.shape[0] * cross_query.shape[1] // DH * text_keys.shape[0]
    return pl.pallas_call(
        cross_kernel,
        out_shape=jax.ShapeDtypeStruct(cross_query.shape, jnp.bfloat16),
        in_specs=[VMEM] * 3,
        out_specs=VMEM,
        compiler_params=pltpu.CompilerParams(vmem_limit_bytes=8 << 20),
        cost_estimate=pl.CostEstimate(
            flops=40 * elements * DH, bytes_accessed=4 * cross_query.size, transcendentals=elements
        ),
        name="cross",
    )(cross_query, text_keys, text_values)


def project_kernel(first, sources, last, *refs):
    keep_ref = refs[0] if last else None
    refs = refs[1:] if last else refs
    heads, weights, refs = refs[:sources], refs[sources : 3 * sources], refs[3 * sources :]
    depth = heads[0].shape[1]
    rows = slice(first * DH, first * DH + depth)
    total_ref = refs[-1]
    for block in range(2):
        total = refs[0][block] if len(refs) > 1 + 2 * last else None
        for head_ref, weight_ref in zip(heads, weights[block::2]):
            part = jnp.dot(head_ref[...], weight_ref[rows, :], preferred_element_type=jnp.float32)
            total = part if total is None else total + part
        total_ref[block] = total
    if last:
        refs[-3][...] = total_ref[keep_ref[0]]
        refs[-2][...] = total_ref[1 - keep_ref[0]].astype(jnp.bfloat16)


def project(first, heads, weights, before=None, keep=None):
    rows, depth = heads[0].shape
    width = weights[0].shape[1]
    given = [*heads, *weights] + ([] if before is None else [before])
    both = jax.ShapeDtypeStruct((2, rows, width), jnp.float32)
    split = [jax.ShapeDtypeStruct((rows, width), dtype) for dtype in (jnp.float32, jnp.bfloat16)]
    last = keep is not None
    return pl.pallas_call(
        functools.partial(project_kernel, first, len(heads), last),
        out_shape=split if last else both,
        in_specs=[SMEM] * last + [VMEM] * len(given),
        out_specs=[VMEM] * 2 if last else VMEM,
        scratch_shapes=[pltpu.VMEM(both.shape, both.dtype)] if last else [],
        compiler_params=pltpu.CompilerParams(vmem_limit_bytes=22 << 20),
        cost_estimate=pl.CostEstimate(
            flops=4 * len(heads) * rows * depth * width,
            bytes_accessed=2 * len(heads) * depth * (rows + 2 * width),
            transcendentals=0,
        ),
        name="project",
    )(*([keep] if last else []), *given)


def body(n_seq, n_head, queries, keys, values, cross_query, text_keys, text_values, out_weight, block_list, block_count):
    n_z, n_y = n_seq // 2, n_head // 2
    seq = lax.axis_index("seq").reshape(1)
    head = lax.axis_index("head").reshape(1)
    pair = lax.axis_index("pair").reshape(1)
    cross_heads = cross(cross_query, text_keys, text_values)
    swap = [(s, s ^ 1) for s in range(n_seq)]

    def to_other(array):
        return lax.ppermute(array, "seq", swap)

    def z_shift(step):
        return [(s, (s // 2 + step) % n_z * 2 + s % 2) for s in range(n_seq)]

    def y_shift(step):
        return [(g, (g // 2 + step) % n_y * 2 + g % 2) for g in range(n_head)]

    held = [{0: array} for array in pack(keys, values)]
    sent = {1: [], -1: []}

    def hop(way, group, step, after=None):
        done = sent[way]
        array = held[group][way * (step - 1) % n_z]
        if len(done) >= IN_FLIGHT:
            at, where = done[-IN_FLIGHT]
            array, held[at][where] = lax.optimization_barrier((array, held[at][where]))
        if after is not None:
            array, after[0] = lax.optimization_barrier((array, after[0]))
        place = way * step % n_z
        held[group][place] = lax.ppermute(array, "seq", z_shift(way))
        done.append((group, place))

    def partial(group, start, stop):
        pieces = [held[group][d] for d in range(n_z)]
        return list(attend(GROUPS[group][start:stop], start, queries, queries_other, pieces, seq, near, blocks, counts))

    def join(part):
        return merge(*part[:2], to_other(part[2]))

    def along_y(array):
        return [array] + [lax.ppermute(array, "head", y_shift(-dy)) for dy in range(1, n_y)]

    for group in (0, 1):
        hop(1, group, 1)
        hop(-1, group, 1)
    queries_other = to_other(queries)
    early = list(plan(n_seq, seq, block_list, block_count))
    tiles = list(tile(lax.div(head, 2), pair, out_weight, n_y))
    early[0], tiles[0] = lax.optimization_barrier((early[0], tiles[0]))
    hop(1, 0, 2, early)
    hop(-1, 0, 2)
    blocks, counts, near = early
    tiles[1:n_y] = [lax.ppermute(tiles[dy], "head", y_shift(dy)) for dy in range(1, n_y)][::-1]
    one_away = [(tiles[1], tiles[n_y - 1])]
    hop(1, 0, 3, one_away)
    tiles[1], tiles[n_y - 1] = one_away[0]
    hop(-1, 0, 3)
    hop(1, 0, 4)
    hop(-1, 1, 2)
    hop(1, 1, 2)
    hop(-1, 1, 3)
    near, tiles[2] = lax.optimization_barrier((near, tiles[2]))
    weights = [tiles[0], tiles[n_y]]
    for mine in tiles[1:n_y]:
        weights += [mine, lax.ppermute(mine, "pair", [(0, 1), (1, 0)])]
    most = partial(0, 0, 3)
    hop(1, 1, 3, most)
    hop(-1, 1, 4, most)
    before = project(GROUPS[0][0], along_y(join(most)), weights)
    one, two = partial(1, 0, 1), partial(1, 1, 2)
    two = join(two)
    before, two = lax.optimization_barrier((before, two))
    before = project(GROUPS[1][0], along_y(join(one)), weights, before)
    keep_block = (lax.rem(head, 2) != pair).astype(jnp.int32)
    keep, send = project(GROUPS[1][1], along_y(two), weights, before, keep_block)
    got = lax.ppermute(send, "head", [(g, g ^ 1) for g in range(n_head)])
    return (keep + got.astype(jnp.float32)).astype(jnp.bfloat16), cross_heads


def solution(mesh):
    rows = P(("pair", "seq"), "head")
    text = P("pair", "head")
    return jax.shard_map(
        functools.partial(body, mesh.shape["seq"], mesh.shape["head"]),
        mesh=mesh,
        in_specs=(rows, rows, rows, rows, text, text, P("head", None), P(), P()),
        out_specs=(rows, rows),
        check_vma=False,
    )
```

```python
import functools
import math

import jax
import jax.numpy as jnp
from jax import lax
from jax.experimental import pallas as pl
from jax.experimental.pallas import tpu as pltpu
from jax.sharding import PartitionSpec as P

DH = 128
BLK = 128
FB = 3
ROWS = FB * BLK
MAX_EXTRA = 12
MAX_NEAR = 3
GROUPS = ((0, 1, 2), (3, 4))
IN_FLIGHT = 2
NEG = -1e30
LOG2E = math.log2(math.e)
TO_EXP2 = DH ** (-0.5) * LOG2E
NT = (((1,), (1,)), ((), ()))
SMEM = pl.BlockSpec(memory_space=pltpu.SMEM)
VMEM = pl.BlockSpec(memory_space=pltpu.VMEM)


def plan_kernel(last, seq_ref, list_ref, count_ref, blocks_out, count_out, near_out):
    side = seq_ref[0] % 2
    for which in range(2):
        frame = seq_ref[0] + which * (1 - 2 * side)
        found = jnp.int32(0)
        for w in range(MAX_NEAR):
            near_out[which * (MAX_NEAR + 1) + w] = 0
        for key_frame in (frame - 1, frame, frame + 1, 0):
            here = (key_frame % 2 == side) & (key_frame >= 0) & (key_frame <= last)
            if isinstance(key_frame, int):
                here &= frame > 1
            near_out[which * (MAX_NEAR + 1) + found] = jnp.where(here, key_frame // 2, 0)
            found += here.astype(jnp.int32)
        near_out[which * (MAX_NEAR + 1) + MAX_NEAR] = found
        for r in range(FB):
            row, out = frame * FB + r, which * FB + r
            for e in range(MAX_EXTRA + 1):
                blocks_out[out, e] = 0

            def one(j, extras, row=row, out=out, frame=frame):
                block = list_ref[row, j]
                key_frame = lax.div(block, FB)
                far = (jnp.abs(key_frame - frame) > 1) & (key_frame > 0) & (key_frame % 2 == side)
                blocks_out[out, extras] = jnp.where(
                    far, lax.div(key_frame, 2) * FB + block - key_frame * FB, 0
                )
                return extras + far.astype(jnp.int32)

            extras = lax.fori_loop(0, count_ref[row], one, jnp.int32(0))
            count_out[out] = extras


def plan(frames, seq, block_list, block_count):
    return pl.pallas_call(
        functools.partial(plan_kernel, frames - 1),
        out_shape=[
            jax.ShapeDtypeStruct((2 * FB, MAX_EXTRA + 1), jnp.int32),
            jax.ShapeDtypeStruct((2 * FB,), jnp.int32),
            jax.ShapeDtypeStruct((2 * (MAX_NEAR + 1),), jnp.int32),
        ],
        in_specs=[SMEM] * 3,
        out_specs=[SMEM] * 3,
        compiler_params=pltpu.CompilerParams(vmem_limit_bytes=1 << 20),
        cost_estimate=pl.CostEstimate(flops=1000, bytes_accessed=8000, transcendentals=0),
        name="plan",
    )(seq, block_list, block_count)


def pack_kernel(k_ref, v_ref, *outs):
    for heads, out in zip(GROUPS, outs):
        for n, head in enumerate(heads):
            columns = slice(head * DH, (head + 1) * DH)
            out[2 * n * ROWS : (2 * n + 1) * ROWS, :] = k_ref[:, columns]
            out[(2 * n + 1) * ROWS : (2 * n + 2) * ROWS, :] = v_ref[:, columns]


def pack(keys, values):
    return pl.pallas_call(
        pack_kernel,
        out_shape=[jax.ShapeDtypeStruct((2 * ROWS * len(heads), DH), jnp.bfloat16) for heads in GROUPS],
        in_specs=[VMEM, VMEM],
        out_specs=[VMEM] * len(GROUPS),
        compiler_params=pltpu.CompilerParams(vmem_limit_bytes=6 << 20),
        cost_estimate=pl.CostEstimate(flops=0, bytes_accessed=4 * keys.size * 2, transcendentals=0),
        name="pack",
    )(keys, values)


def attend_lanes(lanes, near_ref, blocks_ref, count_ref, q_s, o_s, lse_s, k_s, v_s, near_s, far_s, top_s, sum_s):
    frames = sorted({which for _, which in lanes}, key=str) if all(isinstance(w, int) for _, w in lanes) else [lanes[0][1]]
    nears = near_ref[frames[0] * (MAX_NEAR + 1) + MAX_NEAR]
    most = count_ref[frames[0] * FB]
    for which in frames:
        nears = jnp.maximum(nears, near_ref[which * (MAX_NEAR + 1) + MAX_NEAR])
        for r in range(FB):
            most = jnp.maximum(most, count_ref[which * FB + r])
    pairs = lax.div(most + 1, 2)

    def near_rows(which, w):
        return pl.ds(pl.multiple_of(near_ref[which * (MAX_NEAR + 1) + w] * ROWS, ROWS), ROWS)

    def far_rows(which, r, e):
        return pl.ds(pl.multiple_of(blocks_ref[which * FB + r, e] * BLK, BLK), BLK)

    top_s[...] = jnp.full_like(top_s, NEG)

    def near_scores(w, carry):
        for lane, (n, which) in enumerate(lanes):
            score = lax.dot_general(
                q_s[2 * n + which], k_s[n, near_rows(which, w), :], NT, preferred_element_type=jnp.float32
            )
            if len(frames) > 1:
                score = jnp.where(w < near_ref[which * (MAX_NEAR + 1) + MAX_NEAR], score, NEG)
            near_s[lane, w] = score
            best = jnp.maximum(jnp.maximum(score[:, :BLK], score[:, BLK : 2 * BLK]), score[:, 2 * BLK :])
            top_s[lane] = jnp.maximum(top_s[lane], best)
        return carry

    lax.fori_loop(0, nears, near_scores, 0)

    def far_scores(i, carry):
        for lane, (n, which) in enumerate(lanes):
            for r in range(FB):
                rows = slice(r * BLK, (r + 1) * BLK)
                best = top_s[lane, rows, :]
                for j in range(2):
                    e = 2 * i + j
                    score = lax.dot_general(
                        q_s[2 * n + which, rows, :], k_s[n, far_rows(which, r, e), :], NT, preferred_element_type=jnp.float32
                    )
                    score = jnp.where(e < count_ref[which * FB + r], score, NEG)
                    far_s[lane, r, e] = score
                    best = jnp.maximum(best, score)
                top_s[lane, rows, :] = best
        return carry

    lax.fori_loop(0, pairs, far_scores, 0)
    for lane in range(len(lanes)):
        top_s[lane] = jnp.broadcast_to(jnp.max(top_s[lane], axis=1, keepdims=True) * TO_EXP2, (ROWS, BLK))
    sum_s[...] = jnp.zeros_like(sum_s)

    def near_weights(w, carry):
        for lane, (n, which) in enumerate(lanes):
            top = top_s[lane]
            weights = [jnp.exp2(near_s[lane, w, :, c * BLK : (c + 1) * BLK] * TO_EXP2 - top) for c in range(FB)]
            weight = jnp.concatenate([p.astype(jnp.bfloat16) for p in weights], axis=1)
            sum_s[lane] += jnp.dot(weight, v_s[n, near_rows(which, w), :], preferred_element_type=jnp.float32)
        return carry

    lax.fori_loop(0, nears, near_weights, 0)

    def far_weights(i, carry):
        for lane, (n, which) in enumerate(lanes):
            for r in range(FB):
                rows = slice(r * BLK, (r + 1) * BLK)
                top = top_s[lane, rows, :]
                part = None
                for j in range(2):
                    weight = jnp.exp2(far_s[lane, r, 2 * i + j] * TO_EXP2 - top).astype(jnp.bfloat16)
                    value = v_s[n, far_rows(which, r, 2 * i + j), :]
                    added = jnp.dot(weight, value, preferred_element_type=jnp.float32)
                    part = added if part is None else part + added
                sum_s[lane, rows, :] += part
        return carry

    lax.fori_loop(0, pairs, far_weights, 0)
    for lane, (n, which) in enumerate(lanes):
        total = sum_s[lane, :, DH:]
        o_s[2 * n + which] = sum_s[lane, :, :DH] / total
        lse_s[2 * n + which] = top_s[lane] + jnp.log(total) * LOG2E


def attend_kernel(heads, first, planes, seq_ref, near_ref, blocks_ref, count_ref, q_ref, q_other_ref, *refs):
    piece_refs = refs[:planes]
    keep_o, keep_lse, send = refs[planes : planes + 3]
    q_s, o_s, lse_s, k_s, v_s, near_s, far_s, top_s, sum_s = refs[planes + 3 :]
    z = lax.div(seq_ref[0], 2)
    v_s[:, :, DH:] = jnp.ones((len(heads), planes * ROWS, DH), jnp.bfloat16)
    for d, piece in enumerate(piece_refs):
        rows = pl.ds(pl.multiple_of(lax.rem(z + planes - d, planes) * ROWS, ROWS), ROWS)
        for n in range(len(heads)):
            at = 2 * (first + n) * ROWS
            k_s[n, rows, :] = piece[at : at + ROWS, :]
            v_s[n, rows, 0:DH] = piece[at + ROWS : at + 2 * ROWS, :]
    for n, head in enumerate(heads):
        columns = slice(head * DH, (head + 1) * DH)
        q_s[2 * n] = q_ref[:, columns]
        q_s[2 * n + 1] = q_other_ref[:, columns]
    tables = (near_ref, blocks_ref, count_ref, q_s, o_s, lse_s, k_s, v_s, near_s, far_s, top_s, sum_s)
    if len(heads) == 1:
        attend_lanes([(0, 0), (0, 1)], *tables)
    else:

        def one(which, carry):
            attend_lanes([(n, which) for n in range(len(heads))], *tables)
            return carry

        lax.fori_loop(0, 2, one, 0)
    lane = lax.broadcasted_iota(jnp.int32, (ROWS, DH), 1)
    for n in range(len(heads)):
        rows = slice(n * ROWS, (n + 1) * ROWS)
        keep_o[rows, :] = o_s[2 * n]
        keep_lse[rows, :] = lse_s[2 * n]
        send[2 * n * ROWS : (2 * n + 1) * ROWS, :] = o_s[2 * n + 1].astype(jnp.bfloat16)
        left = lse_s[2 * n + 1]
        packed = jnp.zeros((ROWS, DH), jnp.float32)
        for term in range(3):
            piece = left.astype(jnp.bfloat16).astype(jnp.float32)
            packed = jnp.where(lane == term, piece, packed)
            left = left - piece
        send[(2 * n + 1) * ROWS : (2 * n + 2) * ROWS, :] = packed.astype(jnp.bfloat16)


def attend(heads, first, queries, queries_other, pieces, seq, near, blocks, counts):
    planes, held = len(pieces), len(heads)
    lanes = max(held, 2)
    tokens = planes * ROWS
    each = pltpu.VMEM((2 * held, ROWS, DH), jnp.float32)
    elements = held * ROWS * 18 * BLK
    return pl.pallas_call(
        functools.partial(attend_kernel, heads, first, planes),
        out_shape=[
            jax.ShapeDtypeStruct((held * ROWS, DH), jnp.float32),
            jax.ShapeDtypeStruct((held * ROWS, DH), jnp.float32),
            jax.ShapeDtypeStruct((2 * held * ROWS, DH), jnp.bfloat16),
        ],
        in_specs=[SMEM] * 4 + [VMEM] * (2 + planes),
        out_specs=[VMEM] * 3,
        scratch_shapes=[
            pltpu.VMEM((2 * held, ROWS, DH), jnp.bfloat16),
            each,
            each,
            pltpu.VMEM((held, tokens, DH), jnp.bfloat16),
            pltpu.VMEM((held, tokens, 2 * DH), jnp.bfloat16),
            pltpu.VMEM((lanes, MAX_NEAR, ROWS, ROWS), jnp.float32),
            pltpu.VMEM((lanes, FB, MAX_EXTRA, BLK, BLK), jnp.float32),
            pltpu.VMEM((lanes, ROWS, BLK), jnp.float32),
            pltpu.VMEM((lanes, ROWS, 2 * DH), jnp.float32),
        ],
        compiler_params=pltpu.CompilerParams(vmem_limit_bytes=(36 if held > 2 else 24) << 20),
        cost_estimate=pl.CostEstimate(
            flops=40 * elements * DH, bytes_accessed=4 * held * tokens * DH, transcendentals=elements
        ),
        name="attend",
    )(seq, near, blocks, counts, queries, queries_other, *pieces)


def merge_kernel(*refs):
    out_ref, parts = refs[-1], refs[:-1]
    column = 0
    for o_ref, lse_ref, got_ref in zip(parts[0::3], parts[1::3], parts[2::3]):
        for n in range(o_ref.shape[0] // ROWS):
            rows = slice(n * ROWS, (n + 1) * ROWS)
            other_o = got_ref[2 * n * ROWS : (2 * n + 1) * ROWS, :].astype(jnp.float32)
            packed = got_ref[(2 * n + 1) * ROWS : (2 * n + 2) * ROWS, :].astype(jnp.float32)
            other_lse = jnp.sum(packed, axis=1, keepdims=True)
            lse = lse_ref[rows, :]
            top = jnp.maximum(lse, other_lse)
            mine, other = jnp.exp2(lse - top), jnp.exp2(other_lse - top)
            out = ((o_ref[rows, :] * mine + other_o * other) / (mine + other)).astype(out_ref.dtype)
            out_ref[:, column : column + DH] = out
            column += DH


def merge(*parts):
    size = sum(part.size for part in parts[0::3])
    return pl.pallas_call(
        merge_kernel,
        out_shape=jax.ShapeDtypeStruct((ROWS, size // ROWS), jnp.bfloat16),
        in_specs=[VMEM] * len(parts),
        out_specs=VMEM,
        compiler_params=pltpu.CompilerParams(vmem_limit_bytes=10 << 20),
        cost_estimate=pl.CostEstimate(flops=8 * size, bytes_accessed=30 * size, transcendentals=2 * size),
        name="merge",
    )(*parts)


def tile_kernel(count, y_ref, pair_ref, weight_ref, *refs):
    outs, sems = refs[:-1], refs[-1]
    width = outs[0].shape[1]
    copies = []
    for n, out in enumerate(outs):
        block = pair_ref[0] if n < count else 1 - pair_ref[0]
        start = pl.multiple_of((lax.rem(y_ref[0] + n, count) * 2 + block) * width, width)
        copies.append(pltpu.make_async_copy(weight_ref.at[:, pl.ds(start, width)], out, sems.at[n]))
    for copy in copies:
        copy.start()
    for copy in copies:
        copy.wait()


def tile(y, pair, weight, count):
    stay = pl.BlockSpec(memory_space=pl.ANY)
    shape = (weight.shape[0], weight.shape[1] // (2 * count))
    return pl.pallas_call(
        functools.partial(tile_kernel, count),
        out_shape=[jax.ShapeDtypeStruct(shape, weight.dtype)] * (count + 1),
        in_specs=[SMEM, SMEM, stay],
        out_specs=[stay] * (count + 1),
        scratch_shapes=[pltpu.SemaphoreType.DMA((count + 1,))],
        compiler_params=pltpu.CompilerParams(vmem_limit_bytes=1 << 20),
        cost_estimate=pl.CostEstimate(flops=0, bytes_accessed=4 * weight.size, transcendentals=0),
        name="tile",
    )(y, pair, weight)


def cross_kernel(q_ref, k_ref, v_ref, o_ref):
    def one(h, carry):
        columns = pl.ds(pl.multiple_of(h * DH, DH), DH)
        score = lax.dot_general(q_ref[:, columns], k_ref[:, columns], NT, preferred_element_type=jnp.float32)
        top = jnp.max(score, axis=1, keepdims=True) * TO_EXP2
        weight = jnp.exp2(score * TO_EXP2 - top)
        total = jnp.sum(weight, axis=1, keepdims=True)
        part = jnp.dot(weight.astype(jnp.bfloat16), v_ref[:, columns], preferred_element_type=jnp.float32)
        o_ref[:, columns] = (part / total).astype(o_ref.dtype)
        return carry

    lax.fori_loop(0, q_ref.shape[1] // DH, one, 0)


def cross(cross_query, text_keys, text_values):
    elements = cross_query.shape[0] * cross_query.shape[1] // DH * text_keys.shape[0]
    return pl.pallas_call(
        cross_kernel,
        out_shape=jax.ShapeDtypeStruct(cross_query.shape, jnp.bfloat16),
        in_specs=[VMEM] * 3,
        out_specs=VMEM,
        compiler_params=pltpu.CompilerParams(vmem_limit_bytes=8 << 20),
        cost_estimate=pl.CostEstimate(
            flops=40 * elements * DH, bytes_accessed=4 * cross_query.size, transcendentals=elements
        ),
        name="cross",
    )(cross_query, text_keys, text_values)


def project_kernel(first, sources, last, *refs):
    keep_ref = refs[0] if last else None
    refs = refs[1:] if last else refs
    heads, weights, refs = refs[:sources], refs[sources : 3 * sources], refs[3 * sources :]
    depth = heads[0].shape[1]
    rows = slice(first * DH, first * DH + depth)
    total_ref = refs[-1]
    for block in range(2):
        total = refs[0][block] if len(refs) > 1 + 2 * last else None
        for head_ref, weight_ref in zip(heads, weights[block::2]):
            part = jnp.dot(head_ref[...], weight_ref[rows, :], preferred_element_type=jnp.float32)
            total = part if total is None else total + part
        total_ref[block] = total
    if last:
        refs[-3][...] = total_ref[keep_ref[0]]
        refs[-2][...] = total_ref[1 - keep_ref[0]].astype(jnp.bfloat16)


def project(first, heads, weights, before=None, keep=None):
    rows, depth = heads[0].shape
    width = weights[0].shape[1]
    given = [*heads, *weights] + ([] if before is None else [before])
    both = jax.ShapeDtypeStruct((2, rows, width), jnp.float32)
    split = [jax.ShapeDtypeStruct((rows, width), dtype) for dtype in (jnp.float32, jnp.bfloat16)]
    last = keep is not None
    return pl.pallas_call(
        functools.partial(project_kernel, first, len(heads), last),
        out_shape=split if last else both,
        in_specs=[SMEM] * last + [VMEM] * len(given),
        out_specs=[VMEM] * 2 if last else VMEM,
        scratch_shapes=[pltpu.VMEM(both.shape, both.dtype)] if last else [],
        compiler_params=pltpu.CompilerParams(vmem_limit_bytes=22 << 20),
        cost_estimate=pl.CostEstimate(
            flops=4 * len(heads) * rows * depth * width,
            bytes_accessed=2 * len(heads) * depth * (rows + 2 * width),
            transcendentals=0,
        ),
        name="project",
    )(*([keep] if last else []), *given)


def body(n_seq, n_head, queries, keys, values, cross_query, text_keys, text_values, out_weight, block_list, block_count):
    n_z, n_y = n_seq // 2, n_head // 2
    half = n_z // 2
    seq = lax.axis_index("seq").reshape(1)
    head = lax.axis_index("head").reshape(1)
    pair = lax.axis_index("pair").reshape(1)
    cross_heads = cross(cross_query, text_keys, text_values)
    swap = [(s, s ^ 1) for s in range(n_seq)]

    def to_other(array):
        return lax.ppermute(array, "seq", swap)

    def z_shift(step):
        return [(s, (s // 2 + step) % n_z * 2 + s % 2) for s in range(n_seq)]

    def y_shift(step):
        return [(g, (g // 2 + step) % n_y * 2 + g % 2) for g in range(n_head)]

    held = [{0: array} for array in pack(keys, values)]
    sent = {1: [], -1: []}

    def hop(way, group, step, after=None):
        done = sent[way]
        array = held[group][way * (step - 1) % n_z]
        if len(done) >= IN_FLIGHT:
            at, where = done[-IN_FLIGHT]
            array, held[at][where] = lax.optimization_barrier((array, held[at][where]))
        if after is not None:
            array, after[0] = lax.optimization_barrier((array, after[0]))
        place = way * step % n_z
        held[group][place] = lax.ppermute(array, "seq", z_shift(way))
        done.append((group, place))

    def partial(group, start, stop):
        pieces = [held[group][d] for d in range(n_z)]
        return list(attend(GROUPS[group][start:stop], start, queries, queries_other, pieces, seq, near, blocks, counts))

    def join(part):
        return merge(*part[:2], to_other(part[2]))

    def along_y(array):
        return [array] + [lax.ppermute(array, "head", y_shift(-dy)) for dy in range(1, n_y)]

    for group in (0, 1):
        hop(1, group, 1)
        hop(-1, group, 1)
    queries_other = to_other(queries)
    early = list(plan(n_seq, seq, block_list, block_count))
    tiles = list(tile(lax.div(head, 2), pair, out_weight, n_y))
    early[0], tiles[0] = lax.optimization_barrier((early[0], tiles[0]))
    hop(1, 0, 2, early)
    hop(-1, 0, 2)
    blocks, counts, near = early
    tiles[1:n_y] = [lax.ppermute(tiles[dy], "head", y_shift(dy)) for dy in range(1, n_y)][::-1]
    one_away = [(tiles[1], tiles[n_y - 1])]
    hop(1, 0, 3, one_away)
    tiles[1], tiles[n_y - 1] = one_away[0]
    hop(-1, 0, 3)
    hop(1, 0, 4)
    hop(-1, 1, 2)
    whole = [held[0][half]]
    hop(1, 1, 2, whole)
    held[0][half] = whole[0]
    hop(-1, 1, 3)
    hop(1, 1, 3)
    hop(-1, 1, 4)
    near, tiles[2] = lax.optimization_barrier((near, tiles[2]))
    weights = [tiles[0], tiles[n_y]]
    for mine in tiles[1:n_y]:
        weights += [mine, lax.ppermute(mine, "pair", [(0, 1), (1, 0)])]
    most = partial(0, 0, 3)
    before = project(GROUPS[0][0], along_y(join(most)), weights)
    one, two = partial(1, 0, 1), partial(1, 1, 2)
    two = join(two)
    before, two = lax.optimization_barrier((before, two))
    before = project(GROUPS[1][0], along_y(join(one)), weights, before)
    keep_block = (lax.rem(head, 2) != pair).astype(jnp.int32)
    keep, send = project(GROUPS[1][1], along_y(two), weights, before, keep_block)
    got = lax.ppermute(send, "head", [(g, g ^ 1) for g in range(n_head)])
    return (keep + got.astype(jnp.float32)).astype(jnp.bfloat16), cross_heads


def solution(mesh):
    rows = P(("pair", "seq"), "head")
    text = P("pair", "head")
    return jax.shard_map(
        functools.partial(body, mesh.shape["seq"], mesh.shape["head"]),
        mesh=mesh,
        in_specs=(rows, rows, rows, rows, text, text, P("head", None), P(), P()),
        out_specs=(rows, rows),
        check_vma=False,
    )
```

```python
import functools
import math

import jax
import jax.numpy as jnp
from jax import lax
from jax.experimental import pallas as pl
from jax.experimental.pallas import tpu as pltpu
from jax.sharding import PartitionSpec as P

DH = 128
BLK = 128
FB = 3
ROWS = FB * BLK
MAX_EXTRA = 12
MAX_NEAR = 3
GROUPS = ((0, 1, 2), (3, 4))
IN_FLIGHT = 2
NEG = -1e30
LOG2E = math.log2(math.e)
TO_EXP2 = DH ** (-0.5) * LOG2E
NT = (((1,), (1,)), ((), ()))
SMEM = pl.BlockSpec(memory_space=pltpu.SMEM)
VMEM = pl.BlockSpec(memory_space=pltpu.VMEM)


def plan_kernel(last, seq_ref, list_ref, count_ref, blocks_out, count_out, near_out):
    side = seq_ref[0] % 2
    for which in range(2):
        frame = seq_ref[0] + which * (1 - 2 * side)
        found = jnp.int32(0)
        for w in range(MAX_NEAR):
            near_out[which * (MAX_NEAR + 1) + w] = 0
        for key_frame in (frame - 1, frame, frame + 1, 0):
            here = (key_frame % 2 == side) & (key_frame >= 0) & (key_frame <= last)
            if isinstance(key_frame, int):
                here &= frame > 1
            near_out[which * (MAX_NEAR + 1) + found] = jnp.where(here, key_frame // 2, 0)
            found += here.astype(jnp.int32)
        near_out[which * (MAX_NEAR + 1) + MAX_NEAR] = found
        for r in range(FB):
            row, out = frame * FB + r, which * FB + r
            for e in range(MAX_EXTRA + 1):
                blocks_out[out, e] = 0

            def one(j, extras, row=row, out=out, frame=frame):
                block = list_ref[row, j]
                key_frame = lax.div(block, FB)
                far = (jnp.abs(key_frame - frame) > 1) & (key_frame > 0) & (key_frame % 2 == side)
                blocks_out[out, extras] = jnp.where(
                    far, lax.div(key_frame, 2) * FB + block - key_frame * FB, 0
                )
                return extras + far.astype(jnp.int32)

            extras = lax.fori_loop(0, count_ref[row], one, jnp.int32(0))
            count_out[out] = extras


def plan(frames, seq, block_list, block_count):
    return pl.pallas_call(
        functools.partial(plan_kernel, frames - 1),
        out_shape=[
            jax.ShapeDtypeStruct((2 * FB, MAX_EXTRA + 1), jnp.int32),
            jax.ShapeDtypeStruct((2 * FB,), jnp.int32),
            jax.ShapeDtypeStruct((2 * (MAX_NEAR + 1),), jnp.int32),
        ],
        in_specs=[SMEM] * 3,
        out_specs=[SMEM] * 3,
        compiler_params=pltpu.CompilerParams(vmem_limit_bytes=1 << 20),
        cost_estimate=pl.CostEstimate(flops=1000, bytes_accessed=8000, transcendentals=0),
        name="plan",
    )(seq, block_list, block_count)


def pack_kernel(k_ref, v_ref, *outs):
    for heads, out in zip(GROUPS, outs):
        for n, head in enumerate(heads):
            columns = slice(head * DH, (head + 1) * DH)
            out[2 * n * ROWS : (2 * n + 1) * ROWS, :] = k_ref[:, columns]
            out[(2 * n + 1) * ROWS : (2 * n + 2) * ROWS, :] = v_ref[:, columns]


def pack(keys, values):
    return pl.pallas_call(
        pack_kernel,
        out_shape=[jax.ShapeDtypeStruct((2 * ROWS * len(heads), DH), jnp.bfloat16) for heads in GROUPS],
        in_specs=[VMEM, VMEM],
        out_specs=[VMEM] * len(GROUPS),
        compiler_params=pltpu.CompilerParams(vmem_limit_bytes=6 << 20),
        cost_estimate=pl.CostEstimate(flops=0, bytes_accessed=4 * keys.size * 2, transcendentals=0),
        name="pack",
    )(keys, values)


def attend_lanes(lanes, near_ref, blocks_ref, count_ref, q_s, o_s, lse_s, k_s, v_s, near_s, far_s, top_s, sum_s):
    frames = sorted({which for _, which in lanes}, key=str) if all(isinstance(w, int) for _, w in lanes) else [lanes[0][1]]
    nears = near_ref[frames[0] * (MAX_NEAR + 1) + MAX_NEAR]
    most = count_ref[frames[0] * FB]
    for which in frames:
        nears = jnp.maximum(nears, near_ref[which * (MAX_NEAR + 1) + MAX_NEAR])
        for r in range(FB):
            most = jnp.maximum(most, count_ref[which * FB + r])
    pairs = lax.div(most + 1, 2)

    def near_rows(which, w):
        return pl.ds(pl.multiple_of(near_ref[which * (MAX_NEAR + 1) + w] * ROWS, ROWS), ROWS)

    def far_rows(which, r, e):
        return pl.ds(pl.multiple_of(blocks_ref[which * FB + r, e] * BLK, BLK), BLK)

    top_s[...] = jnp.full_like(top_s, NEG)

    def near_scores(w, carry):
        for lane, (n, which) in enumerate(lanes):
            score = lax.dot_general(
                q_s[2 * n + which], k_s[n, near_rows(which, w), :], NT, preferred_element_type=jnp.float32
            )
            if len(frames) > 1:
                score = jnp.where(w < near_ref[which * (MAX_NEAR + 1) + MAX_NEAR], score, NEG)
            near_s[lane, w] = score
            best = jnp.maximum(jnp.maximum(score[:, :BLK], score[:, BLK : 2 * BLK]), score[:, 2 * BLK :])
            top_s[lane] = jnp.maximum(top_s[lane], best)
        return carry

    lax.fori_loop(0, nears, near_scores, 0)

    def far_scores(i, carry):
        for lane, (n, which) in enumerate(lanes):
            for r in range(FB):
                rows = slice(r * BLK, (r + 1) * BLK)
                best = top_s[lane, rows, :]
                for j in range(2):
                    e = 2 * i + j
                    score = lax.dot_general(
                        q_s[2 * n + which, rows, :], k_s[n, far_rows(which, r, e), :], NT, preferred_element_type=jnp.float32
                    )
                    score = jnp.where(e < count_ref[which * FB + r], score, NEG)
                    far_s[lane, r, e] = score
                    best = jnp.maximum(best, score)
                top_s[lane, rows, :] = best
        return carry

    lax.fori_loop(0, pairs, far_scores, 0)
    for lane in range(len(lanes)):
        top_s[lane] = jnp.broadcast_to(jnp.max(top_s[lane], axis=1, keepdims=True) * TO_EXP2, (ROWS, BLK))
    sum_s[...] = jnp.zeros_like(sum_s)

    def near_weights(w, carry):
        for lane, (n, which) in enumerate(lanes):
            top = top_s[lane]
            weights = [jnp.exp2(near_s[lane, w, :, c * BLK : (c + 1) * BLK] * TO_EXP2 - top) for c in range(FB)]
            weight = jnp.concatenate([p.astype(jnp.bfloat16) for p in weights], axis=1)
            sum_s[lane] += jnp.dot(weight, v_s[n, near_rows(which, w), :], preferred_element_type=jnp.float32)
        return carry

    lax.fori_loop(0, nears, near_weights, 0)

    def far_weights(i, carry):
        for lane, (n, which) in enumerate(lanes):
            for r in range(FB):
                rows = slice(r * BLK, (r + 1) * BLK)
                top = top_s[lane, rows, :]
                part = None
                for j in range(2):
                    weight = jnp.exp2(far_s[lane, r, 2 * i + j] * TO_EXP2 - top).astype(jnp.bfloat16)
                    value = v_s[n, far_rows(which, r, 2 * i + j), :]
                    added = jnp.dot(weight, value, preferred_element_type=jnp.float32)
                    part = added if part is None else part + added
                sum_s[lane, rows, :] += part
        return carry

    lax.fori_loop(0, pairs, far_weights, 0)
    for lane, (n, which) in enumerate(lanes):
        total = sum_s[lane, :, DH:]
        o_s[2 * n + which] = sum_s[lane, :, :DH] / total
        lse_s[2 * n + which] = top_s[lane] + jnp.log(total) * LOG2E


def attend_kernel(heads, first, planes, seq_ref, near_ref, blocks_ref, count_ref, q_ref, q_other_ref, *refs):
    piece_refs = refs[:planes]
    keep_o, keep_lse, send = refs[planes : planes + 3]
    q_s, o_s, lse_s, k_s, v_s, near_s, far_s, top_s, sum_s = refs[planes + 3 :]
    z = lax.div(seq_ref[0], 2)
    v_s[:, :, DH:] = jnp.ones((len(heads), planes * ROWS, DH), jnp.bfloat16)
    for d, piece in enumerate(piece_refs):
        rows = pl.ds(pl.multiple_of(lax.rem(z + planes - d, planes) * ROWS, ROWS), ROWS)
        for n in range(len(heads)):
            at = 2 * (first + n) * ROWS
            k_s[n, rows, :] = piece[at : at + ROWS, :]
            v_s[n, rows, 0:DH] = piece[at + ROWS : at + 2 * ROWS, :]
    for n, head in enumerate(heads):
        columns = slice(head * DH, (head + 1) * DH)
        q_s[2 * n] = q_ref[:, columns]
        q_s[2 * n + 1] = q_other_ref[:, columns]
    tables = (near_ref, blocks_ref, count_ref, q_s, o_s, lse_s, k_s, v_s, near_s, far_s, top_s, sum_s)
    if len(heads) == 1:
        attend_lanes([(0, 0), (0, 1)], *tables)
    else:

        def one(which, carry):
            attend_lanes([(n, which) for n in range(len(heads))], *tables)
            return carry

        lax.fori_loop(0, 2, one, 0)
    lane = lax.broadcasted_iota(jnp.int32, (ROWS, DH), 1)
    for n in range(len(heads)):
        rows = slice(n * ROWS, (n + 1) * ROWS)
        keep_o[rows, :] = o_s[2 * n]
        keep_lse[rows, :] = lse_s[2 * n]
        send[2 * n * ROWS : (2 * n + 1) * ROWS, :] = o_s[2 * n + 1].astype(jnp.bfloat16)
        left = lse_s[2 * n + 1]
        packed = jnp.zeros((ROWS, DH), jnp.float32)
        for term in range(3):
            piece = left.astype(jnp.bfloat16).astype(jnp.float32)
            packed = jnp.where(lane == term, piece, packed)
            left = left - piece
        send[(2 * n + 1) * ROWS : (2 * n + 2) * ROWS, :] = packed.astype(jnp.bfloat16)


def attend(heads, first, queries, queries_other, pieces, seq, near, blocks, counts):
    planes, held = len(pieces), len(heads)
    lanes = max(held, 2)
    tokens = planes * ROWS
    each = pltpu.VMEM((2 * held, ROWS, DH), jnp.float32)
    elements = held * ROWS * 18 * BLK
    return pl.pallas_call(
        functools.partial(attend_kernel, heads, first, planes),
        out_shape=[
            jax.ShapeDtypeStruct((held * ROWS, DH), jnp.float32),
            jax.ShapeDtypeStruct((held * ROWS, DH), jnp.float32),
            jax.ShapeDtypeStruct((2 * held * ROWS, DH), jnp.bfloat16),
        ],
        in_specs=[SMEM] * 4 + [VMEM] * (2 + planes),
        out_specs=[VMEM] * 3,
        scratch_shapes=[
            pltpu.VMEM((2 * held, ROWS, DH), jnp.bfloat16),
            each,
            each,
            pltpu.VMEM((held, tokens, DH), jnp.bfloat16),
            pltpu.VMEM((held, tokens, 2 * DH), jnp.bfloat16),
            pltpu.VMEM((lanes, MAX_NEAR, ROWS, ROWS), jnp.float32),
            pltpu.VMEM((lanes, FB, MAX_EXTRA, BLK, BLK), jnp.float32),
            pltpu.VMEM((lanes, ROWS, BLK), jnp.float32),
            pltpu.VMEM((lanes, ROWS, 2 * DH), jnp.float32),
        ],
        compiler_params=pltpu.CompilerParams(vmem_limit_bytes=(36 if held > 2 else 24) << 20),
        cost_estimate=pl.CostEstimate(
            flops=40 * elements * DH, bytes_accessed=4 * held * tokens * DH, transcendentals=elements
        ),
        name="attend",
    )(seq, near, blocks, counts, queries, queries_other, *pieces)


def merge_kernel(*refs):
    out_ref, parts = refs[-1], refs[:-1]
    column = 0
    for o_ref, lse_ref, got_ref in zip(parts[0::3], parts[1::3], parts[2::3]):
        for n in range(o_ref.shape[0] // ROWS):
            rows = slice(n * ROWS, (n + 1) * ROWS)
            other_o = got_ref[2 * n * ROWS : (2 * n + 1) * ROWS, :].astype(jnp.float32)
            packed = got_ref[(2 * n + 1) * ROWS : (2 * n + 2) * ROWS, :].astype(jnp.float32)
            other_lse = jnp.sum(packed, axis=1, keepdims=True)
            lse = lse_ref[rows, :]
            top = jnp.maximum(lse, other_lse)
            mine, other = jnp.exp2(lse - top), jnp.exp2(other_lse - top)
            out = ((o_ref[rows, :] * mine + other_o * other) / (mine + other)).astype(out_ref.dtype)
            out_ref[:, column : column + DH] = out
            column += DH


def merge(*parts):
    size = sum(part.size for part in parts[0::3])
    return pl.pallas_call(
        merge_kernel,
        out_shape=jax.ShapeDtypeStruct((ROWS, size // ROWS), jnp.bfloat16),
        in_specs=[VMEM] * len(parts),
        out_specs=VMEM,
        compiler_params=pltpu.CompilerParams(vmem_limit_bytes=10 << 20),
        cost_estimate=pl.CostEstimate(flops=8 * size, bytes_accessed=30 * size, transcendentals=2 * size),
        name="merge",
    )(*parts)


def tile_kernel(count, y_ref, pair_ref, weight_ref, *refs):
    outs, sems = refs[:-1], refs[-1]
    width = outs[0].shape[1]
    copies = []
    for n, out in enumerate(outs):
        block = pair_ref[0] if n < count else 1 - pair_ref[0]
        start = pl.multiple_of((lax.rem(y_ref[0] + n, count) * 2 + block) * width, width)
        copies.append(pltpu.make_async_copy(weight_ref.at[:, pl.ds(start, width)], out, sems.at[n]))
    for copy in copies:
        copy.start()
    for copy in copies:
        copy.wait()


def tile(y, pair, weight, count):
    stay = pl.BlockSpec(memory_space=pl.ANY)
    shape = (weight.shape[0], weight.shape[1] // (2 * count))
    return pl.pallas_call(
        functools.partial(tile_kernel, count),
        out_shape=[jax.ShapeDtypeStruct(shape, weight.dtype)] * (count + 1),
        in_specs=[SMEM, SMEM, stay],
        out_specs=[stay] * (count + 1),
        scratch_shapes=[pltpu.SemaphoreType.DMA((count + 1,))],
        compiler_params=pltpu.CompilerParams(vmem_limit_bytes=1 << 20),
        cost_estimate=pl.CostEstimate(flops=0, bytes_accessed=4 * weight.size, transcendentals=0),
        name="tile",
    )(y, pair, weight)


def cross_kernel(q_ref, k_ref, v_ref, o_ref):
    def one(h, carry):
        columns = pl.ds(pl.multiple_of(h * DH, DH), DH)
        score = lax.dot_general(q_ref[:, columns], k_ref[:, columns], NT, preferred_element_type=jnp.float32)
        top = jnp.max(score, axis=1, keepdims=True) * TO_EXP2
        weight = jnp.exp2(score * TO_EXP2 - top)
        total = jnp.sum(weight, axis=1, keepdims=True)
        part = jnp.dot(weight.astype(jnp.bfloat16), v_ref[:, columns], preferred_element_type=jnp.float32)
        o_ref[:, columns] = (part / total).astype(o_ref.dtype)
        return carry

    lax.fori_loop(0, q_ref.shape[1] // DH, one, 0)


def cross(cross_query, text_keys, text_values):
    elements = cross_query.shape[0] * cross_query.shape[1] // DH * text_keys.shape[0]
    return pl.pallas_call(
        cross_kernel,
        out_shape=jax.ShapeDtypeStruct(cross_query.shape, jnp.bfloat16),
        in_specs=[VMEM] * 3,
        out_specs=VMEM,
        compiler_params=pltpu.CompilerParams(vmem_limit_bytes=8 << 20),
        cost_estimate=pl.CostEstimate(
            flops=40 * elements * DH, bytes_accessed=4 * cross_query.size, transcendentals=elements
        ),
        name="cross",
    )(cross_query, text_keys, text_values)


def project_kernel(first, sources, last, *refs):
    keep_ref = refs[0] if last else None
    refs = refs[1:] if last else refs
    heads, weights, refs = refs[:sources], refs[sources : 3 * sources], refs[3 * sources :]
    depth = heads[0].shape[1]
    rows = slice(first * DH, first * DH + depth)
    total_ref = refs[-1]
    for block in range(2):
        total = refs[0][block] if len(refs) > 1 + 2 * last else None
        for head_ref, weight_ref in zip(heads, weights[block::2]):
            part = jnp.dot(head_ref[...], weight_ref[rows, :], preferred_element_type=jnp.float32)
            total = part if total is None else total + part
        total_ref[block] = total
    if last:
        refs[-3][...] = total_ref[keep_ref[0]]
        refs[-2][...] = total_ref[1 - keep_ref[0]].astype(jnp.bfloat16)


def project(first, heads, weights, before=None, keep=None):
    rows, depth = heads[0].shape
    width = weights[0].shape[1]
    given = [*heads, *weights] + ([] if before is None else [before])
    both = jax.ShapeDtypeStruct((2, rows, width), jnp.float32)
    split = [jax.ShapeDtypeStruct((rows, width), dtype) for dtype in (jnp.float32, jnp.bfloat16)]
    last = keep is not None
    return pl.pallas_call(
        functools.partial(project_kernel, first, len(heads), last),
        out_shape=split if last else both,
        in_specs=[SMEM] * last + [VMEM] * len(given),
        out_specs=[VMEM] * 2 if last else VMEM,
        scratch_shapes=[pltpu.VMEM(both.shape, both.dtype)] if last else [],
        compiler_params=pltpu.CompilerParams(vmem_limit_bytes=22 << 20),
        cost_estimate=pl.CostEstimate(
            flops=4 * len(heads) * rows * depth * width,
            bytes_accessed=2 * len(heads) * depth * (rows + 2 * width),
            transcendentals=0,
        ),
        name="project",
    )(*([keep] if last else []), *given)


def body(n_seq, n_head, queries, keys, values, cross_query, text_keys, text_values, out_weight, block_list, block_count):
    n_z, n_y = n_seq // 2, n_head // 2
    seq = lax.axis_index("seq").reshape(1)
    head = lax.axis_index("head").reshape(1)
    pair = lax.axis_index("pair").reshape(1)
    cross_heads = cross(cross_query, text_keys, text_values)
    swap = [(s, s ^ 1) for s in range(n_seq)]

    def to_other(array):
        return lax.ppermute(array, "seq", swap)

    def z_shift(step):
        return [(s, (s // 2 + step) % n_z * 2 + s % 2) for s in range(n_seq)]

    def y_shift(step):
        return [(g, (g // 2 + step) % n_y * 2 + g % 2) for g in range(n_head)]

    held = [{0: array} for array in pack(keys, values)]
    sent = {1: [], -1: []}

    def hop(way, group, step, after=None):
        done = sent[way]
        array = held[group][way * (step - 1) % n_z]
        if len(done) >= IN_FLIGHT:
            at, where = done[-IN_FLIGHT]
            array, held[at][where] = lax.optimization_barrier((array, held[at][where]))
        if after is not None:
            array, after[0] = lax.optimization_barrier((array, after[0]))
        place = way * step % n_z
        held[group][place] = lax.ppermute(array, "seq", z_shift(way))
        done.append((group, place))

    def partial(group, start, stop):
        pieces = [held[group][d] for d in range(n_z)]
        return list(attend(GROUPS[group][start:stop], start, queries, queries_other, pieces, seq, near, blocks, counts))

    def join(*parts):
        return merge(*(array for part in parts for array in (*part[:2], to_other(part[2]))))

    def along_y(array):
        return [array] + [lax.ppermute(array, "head", y_shift(-dy)) for dy in range(1, n_y)]

    for group in (0, 1):
        hop(1, group, 1)
        hop(-1, group, 1)
    queries_other = to_other(queries)
    early = list(plan(n_seq, seq, block_list, block_count))
    tiles = list(tile(lax.div(head, 2), pair, out_weight, n_y))
    early[0], tiles[0], queries_other = lax.optimization_barrier((early[0], tiles[0], queries_other))
    hop(1, 0, 2, early)
    hop(-1, 0, 2)
    blocks, counts, near = early
    tiles[1:n_y] = [lax.ppermute(tiles[dy], "head", y_shift(dy)) for dy in range(1, n_y)][::-1]
    one_away = [(tiles[1], tiles[n_y - 1])]
    hop(1, 0, 3, one_away)
    tiles[1], tiles[n_y - 1] = one_away[0]
    hop(-1, 0, 3)
    hop(1, 0, 4)
    hop(-1, 1, 2)
    hop(1, 1, 2)
    hop(-1, 1, 3)
    hop(1, 1, 3)
    hop(-1, 1, 4)
    near, tiles[2] = lax.optimization_barrier((near, tiles[2]))
    weights = [tiles[0], tiles[n_y]]
    for mine in tiles[1:n_y]:
        weights += [mine, lax.ppermute(mine, "pair", [(0, 1), (1, 0)])]
    most = partial(0, 0, 3)
    near, *weights = lax.optimization_barrier((near, *weights))
    one, two = partial(1, 0, 1), partial(1, 1, 2)
    most[0], two[2] = lax.optimization_barrier((most[0], two[2]))
    before = project(GROUPS[0][0], along_y(join(most)), weights)
    rest = join(one, two)
    keep_block = (lax.rem(head, 2) != pair).astype(jnp.int32)
    keep, send = project(GROUPS[1][0], along_y(rest), weights, before, keep_block)
    got = lax.ppermute(send, "head", [(g, g ^ 1) for g in range(n_head)])
    return (keep + got.astype(jnp.float32)).astype(jnp.bfloat16), cross_heads


def solution(mesh):
    rows = P(("pair", "seq"), "head")
    text = P("pair", "head")
    return jax.shard_map(
        functools.partial(body, mesh.shape["seq"], mesh.shape["head"]),
        mesh=mesh,
        in_specs=(rows, rows, rows, rows, text, text, P("head", None), P(), P()),
        out_specs=(rows, rows),
        check_vma=False,
    )
```

```python
import functools
import math

import jax
import jax.numpy as jnp
from jax import lax
from jax.experimental import pallas as pl
from jax.experimental.pallas import tpu as pltpu
from jax.sharding import PartitionSpec as P

DH = 128
BLK = 128
FB = 3
ROWS = FB * BLK
MAX_EXTRA = 12
MAX_NEAR = 3
GROUPS = ((0, 1, 2), (3, 4))
IN_FLIGHT = 2
NEG = -1e30
LOG2E = math.log2(math.e)
TO_EXP2 = DH ** (-0.5) * LOG2E
NT = (((1,), (1,)), ((), ()))
SMEM = pl.BlockSpec(memory_space=pltpu.SMEM)
VMEM = pl.BlockSpec(memory_space=pltpu.VMEM)


def plan_kernel(last, seq_ref, list_ref, count_ref, blocks_out, count_out, near_out):
    side = seq_ref[0] % 2
    for which in range(2):
        frame = seq_ref[0] + which * (1 - 2 * side)
        found = jnp.int32(0)
        for w in range(MAX_NEAR):
            near_out[which * (MAX_NEAR + 1) + w] = 0
        for key_frame in (frame - 1, frame, frame + 1, 0):
            here = (key_frame % 2 == side) & (key_frame >= 0) & (key_frame <= last)
            if isinstance(key_frame, int):
                here &= frame > 1
            near_out[which * (MAX_NEAR + 1) + found] = jnp.where(here, key_frame // 2, 0)
            found += here.astype(jnp.int32)
        near_out[which * (MAX_NEAR + 1) + MAX_NEAR] = found
        for r in range(FB):
            row, out = frame * FB + r, which * FB + r
            for e in range(MAX_EXTRA + 1):
                blocks_out[out, e] = 0

            def one(j, extras, row=row, out=out, frame=frame):
                block = list_ref[row, j]
                key_frame = lax.div(block, FB)
                far = (jnp.abs(key_frame - frame) > 1) & (key_frame > 0) & (key_frame % 2 == side)
                blocks_out[out, extras] = jnp.where(
                    far, lax.div(key_frame, 2) * FB + block - key_frame * FB, 0
                )
                return extras + far.astype(jnp.int32)

            extras = lax.fori_loop(0, count_ref[row], one, jnp.int32(0))
            count_out[out] = extras


def plan(frames, seq, block_list, block_count):
    return pl.pallas_call(
        functools.partial(plan_kernel, frames - 1),
        out_shape=[
            jax.ShapeDtypeStruct((2 * FB, MAX_EXTRA + 1), jnp.int32),
            jax.ShapeDtypeStruct((2 * FB,), jnp.int32),
            jax.ShapeDtypeStruct((2 * (MAX_NEAR + 1),), jnp.int32),
        ],
        in_specs=[SMEM] * 3,
        out_specs=[SMEM] * 3,
        compiler_params=pltpu.CompilerParams(vmem_limit_bytes=1 << 20),
        cost_estimate=pl.CostEstimate(flops=1000, bytes_accessed=8000, transcendentals=0),
        name="plan",
    )(seq, block_list, block_count)


def pack_kernel(k_ref, v_ref, *refs):
    outs, sems = refs[:-1], refs[-1]
    copies = []
    for heads, out in zip(GROUPS, outs):
        for n, head in enumerate(heads):
            for m, ref in enumerate((k_ref, v_ref)):
                source = ref.at[:, head * DH : (head + 1) * DH]
                target = out.at[(2 * n + m) * ROWS : (2 * n + m + 1) * ROWS, :]
                copies.append(pltpu.make_async_copy(source, target, sems.at[len(copies)]))
    for copy in copies:
        copy.start()
    for copy in copies:
        copy.wait()


def pack(keys, values):
    stay = pl.BlockSpec(memory_space=pltpu.HBM)
    return pl.pallas_call(
        pack_kernel,
        out_shape=[jax.ShapeDtypeStruct((2 * ROWS * len(heads), DH), jnp.bfloat16) for heads in GROUPS],
        in_specs=[stay] * 2,
        out_specs=[stay] * len(GROUPS),
        scratch_shapes=[pltpu.SemaphoreType.DMA((2 * sum(len(heads) for heads in GROUPS),))],
        compiler_params=pltpu.CompilerParams(vmem_limit_bytes=1 << 20),
        cost_estimate=pl.CostEstimate(flops=0, bytes_accessed=4 * keys.size * 2, transcendentals=0),
        name="pack",
    )(keys, values)


def attend_lanes(lanes, near_ref, blocks_ref, count_ref, q_s, o_s, lse_s, k_s, v_s, near_s, far_s, top_s, sum_s):
    frames = sorted({which for _, which in lanes}, key=str) if all(isinstance(w, int) for _, w in lanes) else [lanes[0][1]]
    nears = near_ref[frames[0] * (MAX_NEAR + 1) + MAX_NEAR]
    most = count_ref[frames[0] * FB]
    for which in frames:
        nears = jnp.maximum(nears, near_ref[which * (MAX_NEAR + 1) + MAX_NEAR])
        for r in range(FB):
            most = jnp.maximum(most, count_ref[which * FB + r])
    pairs = lax.div(most + 1, 2)

    def near_rows(which, w):
        return pl.ds(pl.multiple_of(near_ref[which * (MAX_NEAR + 1) + w] * ROWS, ROWS), ROWS)

    def far_rows(which, r, e):
        return pl.ds(pl.multiple_of(blocks_ref[which * FB + r, e] * BLK, BLK), BLK)

    top_s[...] = jnp.full_like(top_s, NEG)

    def near_scores(w, carry):
        for lane, (n, which) in enumerate(lanes):
            score = lax.dot_general(
                q_s[2 * n + which], k_s[n, near_rows(which, w), :], NT, preferred_element_type=jnp.float32
            )
            if len(frames) > 1:
                score = jnp.where(w < near_ref[which * (MAX_NEAR + 1) + MAX_NEAR], score, NEG)
            near_s[lane, w] = score
            best = jnp.maximum(jnp.maximum(score[:, :BLK], score[:, BLK : 2 * BLK]), score[:, 2 * BLK :])
            top_s[lane] = jnp.maximum(top_s[lane], best)
        return carry

    lax.fori_loop(0, nears, near_scores, 0)

    def far_scores(i, carry):
        for lane, (n, which) in enumerate(lanes):
            for r in range(FB):
                rows = slice(r * BLK, (r + 1) * BLK)
                best = top_s[lane, rows, :]
                for j in range(2):
                    e = 2 * i + j
                    score = lax.dot_general(
                        q_s[2 * n + which, rows, :], k_s[n, far_rows(which, r, e), :], NT, preferred_element_type=jnp.float32
                    )
                    score = jnp.where(e < count_ref[which * FB + r], score, NEG)
                    far_s[lane, r, e] = score
                    best = jnp.maximum(best, score)
                top_s[lane, rows, :] = best
        return carry

    lax.fori_loop(0, pairs, far_scores, 0)
    for lane in range(len(lanes)):
        top_s[lane] = jnp.broadcast_to(jnp.max(top_s[lane], axis=1, keepdims=True) * TO_EXP2, (ROWS, BLK))
    sum_s[...] = jnp.zeros_like(sum_s)

    def near_weights(w, carry):
        for lane, (n, which) in enumerate(lanes):
            top = top_s[lane]
            weights = [jnp.exp2(near_s[lane, w, :, c * BLK : (c + 1) * BLK] * TO_EXP2 - top) for c in range(FB)]
            weight = jnp.concatenate([p.astype(jnp.bfloat16) for p in weights], axis=1)
            sum_s[lane] += jnp.dot(weight, v_s[n, near_rows(which, w), :], preferred_element_type=jnp.float32)
        return carry

    lax.fori_loop(0, nears, near_weights, 0)

    def far_weights(i, carry):
        for lane, (n, which) in enumerate(lanes):
            for r in range(FB):
                rows = slice(r * BLK, (r + 1) * BLK)
                top = top_s[lane, rows, :]
                part = None
                for j in range(2):
                    weight = jnp.exp2(far_s[lane, r, 2 * i + j] * TO_EXP2 - top).astype(jnp.bfloat16)
                    value = v_s[n, far_rows(which, r, 2 * i + j), :]
                    added = jnp.dot(weight, value, preferred_element_type=jnp.float32)
                    part = added if part is None else part + added
                sum_s[lane, rows, :] += part
        return carry

    lax.fori_loop(0, pairs, far_weights, 0)
    for lane, (n, which) in enumerate(lanes):
        total = sum_s[lane, :, DH:]
        o_s[2 * n + which] = sum_s[lane, :, :DH] / total
        lse_s[2 * n + which] = top_s[lane] + jnp.log(total) * LOG2E


def attend_kernel(heads, first, planes, seq_ref, near_ref, blocks_ref, count_ref, q_ref, q_other_ref, *refs):
    piece_refs = refs[:planes]
    keep_o, keep_lse, send = refs[planes : planes + 3]
    q_s, o_s, lse_s, k_s, v_s, near_s, far_s, top_s, sum_s = refs[planes + 3 :]
    z = lax.div(seq_ref[0], 2)
    v_s[:, :, DH:] = jnp.ones((len(heads), planes * ROWS, DH), jnp.bfloat16)
    for d, piece in enumerate(piece_refs):
        rows = pl.ds(pl.multiple_of(lax.rem(z + planes - d, planes) * ROWS, ROWS), ROWS)
        for n in range(len(heads)):
            at = 2 * (first + n) * ROWS
            k_s[n, rows, :] = piece[at : at + ROWS, :]
            v_s[n, rows, 0:DH] = piece[at + ROWS : at + 2 * ROWS, :]
    for n, head in enumerate(heads):
        columns = slice(head * DH, (head + 1) * DH)
        q_s[2 * n] = q_ref[:, columns]
        q_s[2 * n + 1] = q_other_ref[:, columns]
    tables = (near_ref, blocks_ref, count_ref, q_s, o_s, lse_s, k_s, v_s, near_s, far_s, top_s, sum_s)
    if len(heads) == 1:
        attend_lanes([(0, 0), (0, 1)], *tables)
    else:

        def one(which, carry):
            attend_lanes([(n, which) for n in range(len(heads))], *tables)
            return carry

        lax.fori_loop(0, 2, one, 0)
    lane = lax.broadcasted_iota(jnp.int32, (ROWS, DH), 1)
    for n in range(len(heads)):
        rows = slice(n * ROWS, (n + 1) * ROWS)
        keep_o[rows, :] = o_s[2 * n]
        keep_lse[rows, :] = lse_s[2 * n]
        send[2 * n * ROWS : (2 * n + 1) * ROWS, :] = o_s[2 * n + 1].astype(jnp.bfloat16)
        left = lse_s[2 * n + 1]
        packed = jnp.zeros((ROWS, DH), jnp.float32)
        for term in range(3):
            piece = left.astype(jnp.bfloat16).astype(jnp.float32)
            packed = jnp.where(lane == term, piece, packed)
            left = left - piece
        send[(2 * n + 1) * ROWS : (2 * n + 2) * ROWS, :] = packed.astype(jnp.bfloat16)


def attend(heads, first, queries, queries_other, pieces, seq, near, blocks, counts):
    planes, held = len(pieces), len(heads)
    lanes = max(held, 2)
    tokens = planes * ROWS
    each = pltpu.VMEM((2 * held, ROWS, DH), jnp.float32)
    elements = held * ROWS * 18 * BLK
    return pl.pallas_call(
        functools.partial(attend_kernel, heads, first, planes),
        out_shape=[
            jax.ShapeDtypeStruct((held * ROWS, DH), jnp.float32),
            jax.ShapeDtypeStruct((held * ROWS, DH), jnp.float32),
            jax.ShapeDtypeStruct((2 * held * ROWS, DH), jnp.bfloat16),
        ],
        in_specs=[SMEM] * 4 + [VMEM] * (2 + planes),
        out_specs=[VMEM] * 3,
        scratch_shapes=[
            pltpu.VMEM((2 * held, ROWS, DH), jnp.bfloat16),
            each,
            each,
            pltpu.VMEM((held, tokens, DH), jnp.bfloat16),
            pltpu.VMEM((held, tokens, 2 * DH), jnp.bfloat16),
            pltpu.VMEM((lanes, MAX_NEAR, ROWS, ROWS), jnp.float32),
            pltpu.VMEM((lanes, FB, MAX_EXTRA, BLK, BLK), jnp.float32),
            pltpu.VMEM((lanes, ROWS, BLK), jnp.float32),
            pltpu.VMEM((lanes, ROWS, 2 * DH), jnp.float32),
        ],
        compiler_params=pltpu.CompilerParams(vmem_limit_bytes=(36 if held > 2 else 24) << 20),
        cost_estimate=pl.CostEstimate(
            flops=40 * elements * DH, bytes_accessed=4 * held * tokens * DH, transcendentals=elements
        ),
        name="attend",
    )(seq, near, blocks, counts, queries, queries_other, *pieces)


def merge_kernel(*refs):
    out_ref, parts = refs[-1], refs[:-1]
    column = 0
    for o_ref, lse_ref, got_ref in zip(parts[0::3], parts[1::3], parts[2::3]):
        for n in range(o_ref.shape[0] // ROWS):
            rows = slice(n * ROWS, (n + 1) * ROWS)
            other_o = got_ref[2 * n * ROWS : (2 * n + 1) * ROWS, :].astype(jnp.float32)
            packed = got_ref[(2 * n + 1) * ROWS : (2 * n + 2) * ROWS, :].astype(jnp.float32)
            other_lse = jnp.sum(packed, axis=1, keepdims=True)
            lse = lse_ref[rows, :]
            top = jnp.maximum(lse, other_lse)
            mine, other = jnp.exp2(lse - top), jnp.exp2(other_lse - top)
            out = ((o_ref[rows, :] * mine + other_o * other) / (mine + other)).astype(out_ref.dtype)
            out_ref[:, column : column + DH] = out
            column += DH


def merge(*parts):
    size = sum(part.size for part in parts[0::3])
    return pl.pallas_call(
        merge_kernel,
        out_shape=jax.ShapeDtypeStruct((ROWS, size // ROWS), jnp.bfloat16),
        in_specs=[VMEM] * len(parts),
        out_specs=VMEM,
        compiler_params=pltpu.CompilerParams(vmem_limit_bytes=10 << 20),
        cost_estimate=pl.CostEstimate(flops=8 * size, bytes_accessed=30 * size, transcendentals=2 * size),
        name="merge",
    )(*parts)


def tile_kernel(count, y_ref, pair_ref, weight_ref, *refs):
    outs, sems = refs[:-1], refs[-1]
    width = outs[0].shape[1]
    copies = []
    for n, out in enumerate(outs):
        block = pair_ref[0] if n < count else 1 - pair_ref[0]
        start = pl.multiple_of((lax.rem(y_ref[0] + n, count) * 2 + block) * width, width)
        copies.append(pltpu.make_async_copy(weight_ref.at[:, pl.ds(start, width)], out, sems.at[n]))
    for copy in copies:
        copy.start()
    for copy in copies:
        copy.wait()


def tile(y, pair, weight, count):
    stay = pl.BlockSpec(memory_space=pl.ANY)
    shape = (weight.shape[0], weight.shape[1] // (2 * count))
    return pl.pallas_call(
        functools.partial(tile_kernel, count),
        out_shape=[jax.ShapeDtypeStruct(shape, weight.dtype)] * (count + 1),
        in_specs=[SMEM, SMEM, stay],
        out_specs=[stay] * (count + 1),
        scratch_shapes=[pltpu.SemaphoreType.DMA((count + 1,))],
        compiler_params=pltpu.CompilerParams(vmem_limit_bytes=1 << 20),
        cost_estimate=pl.CostEstimate(flops=0, bytes_accessed=4 * weight.size, transcendentals=0),
        name="tile",
    )(y, pair, weight)


def cross_kernel(q_ref, k_ref, v_ref, o_ref):
    def one(h, carry):
        columns = pl.ds(pl.multiple_of(h * DH, DH), DH)
        score = lax.dot_general(q_ref[:, columns], k_ref[:, columns], NT, preferred_element_type=jnp.float32)
        top = jnp.max(score, axis=1, keepdims=True) * TO_EXP2
        weight = jnp.exp2(score * TO_EXP2 - top)
        total = jnp.sum(weight, axis=1, keepdims=True)
        part = jnp.dot(weight.astype(jnp.bfloat16), v_ref[:, columns], preferred_element_type=jnp.float32)
        o_ref[:, columns] = (part / total).astype(o_ref.dtype)
        return carry

    lax.fori_loop(0, q_ref.shape[1] // DH, one, 0)


def cross(cross_query, text_keys, text_values):
    elements = cross_query.shape[0] * cross_query.shape[1] // DH * text_keys.shape[0]
    return pl.pallas_call(
        cross_kernel,
        out_shape=jax.ShapeDtypeStruct(cross_query.shape, jnp.bfloat16),
        in_specs=[VMEM] * 3,
        out_specs=VMEM,
        compiler_params=pltpu.CompilerParams(vmem_limit_bytes=8 << 20),
        cost_estimate=pl.CostEstimate(
            flops=40 * elements * DH, bytes_accessed=4 * cross_query.size, transcendentals=elements
        ),
        name="cross",
    )(cross_query, text_keys, text_values)


def project_kernel(first, sources, last, *refs):
    keep_ref = refs[0] if last else None
    refs = refs[1:] if last else refs
    heads, weights, refs = refs[:sources], refs[sources : 3 * sources], refs[3 * sources :]
    depth = heads[0].shape[1]
    rows = slice(first * DH, first * DH + depth)
    total_ref = refs[-1]
    for block in range(2):
        total = refs[0][block] if len(refs) > 1 + 2 * last else None
        for head_ref, weight_ref in zip(heads, weights[block::2]):
            part = jnp.dot(head_ref[...], weight_ref[rows, :], preferred_element_type=jnp.float32)
            total = part if total is None else total + part
        total_ref[block] = total
    if last:
        refs[-3][...] = total_ref[keep_ref[0]]
        refs[-2][...] = total_ref[1 - keep_ref[0]].astype(jnp.bfloat16)


def project(first, heads, weights, before=None, keep=None):
    rows, depth = heads[0].shape
    width = weights[0].shape[1]
    given = [*heads, *weights] + ([] if before is None else [before])
    both = jax.ShapeDtypeStruct((2, rows, width), jnp.float32)
    split = [jax.ShapeDtypeStruct((rows, width), dtype) for dtype in (jnp.float32, jnp.bfloat16)]
    last = keep is not None
    return pl.pallas_call(
        functools.partial(project_kernel, first, len(heads), last),
        out_shape=split if last else both,
        in_specs=[SMEM] * last + [VMEM] * len(given),
        out_specs=[VMEM] * 2 if last else VMEM,
        scratch_shapes=[pltpu.VMEM(both.shape, both.dtype)] if last else [],
        compiler_params=pltpu.CompilerParams(vmem_limit_bytes=22 << 20),
        cost_estimate=pl.CostEstimate(
            flops=4 * len(heads) * rows * depth * width,
            bytes_accessed=2 * len(heads) * depth * (rows + 2 * width),
            transcendentals=0,
        ),
        name="project",
    )(*([keep] if last else []), *given)


def body(n_seq, n_head, queries, keys, values, cross_query, text_keys, text_values, out_weight, block_list, block_count):
    n_z, n_y = n_seq // 2, n_head // 2
    seq = lax.axis_index("seq").reshape(1)
    head = lax.axis_index("head").reshape(1)
    pair = lax.axis_index("pair").reshape(1)
    cross_heads = cross(cross_query, text_keys, text_values)
    swap = [(s, s ^ 1) for s in range(n_seq)]

    def to_other(array):
        return lax.ppermute(array, "seq", swap)

    def z_shift(step):
        return [(s, (s // 2 + step) % n_z * 2 + s % 2) for s in range(n_seq)]

    def y_shift(step):
        return [(g, (g // 2 + step) % n_y * 2 + g % 2) for g in range(n_head)]

    held = [{0: array} for array in pack(keys, values)]
    sent = {1: [], -1: []}

    def hop(way, group, step, after=None):
        done = sent[way]
        array = held[group][way * (step - 1) % n_z]
        if len(done) >= IN_FLIGHT:
            at, where = done[-IN_FLIGHT]
            array, held[at][where] = lax.optimization_barrier((array, held[at][where]))
        if after is not None:
            array, after[0] = lax.optimization_barrier((array, after[0]))
        place = way * step % n_z
        held[group][place] = lax.ppermute(array, "seq", z_shift(way))
        done.append((group, place))

    def partial(group, start, stop):
        pieces = [held[group][d] for d in range(n_z)]
        return list(attend(GROUPS[group][start:stop], start, queries, queries_other, pieces, seq, near, blocks, counts))

    def join(*parts):
        return merge(*(array for part in parts for array in (*part[:2], to_other(part[2]))))

    def along_y(array):
        return [array] + [lax.ppermute(array, "head", y_shift(-dy)) for dy in range(1, n_y)]

    for group in (0, 1):
        hop(1, group, 1)
        hop(-1, group, 1)
    queries_other = to_other(queries)
    early = list(plan(n_seq, seq, block_list, block_count))
    early[0], queries_other = lax.optimization_barrier((early[0], queries_other))
    hop(1, 0, 2, early)
    out_weight, held[0][1] = lax.optimization_barrier((out_weight, held[0][1]))
    tiles = list(tile(lax.div(head, 2), pair, out_weight, n_y))
    hop(-1, 0, 2)
    blocks, counts, near = early
    tiles[1:n_y] = [lax.ppermute(tiles[dy], "head", y_shift(dy)) for dy in range(1, n_y)][::-1]
    hop(1, 0, 3)
    hop(-1, 0, 3)
    one_away = [(tiles[1], tiles[n_y - 1])]
    hop(1, 0, 4, one_away)
    tiles[1], tiles[n_y - 1] = one_away[0]
    hop(-1, 1, 2)
    hop(1, 1, 2)
    hop(-1, 1, 3)
    hop(1, 1, 3)
    hop(-1, 1, 4)
    near, tiles[2] = lax.optimization_barrier((near, tiles[2]))
    most = partial(0, 0, 3)
    most[1], *tiles[1:n_y] = lax.optimization_barrier((most[1], *tiles[1:n_y]))
    weights = [tiles[0], tiles[n_y]]
    for mine in tiles[1:n_y]:
        weights += [mine, lax.ppermute(mine, "pair", [(0, 1), (1, 0)])]
    one, two = partial(1, 0, 1), partial(1, 1, 2)
    most[0], one[2], two[2] = lax.optimization_barrier((most[0], one[2], two[2]))
    before = project(GROUPS[0][0], along_y(join(most)), weights)
    rest = join(one, two)
    keep_block = (lax.rem(head, 2) != pair).astype(jnp.int32)
    keep, send = project(GROUPS[1][0], along_y(rest), weights, before, keep_block)
    got = lax.ppermute(send, "head", [(g, g ^ 1) for g in range(n_head)])
    return (keep + got.astype(jnp.float32)).astype(jnp.bfloat16), cross_heads


def solution(mesh):
    rows = P(("pair", "seq"), "head")
    text = P("pair", "head")
    return jax.shard_map(
        functools.partial(body, mesh.shape["seq"], mesh.shape["head"]),
        mesh=mesh,
        in_specs=(rows, rows, rows, rows, text, text, P("head", None), P(), P()),
        out_specs=(rows, rows),
        check_vma=False,
    )
```

```python
import functools
import math

import jax
import jax.numpy as jnp
from jax import lax
from jax.experimental import pallas as pl
from jax.experimental.pallas import tpu as pltpu
from jax.sharding import PartitionSpec as P

DH = 128
BLK = 128
FB = 3
ROWS = FB * BLK
MAX_EXTRA = 12
MAX_NEAR = 3
TERMS = 3
GROUPS = ((0, 1, 2), (3, 4))
IN_FLIGHT = 2
NEG = -1e30
LOG2E = math.log2(math.e)
TO_EXP2 = DH ** (-0.5) * LOG2E
NT = (((1,), (1,)), ((), ()))
SMEM = pl.BlockSpec(memory_space=pltpu.SMEM)
VMEM = pl.BlockSpec(memory_space=pltpu.VMEM)


def plan_kernel(last, seq_ref, list_ref, count_ref, blocks_out, count_out, near_out):
    side = seq_ref[0] % 2
    for which in range(2):
        frame = seq_ref[0] + which * (1 - 2 * side)
        found = jnp.int32(0)
        for w in range(MAX_NEAR):
            near_out[which * (MAX_NEAR + 1) + w] = 0
        for key_frame in (frame - 1, frame, frame + 1, 0):
            here = (key_frame % 2 == side) & (key_frame >= 0) & (key_frame <= last)
            if isinstance(key_frame, int):
                here &= frame > 1
            near_out[which * (MAX_NEAR + 1) + found] = jnp.where(here, key_frame // 2, 0)
            found += here.astype(jnp.int32)
        near_out[which * (MAX_NEAR + 1) + MAX_NEAR] = found
        for r in range(FB):
            row, out = frame * FB + r, which * FB + r
            for e in range(MAX_EXTRA + 1):
                blocks_out[out, e] = 0

            def one(j, extras, row=row, out=out, frame=frame):
                block = list_ref[row, j]
                key_frame = lax.div(block, FB)
                far = (jnp.abs(key_frame - frame) > 1) & (key_frame > 0) & (key_frame % 2 == side)
                blocks_out[out, extras] = jnp.where(
                    far, lax.div(key_frame, 2) * FB + block - key_frame * FB, 0
                )
                return extras + far.astype(jnp.int32)

            extras = lax.fori_loop(0, count_ref[row], one, jnp.int32(0))
            count_out[out] = extras


def plan(frames, seq, block_list, block_count):
    return pl.pallas_call(
        functools.partial(plan_kernel, frames - 1),
        out_shape=[
            jax.ShapeDtypeStruct((2 * FB, MAX_EXTRA + 1), jnp.int32),
            jax.ShapeDtypeStruct((2 * FB,), jnp.int32),
            jax.ShapeDtypeStruct((2 * (MAX_NEAR + 1),), jnp.int32),
        ],
        in_specs=[SMEM] * 3,
        out_specs=[SMEM] * 3,
        compiler_params=pltpu.CompilerParams(vmem_limit_bytes=1 << 20),
        cost_estimate=pl.CostEstimate(flops=1000, bytes_accessed=8000, transcendentals=0),
        name="plan",
    )(seq, block_list, block_count)


def pack_kernel(k_ref, v_ref, *outs):
    for heads, out in zip(GROUPS, outs):
        for n, head in enumerate(heads):
            columns = slice(head * DH, (head + 1) * DH)
            out[2 * n * ROWS : (2 * n + 1) * ROWS, :] = k_ref[:, columns]
            out[(2 * n + 1) * ROWS : (2 * n + 2) * ROWS, :] = v_ref[:, columns]


def pack(keys, values):
    return pl.pallas_call(
        pack_kernel,
        out_shape=[jax.ShapeDtypeStruct((2 * ROWS * len(heads), DH), jnp.bfloat16) for heads in GROUPS],
        in_specs=[VMEM, VMEM],
        out_specs=[VMEM] * len(GROUPS),
        compiler_params=pltpu.CompilerParams(vmem_limit_bytes=6 << 20),
        cost_estimate=pl.CostEstimate(flops=0, bytes_accessed=4 * keys.size * 2, transcendentals=0),
        name="pack",
    )(keys, values)


def attend_lanes(lanes, near_ref, blocks_ref, count_ref, q_s, o_s, lse_s, k_s, v_s, near_s, far_s, top_s, sum_s):
    frames = sorted({which for _, which in lanes}, key=str) if all(isinstance(w, int) for _, w in lanes) else [lanes[0][1]]
    nears = near_ref[frames[0] * (MAX_NEAR + 1) + MAX_NEAR]
    most = count_ref[frames[0] * FB]
    for which in frames:
        nears = jnp.maximum(nears, near_ref[which * (MAX_NEAR + 1) + MAX_NEAR])
        for r in range(FB):
            most = jnp.maximum(most, count_ref[which * FB + r])
    pairs = lax.div(most + 1, 2)

    def near_rows(which, w):
        return pl.ds(pl.multiple_of(near_ref[which * (MAX_NEAR + 1) + w] * ROWS, ROWS), ROWS)

    def far_rows(which, r, e):
        return pl.ds(pl.multiple_of(blocks_ref[which * FB + r, e] * BLK, BLK), BLK)

    top_s[...] = jnp.full_like(top_s, NEG)

    def near_scores(w, carry):
        for lane, (n, which) in enumerate(lanes):
            score = lax.dot_general(
                q_s[2 * n + which], k_s[n, near_rows(which, w), :], NT, preferred_element_type=jnp.float32
            )
            if len(frames) > 1:
                score = jnp.where(w < near_ref[which * (MAX_NEAR + 1) + MAX_NEAR], score, NEG)
            near_s[lane, w] = score
            best = jnp.maximum(jnp.maximum(score[:, :BLK], score[:, BLK : 2 * BLK]), score[:, 2 * BLK :])
            top_s[lane] = jnp.maximum(top_s[lane], best)
        return carry

    lax.fori_loop(0, nears, near_scores, 0)

    def far_scores(i, carry):
        for lane, (n, which) in enumerate(lanes):
            for r in range(FB):
                rows = slice(r * BLK, (r + 1) * BLK)
                best = top_s[lane, rows, :]
                for j in range(2):
                    e = 2 * i + j
                    score = lax.dot_general(
                        q_s[2 * n + which, rows, :], k_s[n, far_rows(which, r, e), :], NT, preferred_element_type=jnp.float32
                    )
                    score = jnp.where(e < count_ref[which * FB + r], score, NEG)
                    far_s[lane, r, e] = score
                    best = jnp.maximum(best, score)
                top_s[lane, rows, :] = best
        return carry

    lax.fori_loop(0, pairs, far_scores, 0)
    for lane in range(len(lanes)):
        top_s[lane] = jnp.broadcast_to(jnp.max(top_s[lane], axis=1, keepdims=True) * TO_EXP2, (ROWS, BLK))
    sum_s[...] = jnp.zeros_like(sum_s)

    def near_weights(w, carry):
        for lane, (n, which) in enumerate(lanes):
            top = top_s[lane]
            weights = [jnp.exp2(near_s[lane, w, :, c * BLK : (c + 1) * BLK] * TO_EXP2 - top) for c in range(FB)]
            weight = jnp.concatenate([p.astype(jnp.bfloat16) for p in weights], axis=1)
            sum_s[lane] += jnp.dot(weight, v_s[n, near_rows(which, w), :], preferred_element_type=jnp.float32)
        return carry

    lax.fori_loop(0, nears, near_weights, 0)

    def far_weights(i, carry):
        for lane, (n, which) in enumerate(lanes):
            for r in range(FB):
                rows = slice(r * BLK, (r + 1) * BLK)
                top = top_s[lane, rows, :]
                part = None
                for j in range(2):
                    weight = jnp.exp2(far_s[lane, r, 2 * i + j] * TO_EXP2 - top).astype(jnp.bfloat16)
                    value = v_s[n, far_rows(which, r, 2 * i + j), :]
                    added = jnp.dot(weight, value, preferred_element_type=jnp.float32)
                    part = added if part is None else part + added
                sum_s[lane, rows, :] += part
        return carry

    lax.fori_loop(0, pairs, far_weights, 0)
    for lane, (n, which) in enumerate(lanes):
        total = sum_s[lane, :, DH:]
        o_s[2 * n + which] = sum_s[lane, :, :DH] / total
        lse_s[2 * n + which] = top_s[lane] + jnp.log(total) * LOG2E


def attend_kernel(heads, first, planes, seq_ref, near_ref, blocks_ref, count_ref, q_ref, q_other_ref, *refs):
    piece_refs = refs[:planes]
    keep_o, keep_lse, send = refs[planes : planes + 3]
    q_s, o_s, lse_s, k_s, v_s, near_s, far_s, top_s, sum_s = refs[planes + 3 :]
    z = lax.div(seq_ref[0], 2)
    v_s[:, :, DH:] = jnp.ones((len(heads), planes * ROWS, DH), jnp.bfloat16)
    for d, piece in enumerate(piece_refs):
        rows = pl.ds(pl.multiple_of(lax.rem(z + planes - d, planes) * ROWS, ROWS), ROWS)
        for n in range(len(heads)):
            at = 2 * (first + n) * ROWS
            k_s[n, rows, :] = piece[at : at + ROWS, :]
            v_s[n, rows, 0:DH] = piece[at + ROWS : at + 2 * ROWS, :]
    for n, head in enumerate(heads):
        columns = slice(head * DH, (head + 1) * DH)
        q_s[2 * n] = q_ref[:, columns]
        q_s[2 * n + 1] = q_other_ref[:, columns]
    tables = (near_ref, blocks_ref, count_ref, q_s, o_s, lse_s, k_s, v_s, near_s, far_s, top_s, sum_s)
    if len(heads) == 1:
        attend_lanes([(0, 0), (0, 1)], *tables)
    else:

        def one(which, carry):
            attend_lanes([(n, which) for n in range(len(heads))], *tables)
            return carry

        lax.fori_loop(0, 2, one, 0)
    lane = lax.broadcasted_iota(jnp.int32, (ROWS, DH), 1)
    packed = jnp.zeros((ROWS, DH), jnp.float32)
    for n in range(len(heads)):
        rows = slice(n * ROWS, (n + 1) * ROWS)
        keep_o[rows, :] = o_s[2 * n]
        keep_lse[rows, :] = lse_s[2 * n]
        send[rows, :] = o_s[2 * n + 1].astype(jnp.bfloat16)
        left = lse_s[2 * n + 1]
        for term in range(TERMS):
            piece = left.astype(jnp.bfloat16).astype(jnp.float32)
            packed = jnp.where(lane == n * TERMS + term, piece, packed)
            left = left - piece
    send[len(heads) * ROWS :, :] = packed.astype(jnp.bfloat16)


def attend(heads, first, queries, queries_other, pieces, seq, near, blocks, counts):
    planes, held = len(pieces), len(heads)
    lanes = max(held, 2)
    tokens = planes * ROWS
    each = pltpu.VMEM((2 * held, ROWS, DH), jnp.float32)
    elements = held * ROWS * 18 * BLK
    return pl.pallas_call(
        functools.partial(attend_kernel, heads, first, planes),
        out_shape=[
            jax.ShapeDtypeStruct((held * ROWS, DH), jnp.float32),
            jax.ShapeDtypeStruct((held * ROWS, DH), jnp.float32),
            jax.ShapeDtypeStruct(((held + 1) * ROWS, DH), jnp.bfloat16),
        ],
        in_specs=[SMEM] * 4 + [VMEM] * (2 + planes),
        out_specs=[VMEM] * 3,
        scratch_shapes=[
            pltpu.VMEM((2 * held, ROWS, DH), jnp.bfloat16),
            each,
            each,
            pltpu.VMEM((held, tokens, DH), jnp.bfloat16),
            pltpu.VMEM((held, tokens, 2 * DH), jnp.bfloat16),
            pltpu.VMEM((lanes, MAX_NEAR, ROWS, ROWS), jnp.float32),
            pltpu.VMEM((lanes, FB, MAX_EXTRA, BLK, BLK), jnp.float32),
            pltpu.VMEM((lanes, ROWS, BLK), jnp.float32),
            pltpu.VMEM((lanes, ROWS, 2 * DH), jnp.float32),
        ],
        compiler_params=pltpu.CompilerParams(vmem_limit_bytes=(36 if held > 2 else 24) << 20),
        cost_estimate=pl.CostEstimate(
            flops=40 * elements * DH, bytes_accessed=4 * held * tokens * DH, transcendentals=elements
        ),
        name="attend",
    )(seq, near, blocks, counts, queries, queries_other, *pieces)


def merge_kernel(*refs):
    out_ref, parts = refs[-1], refs[:-1]
    column = 0
    for o_ref, lse_ref, got_ref in zip(parts[0::3], parts[1::3], parts[2::3]):
        held = o_ref.shape[0] // ROWS
        packed = got_ref[held * ROWS :, :].astype(jnp.float32)
        lane = lax.broadcasted_iota(jnp.int32, packed.shape, 1)
        for n in range(held):
            rows = slice(n * ROWS, (n + 1) * ROWS)
            other_o = got_ref[rows, :].astype(jnp.float32)
            terms = (lane >= n * TERMS) & (lane < (n + 1) * TERMS)
            other_lse = jnp.sum(jnp.where(terms, packed, 0.0), axis=1, keepdims=True)
            lse = lse_ref[rows, :]
            top = jnp.maximum(lse, other_lse)
            mine, other = jnp.exp2(lse - top), jnp.exp2(other_lse - top)
            out = ((o_ref[rows, :] * mine + other_o * other) / (mine + other)).astype(out_ref.dtype)
            out_ref[:, column : column + DH] = out
            column += DH


def merge(*parts):
    size = sum(part.size for part in parts[0::3])
    return pl.pallas_call(
        merge_kernel,
        out_shape=jax.ShapeDtypeStruct((ROWS, size // ROWS), jnp.bfloat16),
        in_specs=[VMEM] * len(parts),
        out_specs=VMEM,
        compiler_params=pltpu.CompilerParams(vmem_limit_bytes=10 << 20),
        cost_estimate=pl.CostEstimate(flops=8 * size, bytes_accessed=30 * size, transcendentals=2 * size),
        name="merge",
    )(*parts)


def tile_kernel(count, y_ref, pair_ref, weight_ref, *refs):
    outs, sems = refs[:-1], refs[-1]
    width = outs[0].shape[1]
    copies = []
    for n, out in enumerate(outs):
        block = pair_ref[0] if n < count else 1 - pair_ref[0]
        start = pl.multiple_of((lax.rem(y_ref[0] + n, count) * 2 + block) * width, width)
        copies.append(pltpu.make_async_copy(weight_ref.at[:, pl.ds(start, width)], out, sems.at[n]))
    for copy in copies:
        copy.start()
    for copy in copies:
        copy.wait()


def tile(y, pair, weight, count):
    stay = pl.BlockSpec(memory_space=pl.ANY)
    shape = (weight.shape[0], weight.shape[1] // (2 * count))
    return pl.pallas_call(
        functools.partial(tile_kernel, count),
        out_shape=[jax.ShapeDtypeStruct(shape, weight.dtype)] * (count + 1),
        in_specs=[SMEM, SMEM, stay],
        out_specs=[stay] * (count + 1),
        scratch_shapes=[pltpu.SemaphoreType.DMA((count + 1,))],
        compiler_params=pltpu.CompilerParams(vmem_limit_bytes=1 << 20),
        cost_estimate=pl.CostEstimate(flops=0, bytes_accessed=4 * weight.size, transcendentals=0),
        name="tile",
    )(y, pair, weight)


def cross_kernel(q_ref, k_ref, v_ref, o_ref):
    def one(h, carry):
        columns = pl.ds(pl.multiple_of(h * DH, DH), DH)
        score = lax.dot_general(q_ref[:, columns], k_ref[:, columns], NT, preferred_element_type=jnp.float32)
        top = jnp.max(score, axis=1, keepdims=True) * TO_EXP2
        weight = jnp.exp2(score * TO_EXP2 - top)
        total = jnp.sum(weight, axis=1, keepdims=True)
        part = jnp.dot(weight.astype(jnp.bfloat16), v_ref[:, columns], preferred_element_type=jnp.float32)
        o_ref[:, columns] = (part / total).astype(o_ref.dtype)
        return carry

    lax.fori_loop(0, q_ref.shape[1] // DH, one, 0)


def cross(cross_query, text_keys, text_values):
    elements = cross_query.shape[0] * cross_query.shape[1] // DH * text_keys.shape[0]
    return pl.pallas_call(
        cross_kernel,
        out_shape=jax.ShapeDtypeStruct(cross_query.shape, jnp.bfloat16),
        in_specs=[VMEM] * 3,
        out_specs=VMEM,
        compiler_params=pltpu.CompilerParams(vmem_limit_bytes=8 << 20),
        cost_estimate=pl.CostEstimate(
            flops=40 * elements * DH, bytes_accessed=4 * cross_query.size, transcendentals=elements
        ),
        name="cross",
    )(cross_query, text_keys, text_values)


def project_kernel(first, sources, last, *refs):
    keep_ref = refs[0] if last else None
    refs = refs[1:] if last else refs
    heads, weights, refs = refs[:sources], refs[sources : 3 * sources], refs[3 * sources :]
    depth = heads[0].shape[1]
    rows = slice(first * DH, first * DH + depth)
    total_ref = refs[-1]
    for block in range(2):
        total = refs[0][block] if len(refs) > 1 + 2 * last else None
        for head_ref, weight_ref in zip(heads, weights[block::2]):
            part = jnp.dot(head_ref[...], weight_ref[rows, :], preferred_element_type=jnp.float32)
            total = part if total is None else total + part
        total_ref[block] = total
    if last:
        refs[-3][...] = total_ref[keep_ref[0]]
        refs[-2][...] = total_ref[1 - keep_ref[0]].astype(jnp.bfloat16)


def project(first, heads, weights, before=None, keep=None):
    rows, depth = heads[0].shape
    width = weights[0].shape[1]
    given = [*heads, *weights] + ([] if before is None else [before])
    both = jax.ShapeDtypeStruct((2, rows, width), jnp.float32)
    split = [jax.ShapeDtypeStruct((rows, width), dtype) for dtype in (jnp.float32, jnp.bfloat16)]
    last = keep is not None
    return pl.pallas_call(
        functools.partial(project_kernel, first, len(heads), last),
        out_shape=split if last else both,
        in_specs=[SMEM] * last + [VMEM] * len(given),
        out_specs=[VMEM] * 2 if last else VMEM,
        scratch_shapes=[pltpu.VMEM(both.shape, both.dtype)] if last else [],
        compiler_params=pltpu.CompilerParams(vmem_limit_bytes=22 << 20),
        cost_estimate=pl.CostEstimate(
            flops=4 * len(heads) * rows * depth * width,
            bytes_accessed=2 * len(heads) * depth * (rows + 2 * width),
            transcendentals=0,
        ),
        name="project",
    )(*([keep] if last else []), *given)


def body(n_seq, n_head, queries, keys, values, cross_query, text_keys, text_values, out_weight, block_list, block_count):
    n_z, n_y = n_seq // 2, n_head // 2
    seq = lax.axis_index("seq").reshape(1)
    head = lax.axis_index("head").reshape(1)
    pair = lax.axis_index("pair").reshape(1)
    cross_heads = cross(cross_query, text_keys, text_values)
    swap = [(s, s ^ 1) for s in range(n_seq)]

    def to_other(array):
        return lax.ppermute(array, "seq", swap)

    def z_shift(step):
        return [(s, (s // 2 + step) % n_z * 2 + s % 2) for s in range(n_seq)]

    def y_shift(step):
        return [(g, (g // 2 + step) % n_y * 2 + g % 2) for g in range(n_head)]

    held = [{0: array} for array in pack(keys, values)]
    sent = {1: [], -1: []}

    def hop(way, group, step, after=None):
        done = sent[way]
        array = held[group][way * (step - 1) % n_z]
        if len(done) >= IN_FLIGHT:
            at, where = done[-IN_FLIGHT]
            array, held[at][where] = lax.optimization_barrier((array, held[at][where]))
        if after is not None:
            array, after[0] = lax.optimization_barrier((array, after[0]))
        place = way * step % n_z
        held[group][place] = lax.ppermute(array, "seq", z_shift(way))
        done.append((group, place))

    def partial(group, start, stop):
        pieces = [held[group][d] for d in range(n_z)]
        return list(attend(GROUPS[group][start:stop], start, queries, queries_other, pieces, seq, near, blocks, counts))

    def join(*parts):
        return merge(*(array for part in parts for array in (*part[:2], to_other(part[2]))))

    def along_y(array):
        return [array] + [lax.ppermute(array, "head", y_shift(-dy)) for dy in range(1, n_y)]

    for group in (0, 1):
        hop(1, group, 1)
        hop(-1, group, 1)
    queries_other = to_other(queries)
    early = list(plan(n_seq, seq, block_list, block_count))
    tiles = list(tile(lax.div(head, 2), pair, out_weight, n_y))
    early[0], tiles[0], queries_other = lax.optimization_barrier((early[0], tiles[0], queries_other))
    hop(1, 0, 2)
    hop(-1, 0, 2)
    arrived = [lax.ppermute(tiles[dy], "head", y_shift(dy)) for dy in (1, n_y - 1)]
    arrived[1], tiles[2] = lax.optimization_barrier((arrived[1], tiles[2]))
    tiles[1:n_y] = [arrived[1], lax.ppermute(tiles[2], "head", y_shift(2)), arrived[0]]
    one_away = [(tiles[1], tiles[n_y - 1])]
    hop(1, 0, 3, one_away)
    tiles[1], tiles[n_y - 1] = one_away[0]
    hop(-1, 0, 3, early)
    blocks, counts, near = early
    hop(1, 0, 4)
    hop(-1, 1, 2)
    hop(1, 1, 2)
    hop(-1, 1, 3)
    hop(1, 1, 3)
    hop(-1, 1, 4)
    near, tiles[2] = lax.optimization_barrier((near, tiles[2]))
    weights = [tiles[0], tiles[n_y]]
    for mine in tiles[1:n_y]:
        weights += [mine, lax.ppermute(mine, "pair", [(0, 1), (1, 0)])]
    most = partial(0, 0, 3)
    near, *weights = lax.optimization_barrier((near, *weights))
    one, two = partial(1, 0, 1), partial(1, 1, 2)
    most[0], one[0], two[0] = lax.optimization_barrier((most[0], one[0], two[0]))
    before = project(GROUPS[0][0], along_y(join(most)), weights)
    rest = join(one, two)
    keep_block = (lax.rem(head, 2) != pair).astype(jnp.int32)
    keep, send = project(GROUPS[1][0], along_y(rest), weights, before, keep_block)
    got = lax.ppermute(send, "head", [(g, g ^ 1) for g in range(n_head)])
    return (keep + got.astype(jnp.float32)).astype(jnp.bfloat16), cross_heads


def solution(mesh):
    rows = P(("pair", "seq"), "head")
    text = P("pair", "head")
    return jax.shard_map(
        functools.partial(body, mesh.shape["seq"], mesh.shape["head"]),
        mesh=mesh,
        in_specs=(rows, rows, rows, rows, text, text, P("head", None), P(), P()),
        out_specs=(rows, rows),
        check_vma=False,
    )
```

```python
import functools
import math

import jax
import jax.numpy as jnp
from jax import lax
from jax.experimental import pallas as pl
from jax.experimental.pallas import tpu as pltpu
from jax.sharding import PartitionSpec as P

DH = 128
BLK = 128
FB = 3
ROWS = FB * BLK
MAX_EXTRA = 12
MAX_NEAR = 3
TERMS = 3
GROUPS = ((0, 1, 2), (3, 4))
IN_FLIGHT = 2
NEG = -1e30
LOG2E = math.log2(math.e)
TO_EXP2 = DH ** (-0.5) * LOG2E
NT = (((1,), (1,)), ((), ()))
SMEM = pl.BlockSpec(memory_space=pltpu.SMEM)
VMEM = pl.BlockSpec(memory_space=pltpu.VMEM)


def plan_kernel(last, seq_ref, list_ref, count_ref, blocks_out, count_out, near_out):
    side = seq_ref[0] % 2
    for which in range(2):
        frame = seq_ref[0] + which * (1 - 2 * side)
        found = jnp.int32(0)
        for w in range(MAX_NEAR):
            near_out[which * (MAX_NEAR + 1) + w] = 0
        for key_frame in (frame - 1, frame, frame + 1, 0):
            here = (key_frame % 2 == side) & (key_frame >= 0) & (key_frame <= last)
            if isinstance(key_frame, int):
                here &= frame > 1
            near_out[which * (MAX_NEAR + 1) + found] = jnp.where(here, key_frame // 2, 0)
            found += here.astype(jnp.int32)
        near_out[which * (MAX_NEAR + 1) + MAX_NEAR] = found
        for r in range(FB):
            row, out = frame * FB + r, which * FB + r
            for e in range(MAX_EXTRA + 1):
                blocks_out[out, e] = 0

            def one(j, extras, row=row, out=out, frame=frame):
                block = list_ref[row, j]
                key_frame = lax.div(block, FB)
                far = (jnp.abs(key_frame - frame) > 1) & (key_frame > 0) & (key_frame % 2 == side)
                blocks_out[out, extras] = jnp.where(
                    far, lax.div(key_frame, 2) * FB + block - key_frame * FB, 0
                )
                return extras + far.astype(jnp.int32)

            extras = lax.fori_loop(0, count_ref[row], one, jnp.int32(0))
            count_out[out] = extras


def plan(frames, seq, block_list, block_count):
    return pl.pallas_call(
        functools.partial(plan_kernel, frames - 1),
        out_shape=[
            jax.ShapeDtypeStruct((2 * FB, MAX_EXTRA + 1), jnp.int32),
            jax.ShapeDtypeStruct((2 * FB,), jnp.int32),
            jax.ShapeDtypeStruct((2 * (MAX_NEAR + 1),), jnp.int32),
        ],
        in_specs=[SMEM] * 3,
        out_specs=[SMEM] * 3,
        compiler_params=pltpu.CompilerParams(vmem_limit_bytes=1 << 20),
        cost_estimate=pl.CostEstimate(flops=1000, bytes_accessed=8000, transcendentals=0),
        name="plan",
    )(seq, block_list, block_count)


def pack_kernel(k_ref, v_ref, *outs):
    for heads, out in zip(GROUPS, outs):
        for n, head in enumerate(heads):
            columns = slice(head * DH, (head + 1) * DH)
            out[2 * n * ROWS : (2 * n + 1) * ROWS, :] = k_ref[:, columns]
            out[(2 * n + 1) * ROWS : (2 * n + 2) * ROWS, :] = v_ref[:, columns]


def pack(keys, values):
    return pl.pallas_call(
        pack_kernel,
        out_shape=[jax.ShapeDtypeStruct((2 * ROWS * len(heads), DH), jnp.bfloat16) for heads in GROUPS],
        in_specs=[VMEM, VMEM],
        out_specs=[VMEM] * len(GROUPS),
        compiler_params=pltpu.CompilerParams(vmem_limit_bytes=6 << 20),
        cost_estimate=pl.CostEstimate(flops=0, bytes_accessed=4 * keys.size * 2, transcendentals=0),
        name="pack",
    )(keys, values)


def attend_lanes(lanes, near_ref, blocks_ref, count_ref, q_s, o_s, lse_s, k_s, v_s, near_s, far_s, top_s, sum_s):
    frames = sorted({which for _, which in lanes}, key=str) if all(isinstance(w, int) for _, w in lanes) else [lanes[0][1]]
    nears = near_ref[frames[0] * (MAX_NEAR + 1) + MAX_NEAR]
    most = count_ref[frames[0] * FB]
    for which in frames:
        nears = jnp.maximum(nears, near_ref[which * (MAX_NEAR + 1) + MAX_NEAR])
        for r in range(FB):
            most = jnp.maximum(most, count_ref[which * FB + r])
    pairs = lax.div(most + 1, 2)

    def near_rows(which, w):
        return pl.ds(pl.multiple_of(near_ref[which * (MAX_NEAR + 1) + w] * ROWS, ROWS), ROWS)

    def far_rows(which, r, e):
        return pl.ds(pl.multiple_of(blocks_ref[which * FB + r, e] * BLK, BLK), BLK)

    top_s[...] = jnp.full_like(top_s, NEG)

    def near_scores(w, carry):
        for lane, (n, which) in enumerate(lanes):
            score = lax.dot_general(
                q_s[2 * n + which], k_s[n, near_rows(which, w), :], NT, preferred_element_type=jnp.float32
            )
            if len(frames) > 1:
                score = jnp.where(w < near_ref[which * (MAX_NEAR + 1) + MAX_NEAR], score, NEG)
            near_s[lane, w] = score
            best = jnp.maximum(jnp.maximum(score[:, :BLK], score[:, BLK : 2 * BLK]), score[:, 2 * BLK :])
            top_s[lane] = jnp.maximum(top_s[lane], best)
        return carry

    lax.fori_loop(0, nears, near_scores, 0)

    def far_scores(i, carry):
        for lane, (n, which) in enumerate(lanes):
            for r in range(FB):
                rows = slice(r * BLK, (r + 1) * BLK)
                best = top_s[lane, rows, :]
                for j in range(2):
                    e = 2 * i + j
                    score = lax.dot_general(
                        q_s[2 * n + which, rows, :], k_s[n, far_rows(which, r, e), :], NT, preferred_element_type=jnp.float32
                    )
                    score = jnp.where(e < count_ref[which * FB + r], score, NEG)
                    far_s[lane, r, e] = score
                    best = jnp.maximum(best, score)
                top_s[lane, rows, :] = best
        return carry

    lax.fori_loop(0, pairs, far_scores, 0)
    for lane in range(len(lanes)):
        top_s[lane] = jnp.broadcast_to(jnp.max(top_s[lane], axis=1, keepdims=True) * TO_EXP2, (ROWS, BLK))
    sum_s[...] = jnp.zeros_like(sum_s)

    def near_weights(w, carry):
        for lane, (n, which) in enumerate(lanes):
            top = top_s[lane]
            weights = [jnp.exp2(near_s[lane, w, :, c * BLK : (c + 1) * BLK] * TO_EXP2 - top) for c in range(FB)]
            weight = jnp.concatenate([p.astype(jnp.bfloat16) for p in weights], axis=1)
            sum_s[lane] += jnp.dot(weight, v_s[n, near_rows(which, w), :], preferred_element_type=jnp.float32)
        return carry

    lax.fori_loop(0, nears, near_weights, 0)

    def far_weights(i, carry):
        for lane, (n, which) in enumerate(lanes):
            for r in range(FB):
                rows = slice(r * BLK, (r + 1) * BLK)
                top = top_s[lane, rows, :]
                part = None
                for j in range(2):
                    weight = jnp.exp2(far_s[lane, r, 2 * i + j] * TO_EXP2 - top).astype(jnp.bfloat16)
                    value = v_s[n, far_rows(which, r, 2 * i + j), :]
                    added = jnp.dot(weight, value, preferred_element_type=jnp.float32)
                    part = added if part is None else part + added
                sum_s[lane, rows, :] += part
        return carry

    lax.fori_loop(0, pairs, far_weights, 0)
    for lane, (n, which) in enumerate(lanes):
        total = sum_s[lane, :, DH:]
        o_s[2 * n + which] = sum_s[lane, :, :DH] / total
        lse_s[2 * n + which] = top_s[lane] + jnp.log(total) * LOG2E


def attend_kernel(heads, first, planes, seq_ref, near_ref, blocks_ref, count_ref, q_ref, q_other_ref, *refs):
    piece_refs = refs[:planes]
    keep_o, keep_lse, send = refs[planes : planes + 3]
    q_s, o_s, lse_s, k_s, v_s, near_s, far_s, top_s, sum_s = refs[planes + 3 :]
    z = lax.div(seq_ref[0], 2)
    v_s[:, :, DH:] = jnp.ones((len(heads), planes * ROWS, DH), jnp.bfloat16)
    for d, piece in enumerate(piece_refs):
        rows = pl.ds(pl.multiple_of(lax.rem(z + planes - d, planes) * ROWS, ROWS), ROWS)
        for n in range(len(heads)):
            at = 2 * (first + n) * ROWS
            k_s[n, rows, :] = piece[at : at + ROWS, :]
            v_s[n, rows, 0:DH] = piece[at + ROWS : at + 2 * ROWS, :]
    for n, head in enumerate(heads):
        columns = slice(head * DH, (head + 1) * DH)
        q_s[2 * n] = q_ref[:, columns]
        q_s[2 * n + 1] = q_other_ref[:, columns]
    tables = (near_ref, blocks_ref, count_ref, q_s, o_s, lse_s, k_s, v_s, near_s, far_s, top_s, sum_s)
    if len(heads) == 1:
        attend_lanes([(0, 0), (0, 1)], *tables)
    else:

        def one(which, carry):
            attend_lanes([(n, which) for n in range(len(heads))], *tables)
            return carry

        lax.fori_loop(0, 2, one, 0)
    lane = lax.broadcasted_iota(jnp.int32, (ROWS, DH), 1)
    packed = jnp.zeros((ROWS, DH), jnp.float32)
    for n in range(len(heads)):
        rows = slice(n * ROWS, (n + 1) * ROWS)
        keep_o[rows, :] = o_s[2 * n]
        keep_lse[rows, :] = lse_s[2 * n]
        send[rows, :] = o_s[2 * n + 1].astype(jnp.bfloat16)
        left = lse_s[2 * n + 1]
        for term in range(TERMS):
            piece = left.astype(jnp.bfloat16).astype(jnp.float32)
            packed = jnp.where(lane == n * TERMS + term, piece, packed)
            left = left - piece
    send[len(heads) * ROWS :, :] = packed.astype(jnp.bfloat16)


def attend(heads, first, queries, queries_other, pieces, seq, near, blocks, counts):
    planes, held = len(pieces), len(heads)
    lanes = max(held, 2)
    tokens = planes * ROWS
    each = pltpu.VMEM((2 * held, ROWS, DH), jnp.float32)
    elements = held * ROWS * 18 * BLK
    return pl.pallas_call(
        functools.partial(attend_kernel, heads, first, planes),
        out_shape=[
            jax.ShapeDtypeStruct((held * ROWS, DH), jnp.float32),
            jax.ShapeDtypeStruct((held * ROWS, DH), jnp.float32),
            jax.ShapeDtypeStruct(((held + 1) * ROWS, DH), jnp.bfloat16),
        ],
        in_specs=[SMEM] * 4 + [VMEM] * (2 + planes),
        out_specs=[VMEM] * 3,
        scratch_shapes=[
            pltpu.VMEM((2 * held, ROWS, DH), jnp.bfloat16),
            each,
            each,
            pltpu.VMEM((held, tokens, DH), jnp.bfloat16),
            pltpu.VMEM((held, tokens, 2 * DH), jnp.bfloat16),
            pltpu.VMEM((lanes, MAX_NEAR, ROWS, ROWS), jnp.float32),
            pltpu.VMEM((lanes, FB, MAX_EXTRA, BLK, BLK), jnp.float32),
            pltpu.VMEM((lanes, ROWS, BLK), jnp.float32),
            pltpu.VMEM((lanes, ROWS, 2 * DH), jnp.float32),
        ],
        compiler_params=pltpu.CompilerParams(vmem_limit_bytes=(36 if held > 2 else 24) << 20),
        cost_estimate=pl.CostEstimate(
            flops=40 * elements * DH, bytes_accessed=4 * held * tokens * DH, transcendentals=elements
        ),
        name="attend",
    )(seq, near, blocks, counts, queries, queries_other, *pieces)


def merge_kernel(*refs):
    out_ref, parts = refs[-1], refs[:-1]
    column = 0
    for o_ref, lse_ref, got_ref in zip(parts[0::3], parts[1::3], parts[2::3]):
        held = o_ref.shape[0] // ROWS
        packed = got_ref[held * ROWS :, :].astype(jnp.float32)
        lane = lax.broadcasted_iota(jnp.int32, packed.shape, 1)
        for n in range(held):
            rows = slice(n * ROWS, (n + 1) * ROWS)
            other_o = got_ref[rows, :].astype(jnp.float32)
            terms = (lane >= n * TERMS) & (lane < (n + 1) * TERMS)
            other_lse = jnp.sum(jnp.where(terms, packed, 0.0), axis=1, keepdims=True)
            lse = lse_ref[rows, :]
            top = jnp.maximum(lse, other_lse)
            mine, other = jnp.exp2(lse - top), jnp.exp2(other_lse - top)
            out = ((o_ref[rows, :] * mine + other_o * other) / (mine + other)).astype(out_ref.dtype)
            out_ref[:, column : column + DH] = out
            column += DH


def merge(*parts):
    size = sum(part.size for part in parts[0::3])
    return pl.pallas_call(
        merge_kernel,
        out_shape=jax.ShapeDtypeStruct((ROWS, size // ROWS), jnp.bfloat16),
        in_specs=[VMEM] * len(parts),
        out_specs=VMEM,
        compiler_params=pltpu.CompilerParams(vmem_limit_bytes=10 << 20),
        cost_estimate=pl.CostEstimate(flops=8 * size, bytes_accessed=30 * size, transcendentals=2 * size),
        name="merge",
    )(*parts)


def tile_kernel(count, y_ref, pair_ref, weight_ref, *refs):
    outs, sems = refs[:-1], refs[-1]
    width = outs[0].shape[1]
    copies = []
    for n, out in enumerate(outs):
        block = pair_ref[0] if n < count else 1 - pair_ref[0]
        start = pl.multiple_of((lax.rem(y_ref[0] + n, count) * 2 + block) * width, width)
        copies.append(pltpu.make_async_copy(weight_ref.at[:, pl.ds(start, width)], out, sems.at[n]))
    for copy in copies:
        copy.start()
    for copy in copies:
        copy.wait()


def tile(y, pair, weight, count):
    stay = pl.BlockSpec(memory_space=pl.ANY)
    shape = (weight.shape[0], weight.shape[1] // (2 * count))
    return pl.pallas_call(
        functools.partial(tile_kernel, count),
        out_shape=[jax.ShapeDtypeStruct(shape, weight.dtype)] * (count + 1),
        in_specs=[SMEM, SMEM, stay],
        out_specs=[stay] * (count + 1),
        scratch_shapes=[pltpu.SemaphoreType.DMA((count + 1,))],
        compiler_params=pltpu.CompilerParams(vmem_limit_bytes=1 << 20),
        cost_estimate=pl.CostEstimate(flops=0, bytes_accessed=4 * weight.size, transcendentals=0),
        name="tile",
    )(y, pair, weight)


def cross_kernel(q_ref, k_ref, v_ref, o_ref):
    def one(h, carry):
        columns = pl.ds(pl.multiple_of(h * DH, DH), DH)
        score = lax.dot_general(q_ref[:, columns], k_ref[:, columns], NT, preferred_element_type=jnp.float32)
        top = jnp.max(score, axis=1, keepdims=True) * TO_EXP2
        weight = jnp.exp2(score * TO_EXP2 - top)
        total = jnp.sum(weight, axis=1, keepdims=True)
        part = jnp.dot(weight.astype(jnp.bfloat16), v_ref[:, columns], preferred_element_type=jnp.float32)
        o_ref[:, columns] = (part / total).astype(o_ref.dtype)
        return carry

    lax.fori_loop(0, q_ref.shape[1] // DH, one, 0)


def cross(cross_query, text_keys, text_values):
    elements = cross_query.shape[0] * cross_query.shape[1] // DH * text_keys.shape[0]
    return pl.pallas_call(
        cross_kernel,
        out_shape=jax.ShapeDtypeStruct(cross_query.shape, jnp.bfloat16),
        in_specs=[VMEM] * 3,
        out_specs=VMEM,
        compiler_params=pltpu.CompilerParams(vmem_limit_bytes=8 << 20),
        cost_estimate=pl.CostEstimate(
            flops=40 * elements * DH, bytes_accessed=4 * cross_query.size, transcendentals=elements
        ),
        name="cross",
    )(cross_query, text_keys, text_values)


def project_kernel(first, sources, last, *refs):
    keep_ref = refs[0] if last else None
    refs = refs[1:] if last else refs
    heads, weights, refs = refs[:sources], refs[sources : 3 * sources], refs[3 * sources :]
    depth = heads[0].shape[1]
    rows = slice(first * DH, first * DH + depth)
    total_ref = refs[-1]
    for block in range(2):
        total = refs[0][block] if len(refs) > 1 + 2 * last else None
        for head_ref, weight_ref in zip(heads, weights[block::2]):
            part = jnp.dot(head_ref[...], weight_ref[rows, :], preferred_element_type=jnp.float32)
            total = part if total is None else total + part
        total_ref[block] = total
    if last:
        refs[-3][...] = total_ref[keep_ref[0]]
        refs[-2][...] = total_ref[1 - keep_ref[0]].astype(jnp.bfloat16)


def project(first, heads, weights, before=None, keep=None):
    rows, depth = heads[0].shape
    width = weights[0].shape[1]
    given = [*heads, *weights] + ([] if before is None else [before])
    both = jax.ShapeDtypeStruct((2, rows, width), jnp.float32)
    split = [jax.ShapeDtypeStruct((rows, width), dtype) for dtype in (jnp.float32, jnp.bfloat16)]
    last = keep is not None
    return pl.pallas_call(
        functools.partial(project_kernel, first, len(heads), last),
        out_shape=split if last else both,
        in_specs=[SMEM] * last + [VMEM] * len(given),
        out_specs=[VMEM] * 2 if last else VMEM,
        scratch_shapes=[pltpu.VMEM(both.shape, both.dtype)] if last else [],
        compiler_params=pltpu.CompilerParams(vmem_limit_bytes=22 << 20),
        cost_estimate=pl.CostEstimate(
            flops=4 * len(heads) * rows * depth * width,
            bytes_accessed=2 * len(heads) * depth * (rows + 2 * width),
            transcendentals=0,
        ),
        name="project",
    )(*([keep] if last else []), *given)


def body(n_seq, n_head, queries, keys, values, cross_query, text_keys, text_values, out_weight, block_list, block_count):
    n_z, n_y = n_seq // 2, n_head // 2
    seq = lax.axis_index("seq").reshape(1)
    head = lax.axis_index("head").reshape(1)
    pair = lax.axis_index("pair").reshape(1)
    cross_heads = cross(cross_query, text_keys, text_values)
    swap = [(s, s ^ 1) for s in range(n_seq)]

    def to_other(array):
        return lax.ppermute(array, "seq", swap)

    def z_shift(step):
        return [(s, (s // 2 + step) % n_z * 2 + s % 2) for s in range(n_seq)]

    def y_shift(step):
        return [(g, (g // 2 + step) % n_y * 2 + g % 2) for g in range(n_head)]

    held = [{0: array} for array in pack(keys, values)]
    sent = {1: [], -1: []}

    def hop(way, group, step, after=None):
        done = sent[way]
        array = held[group][way * (step - 1) % n_z]
        if len(done) >= IN_FLIGHT:
            at, where = done[-IN_FLIGHT]
            array, held[at][where] = lax.optimization_barrier((array, held[at][where]))
        if after is not None:
            array, after[0] = lax.optimization_barrier((array, after[0]))
        place = way * step % n_z
        held[group][place] = lax.ppermute(array, "seq", z_shift(way))
        done.append((group, place))

    def partial(group, start, stop):
        pieces = [held[group][d] for d in range(n_z)]
        return list(attend(GROUPS[group][start:stop], start, queries, queries_other, pieces, seq, near, blocks, counts))

    def join(*parts):
        return merge(*(array for part in parts for array in (*part[:2], to_other(part[2]))))

    def along_y(array):
        return [array] + [lax.ppermute(array, "head", y_shift(-dy)) for dy in range(1, n_y)]

    for group in (0, 1):
        hop(1, group, 1)
        hop(-1, group, 1)
    queries_other = to_other(queries)
    early = list(plan(n_seq, seq, block_list, block_count))
    out_weight, queries_other = lax.optimization_barrier((out_weight, queries_other))
    tiles = list(tile(lax.div(head, 2), pair, out_weight, n_y))
    early[0], tiles[0], queries_other = lax.optimization_barrier((early[0], tiles[0], queries_other))
    hop(1, 0, 2)
    hop(-1, 0, 2)
    arrived = [lax.ppermute(tiles[dy], "head", y_shift(dy)) for dy in (1, n_y - 1)]
    arrived[1], tiles[2] = lax.optimization_barrier((arrived[1], tiles[2]))
    tiles[1:n_y] = [arrived[1], lax.ppermute(tiles[2], "head", y_shift(2)), arrived[0]]
    hop(1, 1, 2)
    one_away = [(tiles[1], tiles[n_y - 1])]
    hop(1, 0, 3, one_away)
    tiles[1], tiles[n_y - 1] = one_away[0]
    hop(-1, 0, 3, early)
    blocks, counts, near = early
    hop(1, 0, 4)
    hop(-1, 1, 2)
    hop(-1, 1, 3)
    hop(1, 1, 3)
    hop(-1, 1, 4)
    near, tiles[2] = lax.optimization_barrier((near, tiles[2]))
    weights = [tiles[0], tiles[n_y]]
    for mine in tiles[1:n_y]:
        weights += [mine, lax.ppermute(mine, "pair", [(0, 1), (1, 0)])]
    most = partial(0, 0, 3)
    near, *weights = lax.optimization_barrier((near, *weights))
    rest = partial(1, 0, 2)
    most[0], rest[0] = lax.optimization_barrier((most[0], rest[0]))
    before = project(GROUPS[0][0], along_y(join(most)), weights)
    rest = join(rest)
    keep_block = (lax.rem(head, 2) != pair).astype(jnp.int32)
    keep, send = project(GROUPS[1][0], along_y(rest), weights, before, keep_block)
    got = lax.ppermute(send, "head", [(g, g ^ 1) for g in range(n_head)])
    return (keep + got.astype(jnp.float32)).astype(jnp.bfloat16), cross_heads


def solution(mesh):
    rows = P(("pair", "seq"), "head")
    text = P("pair", "head")
    return jax.shard_map(
        functools.partial(body, mesh.shape["seq"], mesh.shape["head"]),
        mesh=mesh,
        in_specs=(rows, rows, rows, rows, text, text, P("head", None), P(), P()),
        out_specs=(rows, rows),
        check_vma=False,
    )
```

```python
import functools
import math

import jax
import jax.numpy as jnp
from jax import lax
from jax.experimental import pallas as pl
from jax.experimental.pallas import tpu as pltpu
from jax.sharding import PartitionSpec as P

DH = 128
BLK = 128
FB = 3
ROWS = FB * BLK
MAX_EXTRA = 12
MAX_NEAR = 3
TERMS = 3
GROUPS = ((0, 1, 2), (3, 4))
IN_FLIGHT = 2
NEG = -1e30
LOG2E = math.log2(math.e)
TO_EXP2 = DH ** (-0.5) * LOG2E
NT = (((1,), (1,)), ((), ()))
SMEM = pl.BlockSpec(memory_space=pltpu.SMEM)
VMEM = pl.BlockSpec(memory_space=pltpu.VMEM)


def plan_kernel(last, seq_ref, list_ref, count_ref, blocks_out, count_out, near_out):
    side = seq_ref[0] % 2
    for which in range(2):
        frame = seq_ref[0] + which * (1 - 2 * side)
        found = jnp.int32(0)
        for w in range(MAX_NEAR):
            near_out[which * (MAX_NEAR + 1) + w] = 0
        for key_frame in (frame - 1, frame, frame + 1, 0):
            here = (key_frame % 2 == side) & (key_frame >= 0) & (key_frame <= last)
            if isinstance(key_frame, int):
                here &= frame > 1
            near_out[which * (MAX_NEAR + 1) + found] = jnp.where(here, key_frame // 2, 0)
            found += here.astype(jnp.int32)
        near_out[which * (MAX_NEAR + 1) + MAX_NEAR] = found
        for r in range(FB):
            row, out = frame * FB + r, which * FB + r
            for e in range(MAX_EXTRA + 1):
                blocks_out[out, e] = 0

            def one(j, extras, row=row, out=out, frame=frame):
                block = list_ref[row, j]
                key_frame = lax.div(block, FB)
                far = (jnp.abs(key_frame - frame) > 1) & (key_frame > 0) & (key_frame % 2 == side)
                blocks_out[out, extras] = jnp.where(
                    far, lax.div(key_frame, 2) * FB + block - key_frame * FB, 0
                )
                return extras + far.astype(jnp.int32)

            extras = lax.fori_loop(0, count_ref[row], one, jnp.int32(0))
            count_out[out] = extras


def plan(frames, seq, block_list, block_count):
    return pl.pallas_call(
        functools.partial(plan_kernel, frames - 1),
        out_shape=[
            jax.ShapeDtypeStruct((2 * FB, MAX_EXTRA + 1), jnp.int32),
            jax.ShapeDtypeStruct((2 * FB,), jnp.int32),
            jax.ShapeDtypeStruct((2 * (MAX_NEAR + 1),), jnp.int32),
        ],
        in_specs=[SMEM] * 3,
        out_specs=[SMEM] * 3,
        compiler_params=pltpu.CompilerParams(vmem_limit_bytes=1 << 20),
        cost_estimate=pl.CostEstimate(flops=1000, bytes_accessed=8000, transcendentals=0),
        name="plan",
    )(seq, block_list, block_count)


def pack_kernel(k_ref, v_ref, *outs):
    for heads, out in zip(GROUPS, outs):
        for n, head in enumerate(heads):
            columns = slice(head * DH, (head + 1) * DH)
            out[2 * n * ROWS : (2 * n + 1) * ROWS, :] = k_ref[:, columns]
            out[(2 * n + 1) * ROWS : (2 * n + 2) * ROWS, :] = v_ref[:, columns]


def pack(keys, values):
    return pl.pallas_call(
        pack_kernel,
        out_shape=[jax.ShapeDtypeStruct((2 * ROWS * len(heads), DH), jnp.bfloat16) for heads in GROUPS],
        in_specs=[VMEM, VMEM],
        out_specs=[VMEM] * len(GROUPS),
        compiler_params=pltpu.CompilerParams(vmem_limit_bytes=6 << 20),
        cost_estimate=pl.CostEstimate(flops=0, bytes_accessed=4 * keys.size * 2, transcendentals=0),
        name="pack",
    )(keys, values)


def attend_lanes(lanes, near_ref, blocks_ref, count_ref, q_s, o_s, lse_s, k_s, v_s, near_s, far_s, top_s, sum_s):
    frames = sorted({which for _, which in lanes}, key=str) if all(isinstance(w, int) for _, w in lanes) else [lanes[0][1]]
    nears = near_ref[frames[0] * (MAX_NEAR + 1) + MAX_NEAR]
    most = count_ref[frames[0] * FB]
    for which in frames:
        nears = jnp.maximum(nears, near_ref[which * (MAX_NEAR + 1) + MAX_NEAR])
        for r in range(FB):
            most = jnp.maximum(most, count_ref[which * FB + r])
    pairs = lax.div(most + 1, 2)

    def near_rows(which, w):
        return pl.ds(pl.multiple_of(near_ref[which * (MAX_NEAR + 1) + w] * ROWS, ROWS), ROWS)

    def far_rows(which, r, e):
        return pl.ds(pl.multiple_of(blocks_ref[which * FB + r, e] * BLK, BLK), BLK)

    top_s[...] = jnp.full_like(top_s, NEG)

    def near_scores(w, carry):
        for lane, (n, which) in enumerate(lanes):
            score = lax.dot_general(
                q_s[2 * n + which], k_s[n, near_rows(which, w), :], NT, preferred_element_type=jnp.float32
            )
            if len(frames) > 1:
                score = jnp.where(w < near_ref[which * (MAX_NEAR + 1) + MAX_NEAR], score, NEG)
            near_s[lane, w] = score
            best = jnp.maximum(jnp.maximum(score[:, :BLK], score[:, BLK : 2 * BLK]), score[:, 2 * BLK :])
            top_s[lane] = jnp.maximum(top_s[lane], best)
        return carry

    lax.fori_loop(0, nears, near_scores, 0)

    def far_scores(i, carry):
        for lane, (n, which) in enumerate(lanes):
            for r in range(FB):
                rows = slice(r * BLK, (r + 1) * BLK)
                best = top_s[lane, rows, :]
                for j in range(2):
                    e = 2 * i + j
                    score = lax.dot_general(
                        q_s[2 * n + which, rows, :], k_s[n, far_rows(which, r, e), :], NT, preferred_element_type=jnp.float32
                    )
                    score = jnp.where(e < count_ref[which * FB + r], score, NEG)
                    far_s[lane, r, e] = score
                    best = jnp.maximum(best, score)
                top_s[lane, rows, :] = best
        return carry

    lax.fori_loop(0, pairs, far_scores, 0)
    for lane in range(len(lanes)):
        top_s[lane] = jnp.broadcast_to(jnp.max(top_s[lane], axis=1, keepdims=True) * TO_EXP2, (ROWS, BLK))
    sum_s[...] = jnp.zeros_like(sum_s)

    def near_weights(w, carry):
        for lane, (n, which) in enumerate(lanes):
            top = top_s[lane]
            weights = [jnp.exp2(near_s[lane, w, :, c * BLK : (c + 1) * BLK] * TO_EXP2 - top) for c in range(FB)]
            weight = jnp.concatenate([p.astype(jnp.bfloat16) for p in weights], axis=1)
            sum_s[lane] += jnp.dot(weight, v_s[n, near_rows(which, w), :], preferred_element_type=jnp.float32)
        return carry

    lax.fori_loop(0, nears, near_weights, 0)

    def far_weights(i, carry):
        for lane, (n, which) in enumerate(lanes):
            for r in range(FB):
                rows = slice(r * BLK, (r + 1) * BLK)
                top = top_s[lane, rows, :]
                part = None
                for j in range(2):
                    weight = jnp.exp2(far_s[lane, r, 2 * i + j] * TO_EXP2 - top).astype(jnp.bfloat16)
                    value = v_s[n, far_rows(which, r, 2 * i + j), :]
                    added = jnp.dot(weight, value, preferred_element_type=jnp.float32)
                    part = added if part is None else part + added
                sum_s[lane, rows, :] += part
        return carry

    lax.fori_loop(0, pairs, far_weights, 0)
    for lane, (n, which) in enumerate(lanes):
        total = sum_s[lane, :, DH:]
        o_s[2 * n + which] = sum_s[lane, :, :DH] / total
        lse_s[2 * n + which] = top_s[lane] + jnp.log(total) * LOG2E


def attend_kernel(heads, first, planes, seq_ref, near_ref, blocks_ref, count_ref, q_ref, q_other_ref, *refs):
    piece_refs = refs[:planes]
    keep_o, keep_lse, send = refs[planes : planes + 3]
    q_s, o_s, lse_s, k_s, v_s, near_s, far_s, top_s, sum_s = refs[planes + 3 :]
    z = lax.div(seq_ref[0], 2)
    v_s[:, :, DH:] = jnp.ones((len(heads), planes * ROWS, DH), jnp.bfloat16)
    for d, piece in enumerate(piece_refs):
        rows = pl.ds(pl.multiple_of(lax.rem(z + planes - d, planes) * ROWS, ROWS), ROWS)
        for n in range(len(heads)):
            at = 2 * (first + n) * ROWS
            k_s[n, rows, :] = piece[at : at + ROWS, :]
            v_s[n, rows, 0:DH] = piece[at + ROWS : at + 2 * ROWS, :]
    for n, head in enumerate(heads):
        columns = slice(head * DH, (head + 1) * DH)
        q_s[2 * n] = q_ref[:, columns]
        q_s[2 * n + 1] = q_other_ref[:, columns]
    tables = (near_ref, blocks_ref, count_ref, q_s, o_s, lse_s, k_s, v_s, near_s, far_s, top_s, sum_s)
    if len(heads) == 1:
        attend_lanes([(0, 0), (0, 1)], *tables)
    else:

        def one(which, carry):
            attend_lanes([(n, which) for n in range(len(heads))], *tables)
            return carry

        lax.fori_loop(0, 2, one, 0)
    lane = lax.broadcasted_iota(jnp.int32, (ROWS, DH), 1)
    packed = jnp.zeros((ROWS, DH), jnp.float32)
    for n in range(len(heads)):
        rows = slice(n * ROWS, (n + 1) * ROWS)
        keep_o[rows, :] = o_s[2 * n]
        keep_lse[rows, :] = lse_s[2 * n]
        send[rows, :] = o_s[2 * n + 1].astype(jnp.bfloat16)
        left = lse_s[2 * n + 1]
        for term in range(TERMS):
            piece = left.astype(jnp.bfloat16).astype(jnp.float32)
            packed = jnp.where(lane == n * TERMS + term, piece, packed)
            left = left - piece
    send[len(heads) * ROWS :, :] = packed.astype(jnp.bfloat16)


def attend(heads, first, queries, queries_other, pieces, seq, near, blocks, counts):
    planes, held = len(pieces), len(heads)
    lanes = max(held, 2)
    tokens = planes * ROWS
    each = pltpu.VMEM((2 * held, ROWS, DH), jnp.float32)
    elements = held * ROWS * 18 * BLK
    return pl.pallas_call(
        functools.partial(attend_kernel, heads, first, planes),
        out_shape=[
            jax.ShapeDtypeStruct((held * ROWS, DH), jnp.float32),
            jax.ShapeDtypeStruct((held * ROWS, DH), jnp.float32),
            jax.ShapeDtypeStruct(((held + 1) * ROWS, DH), jnp.bfloat16),
        ],
        in_specs=[SMEM] * 4 + [VMEM] * (2 + planes),
        out_specs=[VMEM] * 3,
        scratch_shapes=[
            pltpu.VMEM((2 * held, ROWS, DH), jnp.bfloat16),
            each,
            each,
            pltpu.VMEM((held, tokens, DH), jnp.bfloat16),
            pltpu.VMEM((held, tokens, 2 * DH), jnp.bfloat16),
            pltpu.VMEM((lanes, MAX_NEAR, ROWS, ROWS), jnp.float32),
            pltpu.VMEM((lanes, FB, MAX_EXTRA, BLK, BLK), jnp.float32),
            pltpu.VMEM((lanes, ROWS, BLK), jnp.float32),
            pltpu.VMEM((lanes, ROWS, 2 * DH), jnp.float32),
        ],
        compiler_params=pltpu.CompilerParams(vmem_limit_bytes=(36 if held > 2 else 24) << 20),
        cost_estimate=pl.CostEstimate(
            flops=40 * elements * DH, bytes_accessed=4 * held * tokens * DH, transcendentals=elements
        ),
        name="attend",
    )(seq, near, blocks, counts, queries, queries_other, *pieces)


def merge_kernel(*refs):
    out_ref, parts = refs[-1], refs[:-1]
    column = 0
    for o_ref, lse_ref, got_ref in zip(parts[0::3], parts[1::3], parts[2::3]):
        held = o_ref.shape[0] // ROWS
        packed = got_ref[held * ROWS :, :].astype(jnp.float32)
        lane = lax.broadcasted_iota(jnp.int32, packed.shape, 1)
        for n in range(held):
            rows = slice(n * ROWS, (n + 1) * ROWS)
            other_o = got_ref[rows, :].astype(jnp.float32)
            terms = (lane >= n * TERMS) & (lane < (n + 1) * TERMS)
            other_lse = jnp.sum(jnp.where(terms, packed, 0.0), axis=1, keepdims=True)
            lse = lse_ref[rows, :]
            top = jnp.maximum(lse, other_lse)
            mine, other = jnp.exp2(lse - top), jnp.exp2(other_lse - top)
            out = ((o_ref[rows, :] * mine + other_o * other) / (mine + other)).astype(out_ref.dtype)
            out_ref[:, column : column + DH] = out
            column += DH


def merge(*parts):
    size = sum(part.size for part in parts[0::3])
    return pl.pallas_call(
        merge_kernel,
        out_shape=jax.ShapeDtypeStruct((ROWS, size // ROWS), jnp.bfloat16),
        in_specs=[VMEM] * len(parts),
        out_specs=VMEM,
        compiler_params=pltpu.CompilerParams(vmem_limit_bytes=10 << 20),
        cost_estimate=pl.CostEstimate(flops=8 * size, bytes_accessed=30 * size, transcendentals=2 * size),
        name="merge",
    )(*parts)


def tile_kernel(count, y_ref, pair_ref, weight_ref, *refs):
    outs, sems = refs[:-1], refs[-1]
    width = outs[0].shape[1]
    copies = []
    for n, out in enumerate(outs):
        block = pair_ref[0] if n < count else 1 - pair_ref[0]
        start = pl.multiple_of((lax.rem(y_ref[0] + n, count) * 2 + block) * width, width)
        copies.append(pltpu.make_async_copy(weight_ref.at[:, pl.ds(start, width)], out, sems.at[n]))
    for copy in copies:
        copy.start()
    for copy in copies:
        copy.wait()


def tile(y, pair, weight, count):
    stay = pl.BlockSpec(memory_space=pl.ANY)
    shape = (weight.shape[0], weight.shape[1] // (2 * count))
    return pl.pallas_call(
        functools.partial(tile_kernel, count),
        out_shape=[jax.ShapeDtypeStruct(shape, weight.dtype)] * (count + 1),
        in_specs=[SMEM, SMEM, stay],
        out_specs=[stay] * (count + 1),
        scratch_shapes=[pltpu.SemaphoreType.DMA((count + 1,))],
        compiler_params=pltpu.CompilerParams(vmem_limit_bytes=1 << 20),
        cost_estimate=pl.CostEstimate(flops=0, bytes_accessed=4 * weight.size, transcendentals=0),
        name="tile",
    )(y, pair, weight)


def cross_kernel(q_ref, k_ref, v_ref, o_ref):
    def one(h, carry):
        columns = pl.ds(pl.multiple_of(h * DH, DH), DH)
        score = lax.dot_general(q_ref[:, columns], k_ref[:, columns], NT, preferred_element_type=jnp.float32)
        top = jnp.max(score, axis=1, keepdims=True) * TO_EXP2
        weight = jnp.exp2(score * TO_EXP2 - top)
        total = jnp.sum(weight, axis=1, keepdims=True)
        part = jnp.dot(weight.astype(jnp.bfloat16), v_ref[:, columns], preferred_element_type=jnp.float32)
        o_ref[:, columns] = (part / total).astype(o_ref.dtype)
        return carry

    lax.fori_loop(0, q_ref.shape[1] // DH, one, 0)


def cross(cross_query, text_keys, text_values):
    elements = cross_query.shape[0] * cross_query.shape[1] // DH * text_keys.shape[0]
    return pl.pallas_call(
        cross_kernel,
        out_shape=jax.ShapeDtypeStruct(cross_query.shape, jnp.bfloat16),
        in_specs=[VMEM] * 3,
        out_specs=VMEM,
        compiler_params=pltpu.CompilerParams(vmem_limit_bytes=8 << 20),
        cost_estimate=pl.CostEstimate(
            flops=40 * elements * DH, bytes_accessed=4 * cross_query.size, transcendentals=elements
        ),
        name="cross",
    )(cross_query, text_keys, text_values)


def project_kernel(first, sources, last, *refs):
    keep_ref = refs[0] if last else None
    refs = refs[1:] if last else refs
    heads, weights, refs = refs[:sources], refs[sources : 3 * sources], refs[3 * sources :]
    depth = heads[0].shape[1]
    rows = slice(first * DH, first * DH + depth)
    total_ref = refs[-1]
    for block in range(2):
        total = refs[0][block] if len(refs) > 1 + 2 * last else None
        for head_ref, weight_ref in zip(heads, weights[block::2]):
            part = jnp.dot(head_ref[...], weight_ref[rows, :], preferred_element_type=jnp.float32)
            total = part if total is None else total + part
        total_ref[block] = total
    if last:
        refs[-3][...] = total_ref[keep_ref[0]]
        refs[-2][...] = total_ref[1 - keep_ref[0]].astype(jnp.bfloat16)


def project(first, heads, weights, before=None, keep=None):
    rows, depth = heads[0].shape
    width = weights[0].shape[1]
    given = [*heads, *weights] + ([] if before is None else [before])
    both = jax.ShapeDtypeStruct((2, rows, width), jnp.float32)
    split = [jax.ShapeDtypeStruct((rows, width), dtype) for dtype in (jnp.float32, jnp.bfloat16)]
    last = keep is not None
    return pl.pallas_call(
        functools.partial(project_kernel, first, len(heads), last),
        out_shape=split if last else both,
        in_specs=[SMEM] * last + [VMEM] * len(given),
        out_specs=[VMEM] * 2 if last else VMEM,
        scratch_shapes=[pltpu.VMEM(both.shape, both.dtype)] if last else [],
        compiler_params=pltpu.CompilerParams(vmem_limit_bytes=22 << 20),
        cost_estimate=pl.CostEstimate(
            flops=4 * len(heads) * rows * depth * width,
            bytes_accessed=2 * len(heads) * depth * (rows + 2 * width),
            transcendentals=0,
        ),
        name="project",
    )(*([keep] if last else []), *given)


def body(n_seq, n_head, queries, keys, values, cross_query, text_keys, text_values, out_weight, block_list, block_count):
    n_z, n_y = n_seq // 2, n_head // 2
    seq = lax.axis_index("seq").reshape(1)
    head = lax.axis_index("head").reshape(1)
    pair = lax.axis_index("pair").reshape(1)
    cross_heads = cross(cross_query, text_keys, text_values)
    swap = [(s, s ^ 1) for s in range(n_seq)]

    def to_other(array):
        return lax.ppermute(array, "seq", swap)

    def z_shift(step):
        return [(s, (s // 2 + step) % n_z * 2 + s % 2) for s in range(n_seq)]

    def y_shift(step):
        return [(g, (g // 2 + step) % n_y * 2 + g % 2) for g in range(n_head)]

    held = [{0: array} for array in pack(keys, values)]
    sent = {1: [], -1: []}

    def hop(way, group, step, after=None):
        done = sent[way]
        array = held[group][way * (step - 1) % n_z]
        if len(done) >= IN_FLIGHT:
            at, where = done[-IN_FLIGHT]
            array, held[at][where] = lax.optimization_barrier((array, held[at][where]))
        if after is not None:
            array, after[0] = lax.optimization_barrier((array, after[0]))
        place = way * step % n_z
        held[group][place] = lax.ppermute(array, "seq", z_shift(way))
        done.append((group, place))

    def partial(group, start, stop):
        pieces = [held[group][d] for d in range(n_z)]
        return list(attend(GROUPS[group][start:stop], start, queries, queries_other, pieces, seq, near, blocks, counts))

    def join(*parts):
        return merge(*(array for part in parts for array in (*part[:2], to_other(part[2]))))

    def along_y(array):
        return [array] + [lax.ppermute(array, "head", y_shift(-dy)) for dy in range(1, n_y)]

    for group in (0, 1):
        hop(1, group, 1)
        hop(-1, group, 1)
    queries_other = to_other(queries)
    early = list(plan(n_seq, seq, block_list, block_count))
    out_weight, held[0][1] = lax.optimization_barrier((out_weight, held[0][1]))
    tiles = list(tile(lax.div(head, 2), pair, out_weight, n_y))
    early[0], tiles[0], queries_other = lax.optimization_barrier((early[0], tiles[0], queries_other))
    hop(1, 0, 2)
    hop(-1, 0, 2)
    arrived = [lax.ppermute(tiles[dy], "head", y_shift(dy)) for dy in (1, n_y - 1)]
    arrived[1], tiles[2] = lax.optimization_barrier((arrived[1], tiles[2]))
    tiles[1:n_y] = [arrived[1], lax.ppermute(tiles[2], "head", y_shift(2)), arrived[0]]
    hop(1, 1, 2)
    hop(1, 0, 3)
    hop(-1, 0, 3, early)
    blocks, counts, near = early
    one_away = [(tiles[1], tiles[n_y - 1])]
    hop(1, 0, 4, one_away)
    tiles[1], tiles[n_y - 1] = one_away[0]
    hop(-1, 1, 2)
    hop(-1, 1, 3)
    hop(1, 1, 3)
    hop(-1, 1, 4)
    near, tiles[2] = lax.optimization_barrier((near, tiles[2]))
    weights = [tiles[0], tiles[n_y]]
    for mine in tiles[1:n_y]:
        weights += [mine, lax.ppermute(mine, "pair", [(0, 1), (1, 0)])]
    most = partial(0, 0, 3)
    near, *weights = lax.optimization_barrier((near, *weights))
    rest = partial(1, 0, 2)
    most[0], rest[0] = lax.optimization_barrier((most[0], rest[0]))
    before = project(GROUPS[0][0], along_y(join(most)), weights)
    rest = join(rest)
    keep_block = (lax.rem(head, 2) != pair).astype(jnp.int32)
    keep, send = project(GROUPS[1][0], along_y(rest), weights, before, keep_block)
    got = lax.ppermute(send, "head", [(g, g ^ 1) for g in range(n_head)])
    return (keep + got.astype(jnp.float32)).astype(jnp.bfloat16), cross_heads


def solution(mesh):
    rows = P(("pair", "seq"), "head")
    text = P("pair", "head")
    return jax.shard_map(
        functools.partial(body, mesh.shape["seq"], mesh.shape["head"]),
        mesh=mesh,
        in_specs=(rows, rows, rows, rows, text, text, P("head", None), P(), P()),
        out_specs=(rows, rows),
        check_vma=False,
    )
```

```python
import functools
import math

import jax
import jax.numpy as jnp
from jax import lax
from jax.experimental import pallas as pl
from jax.experimental.pallas import tpu as pltpu
from jax.sharding import PartitionSpec as P

DH = 128
BLK = 128
FB = 3
ROWS = FB * BLK
MAX_EXTRA = 12
MAX_NEAR = 3
TERMS = 3
GROUPS = ((0, 1, 2), (3, 4))
IN_FLIGHT = 2
NEG = -1e30
LOG2E = math.log2(math.e)
TO_EXP2 = DH ** (-0.5) * LOG2E
NT = (((1,), (1,)), ((), ()))
SMEM = pl.BlockSpec(memory_space=pltpu.SMEM)
VMEM = pl.BlockSpec(memory_space=pltpu.VMEM)


def plan_kernel(last, seq_ref, list_ref, count_ref, blocks_out, count_out, near_out):
    side = seq_ref[0] % 2
    for which in range(2):
        frame = seq_ref[0] + which * (1 - 2 * side)
        found = jnp.int32(0)
        for w in range(MAX_NEAR):
            near_out[which * (MAX_NEAR + 1) + w] = 0
        for key_frame in (frame - 1, frame, frame + 1, 0):
            here = (key_frame % 2 == side) & (key_frame >= 0) & (key_frame <= last)
            if isinstance(key_frame, int):
                here &= frame > 1
            near_out[which * (MAX_NEAR + 1) + found] = jnp.where(here, key_frame // 2, 0)
            found += here.astype(jnp.int32)
        near_out[which * (MAX_NEAR + 1) + MAX_NEAR] = found
        for r in range(FB):
            row, out = frame * FB + r, which * FB + r
            for e in range(MAX_EXTRA + 1):
                blocks_out[out, e] = 0

            def one(j, extras, row=row, out=out, frame=frame):
                block = list_ref[row, j]
                key_frame = lax.div(block, FB)
                far = (jnp.abs(key_frame - frame) > 1) & (key_frame > 0) & (key_frame % 2 == side)
                blocks_out[out, extras] = jnp.where(
                    far, lax.div(key_frame, 2) * FB + block - key_frame * FB, 0
                )
                return extras + far.astype(jnp.int32)

            extras = lax.fori_loop(0, count_ref[row], one, jnp.int32(0))
            count_out[out] = extras


def plan(frames, seq, block_list, block_count):
    return pl.pallas_call(
        functools.partial(plan_kernel, frames - 1),
        out_shape=[
            jax.ShapeDtypeStruct((2 * FB, MAX_EXTRA + 1), jnp.int32),
            jax.ShapeDtypeStruct((2 * FB,), jnp.int32),
            jax.ShapeDtypeStruct((2 * (MAX_NEAR + 1),), jnp.int32),
        ],
        in_specs=[SMEM] * 3,
        out_specs=[SMEM] * 3,
        compiler_params=pltpu.CompilerParams(vmem_limit_bytes=1 << 20),
        cost_estimate=pl.CostEstimate(flops=1000, bytes_accessed=8000, transcendentals=0),
        name="plan",
    )(seq, block_list, block_count)


def pack_kernel(k_ref, v_ref, *outs):
    for heads, out in zip(GROUPS, outs):
        for n, head in enumerate(heads):
            columns = slice(head * DH, (head + 1) * DH)
            out[2 * n * ROWS : (2 * n + 1) * ROWS, :] = k_ref[:, columns]
            out[(2 * n + 1) * ROWS : (2 * n + 2) * ROWS, :] = v_ref[:, columns]


def pack(keys, values):
    return pl.pallas_call(
        pack_kernel,
        out_shape=[jax.ShapeDtypeStruct((2 * ROWS * len(heads), DH), jnp.bfloat16) for heads in GROUPS],
        in_specs=[VMEM, VMEM],
        out_specs=[VMEM] * len(GROUPS),
        compiler_params=pltpu.CompilerParams(vmem_limit_bytes=6 << 20),
        cost_estimate=pl.CostEstimate(flops=0, bytes_accessed=4 * keys.size * 2, transcendentals=0),
        name="pack",
    )(keys, values)


def attend_lanes(lanes, near_ref, blocks_ref, count_ref, q_s, o_s, lse_s, k_s, v_s, near_s, far_s, top_s, sum_s):
    frames = sorted({which for _, which in lanes}, key=str) if all(isinstance(w, int) for _, w in lanes) else [lanes[0][1]]
    nears = near_ref[frames[0] * (MAX_NEAR + 1) + MAX_NEAR]
    most = count_ref[frames[0] * FB]
    for which in frames:
        nears = jnp.maximum(nears, near_ref[which * (MAX_NEAR + 1) + MAX_NEAR])
        for r in range(FB):
            most = jnp.maximum(most, count_ref[which * FB + r])
    pairs = lax.div(most + 1, 2)

    def near_rows(which, w):
        return pl.ds(pl.multiple_of(near_ref[which * (MAX_NEAR + 1) + w] * ROWS, ROWS), ROWS)

    def far_rows(which, r, e):
        return pl.ds(pl.multiple_of(blocks_ref[which * FB + r, e] * BLK, BLK), BLK)

    top_s[...] = jnp.full_like(top_s, NEG)

    def near_scores(w, carry):
        for lane, (n, which) in enumerate(lanes):
            score = lax.dot_general(
                q_s[2 * n + which], k_s[n, near_rows(which, w), :], NT, preferred_element_type=jnp.float32
            )
            if len(frames) > 1:
                score = jnp.where(w < near_ref[which * (MAX_NEAR + 1) + MAX_NEAR], score, NEG)
            near_s[lane, w] = score
            best = jnp.maximum(jnp.maximum(score[:, :BLK], score[:, BLK : 2 * BLK]), score[:, 2 * BLK :])
            top_s[lane] = jnp.maximum(top_s[lane], best)
        return carry

    lax.fori_loop(0, nears, near_scores, 0)

    def far_scores(i, carry):
        for lane, (n, which) in enumerate(lanes):
            for r in range(FB):
                rows = slice(r * BLK, (r + 1) * BLK)
                best = top_s[lane, rows, :]
                for j in range(2):
                    e = 2 * i + j
                    score = lax.dot_general(
                        q_s[2 * n + which, rows, :], k_s[n, far_rows(which, r, e), :], NT, preferred_element_type=jnp.float32
                    )
                    score = jnp.where(e < count_ref[which * FB + r], score, NEG)
                    far_s[lane, r, e] = score
                    best = jnp.maximum(best, score)
                top_s[lane, rows, :] = best
        return carry

    lax.fori_loop(0, pairs, far_scores, 0)
    for lane in range(len(lanes)):
        top_s[lane] = jnp.broadcast_to(jnp.max(top_s[lane], axis=1, keepdims=True) * TO_EXP2, (ROWS, BLK))
    sum_s[...] = jnp.zeros_like(sum_s)

    def near_weights(w, carry):
        for lane, (n, which) in enumerate(lanes):
            top = top_s[lane]
            weights = [jnp.exp2(near_s[lane, w, :, c * BLK : (c + 1) * BLK] * TO_EXP2 - top) for c in range(FB)]
            weight = jnp.concatenate([p.astype(jnp.bfloat16) for p in weights], axis=1)
            sum_s[lane] += jnp.dot(weight, v_s[n, near_rows(which, w), :], preferred_element_type=jnp.float32)
        return carry

    lax.fori_loop(0, nears, near_weights, 0)

    def far_weights(i, carry):
        for lane, (n, which) in enumerate(lanes):
            for r in range(FB):
                rows = slice(r * BLK, (r + 1) * BLK)
                top = top_s[lane, rows, :]
                part = None
                for j in range(2):
                    weight = jnp.exp2(far_s[lane, r, 2 * i + j] * TO_EXP2 - top).astype(jnp.bfloat16)
                    value = v_s[n, far_rows(which, r, 2 * i + j), :]
                    added = jnp.dot(weight, value, preferred_element_type=jnp.float32)
                    part = added if part is None else part + added
                sum_s[lane, rows, :] += part
        return carry

    lax.fori_loop(0, pairs, far_weights, 0)
    for lane, (n, which) in enumerate(lanes):
        total = sum_s[lane, :, DH:]
        o_s[2 * n + which] = sum_s[lane, :, :DH] / total
        lse_s[2 * n + which] = top_s[lane] + jnp.log(total) * LOG2E


def attend_kernel(heads, first, planes, seq_ref, near_ref, blocks_ref, count_ref, q_ref, q_other_ref, *refs):
    piece_refs = refs[:planes]
    keep_o, keep_lse, send = refs[planes : planes + 3]
    q_s, o_s, lse_s, k_s, v_s, near_s, far_s, top_s, sum_s = refs[planes + 3 :]
    z = lax.div(seq_ref[0], 2)
    v_s[:, :, DH:] = jnp.ones((len(heads), planes * ROWS, DH), jnp.bfloat16)
    for d, piece in enumerate(piece_refs):
        rows = pl.ds(pl.multiple_of(lax.rem(z + planes - d, planes) * ROWS, ROWS), ROWS)
        for n in range(len(heads)):
            at = 2 * (first + n) * ROWS
            k_s[n, rows, :] = piece[at : at + ROWS, :]
            v_s[n, rows, 0:DH] = piece[at + ROWS : at + 2 * ROWS, :]
    for n, head in enumerate(heads):
        columns = slice(head * DH, (head + 1) * DH)
        q_s[2 * n] = q_ref[:, columns]
        q_s[2 * n + 1] = q_other_ref[:, columns]
    tables = (near_ref, blocks_ref, count_ref, q_s, o_s, lse_s, k_s, v_s, near_s, far_s, top_s, sum_s)
    if len(heads) == 1:
        attend_lanes([(0, 0), (0, 1)], *tables)
    else:

        def one(which, carry):
            attend_lanes([(n, which) for n in range(len(heads))], *tables)
            return carry

        lax.fori_loop(0, 2, one, 0)
    lane = lax.broadcasted_iota(jnp.int32, (ROWS, DH), 1)
    packed = jnp.zeros((ROWS, DH), jnp.float32)
    for n in range(len(heads)):
        rows = slice(n * ROWS, (n + 1) * ROWS)
        keep_o[rows, :] = o_s[2 * n]
        keep_lse[rows, :] = lse_s[2 * n]
        send[rows, :] = o_s[2 * n + 1].astype(jnp.bfloat16)
        left = lse_s[2 * n + 1]
        for term in range(TERMS):
            piece = left.astype(jnp.bfloat16).astype(jnp.float32)
            packed = jnp.where(lane == n * TERMS + term, piece, packed)
            left = left - piece
    send[len(heads) * ROWS :, :] = packed.astype(jnp.bfloat16)


def attend(heads, first, queries, queries_other, pieces, seq, near, blocks, counts):
    planes, held = len(pieces), len(heads)
    lanes = max(held, 2)
    tokens = planes * ROWS
    each = pltpu.VMEM((2 * held, ROWS, DH), jnp.float32)
    elements = held * ROWS * 18 * BLK
    return pl.pallas_call(
        functools.partial(attend_kernel, heads, first, planes),
        out_shape=[
            jax.ShapeDtypeStruct((held * ROWS, DH), jnp.float32),
            jax.ShapeDtypeStruct((held * ROWS, DH), jnp.float32),
            jax.ShapeDtypeStruct(((held + 1) * ROWS, DH), jnp.bfloat16),
        ],
        in_specs=[SMEM] * 4 + [VMEM] * (2 + planes),
        out_specs=[VMEM] * 3,
        scratch_shapes=[
            pltpu.VMEM((2 * held, ROWS, DH), jnp.bfloat16),
            each,
            each,
            pltpu.VMEM((held, tokens, DH), jnp.bfloat16),
            pltpu.VMEM((held, tokens, 2 * DH), jnp.bfloat16),
            pltpu.VMEM((lanes, MAX_NEAR, ROWS, ROWS), jnp.float32),
            pltpu.VMEM((lanes, FB, MAX_EXTRA, BLK, BLK), jnp.float32),
            pltpu.VMEM((lanes, ROWS, BLK), jnp.float32),
            pltpu.VMEM((lanes, ROWS, 2 * DH), jnp.float32),
        ],
        compiler_params=pltpu.CompilerParams(vmem_limit_bytes=(36 if held > 2 else 24) << 20),
        cost_estimate=pl.CostEstimate(
            flops=40 * elements * DH, bytes_accessed=4 * held * tokens * DH, transcendentals=elements
        ),
        name="attend",
    )(seq, near, blocks, counts, queries, queries_other, *pieces)


def merge_kernel(*refs):
    out_ref, parts = refs[-1], refs[:-1]
    column = 0
    for o_ref, lse_ref, got_ref in zip(parts[0::3], parts[1::3], parts[2::3]):
        held = o_ref.shape[0] // ROWS
        packed = got_ref[held * ROWS :, :].astype(jnp.float32)
        lane = lax.broadcasted_iota(jnp.int32, packed.shape, 1)
        for n in range(held):
            rows = slice(n * ROWS, (n + 1) * ROWS)
            other_o = got_ref[rows, :].astype(jnp.float32)
            terms = (lane >= n * TERMS) & (lane < (n + 1) * TERMS)
            other_lse = jnp.sum(jnp.where(terms, packed, 0.0), axis=1, keepdims=True)
            lse = lse_ref[rows, :]
            top = jnp.maximum(lse, other_lse)
            mine, other = jnp.exp2(lse - top), jnp.exp2(other_lse - top)
            out = ((o_ref[rows, :] * mine + other_o * other) / (mine + other)).astype(out_ref.dtype)
            out_ref[:, column : column + DH] = out
            column += DH


def merge(*parts):
    size = sum(part.size for part in parts[0::3])
    return pl.pallas_call(
        merge_kernel,
        out_shape=jax.ShapeDtypeStruct((ROWS, size // ROWS), jnp.bfloat16),
        in_specs=[VMEM] * len(parts),
        out_specs=VMEM,
        compiler_params=pltpu.CompilerParams(vmem_limit_bytes=10 << 20),
        cost_estimate=pl.CostEstimate(flops=8 * size, bytes_accessed=30 * size, transcendentals=2 * size),
        name="merge",
    )(*parts)


def tile_kernel(count, y_ref, pair_ref, weight_ref, *refs):
    outs, sems = refs[:-1], refs[-1]
    width = outs[0].shape[1]
    copies = []
    for n, out in enumerate(outs):
        block = pair_ref[0] if n < count else 1 - pair_ref[0]
        start = pl.multiple_of((lax.rem(y_ref[0] + n, count) * 2 + block) * width, width)
        copies.append(pltpu.make_async_copy(weight_ref.at[:, pl.ds(start, width)], out, sems.at[n]))
    for copy in copies:
        copy.start()
    for copy in copies:
        copy.wait()


def tile(y, pair, weight, count):
    stay = pl.BlockSpec(memory_space=pl.ANY)
    shape = (weight.shape[0], weight.shape[1] // (2 * count))
    return pl.pallas_call(
        functools.partial(tile_kernel, count),
        out_shape=[jax.ShapeDtypeStruct(shape, weight.dtype)] * (count + 1),
        in_specs=[SMEM, SMEM, stay],
        out_specs=[stay] * (count + 1),
        scratch_shapes=[pltpu.SemaphoreType.DMA((count + 1,))],
        compiler_params=pltpu.CompilerParams(vmem_limit_bytes=1 << 20),
        cost_estimate=pl.CostEstimate(flops=0, bytes_accessed=4 * weight.size, transcendentals=0),
        name="tile",
    )(y, pair, weight)


def cross_kernel(q_ref, k_ref, v_ref, o_ref):
    def one(h, carry):
        columns = pl.ds(pl.multiple_of(h * DH, DH), DH)
        score = lax.dot_general(q_ref[:, columns], k_ref[:, columns], NT, preferred_element_type=jnp.float32)
        top = jnp.max(score, axis=1, keepdims=True) * TO_EXP2
        weight = jnp.exp2(score * TO_EXP2 - top)
        total = jnp.sum(weight, axis=1, keepdims=True)
        part = jnp.dot(weight.astype(jnp.bfloat16), v_ref[:, columns], preferred_element_type=jnp.float32)
        o_ref[:, columns] = (part / total).astype(o_ref.dtype)
        return carry

    lax.fori_loop(0, q_ref.shape[1] // DH, one, 0)


def cross(cross_query, text_keys, text_values):
    elements = cross_query.shape[0] * cross_query.shape[1] // DH * text_keys.shape[0]
    return pl.pallas_call(
        cross_kernel,
        out_shape=jax.ShapeDtypeStruct(cross_query.shape, jnp.bfloat16),
        in_specs=[VMEM] * 3,
        out_specs=VMEM,
        compiler_params=pltpu.CompilerParams(vmem_limit_bytes=8 << 20),
        cost_estimate=pl.CostEstimate(
            flops=40 * elements * DH, bytes_accessed=4 * cross_query.size, transcendentals=elements
        ),
        name="cross",
    )(cross_query, text_keys, text_values)


def project_kernel(first, sources, last, *refs):
    keep_ref = refs[0] if last else None
    refs = refs[1:] if last else refs
    heads, weights, refs = refs[:sources], refs[sources : 3 * sources], refs[3 * sources :]
    depth = heads[0].shape[1]
    rows = slice(first * DH, first * DH + depth)
    total_ref = refs[-1]
    for block in range(2):
        total = refs[0][block] if len(refs) > 1 + 2 * last else None
        for head_ref, weight_ref in zip(heads, weights[block::2]):
            part = jnp.dot(head_ref[...], weight_ref[rows, :], preferred_element_type=jnp.float32)
            total = part if total is None else total + part
        total_ref[block] = total
    if last:
        refs[-3][...] = total_ref[keep_ref[0]]
        refs[-2][...] = total_ref[1 - keep_ref[0]].astype(jnp.bfloat16)


def project(first, heads, weights, before=None, keep=None):
    rows, depth = heads[0].shape
    width = weights[0].shape[1]
    given = [*heads, *weights] + ([] if before is None else [before])
    both = jax.ShapeDtypeStruct((2, rows, width), jnp.float32)
    split = [jax.ShapeDtypeStruct((rows, width), dtype) for dtype in (jnp.float32, jnp.bfloat16)]
    last = keep is not None
    return pl.pallas_call(
        functools.partial(project_kernel, first, len(heads), last),
        out_shape=split if last else both,
        in_specs=[SMEM] * last + [VMEM] * len(given),
        out_specs=[VMEM] * 2 if last else VMEM,
        scratch_shapes=[pltpu.VMEM(both.shape, both.dtype)] if last else [],
        compiler_params=pltpu.CompilerParams(vmem_limit_bytes=22 << 20),
        cost_estimate=pl.CostEstimate(
            flops=4 * len(heads) * rows * depth * width,
            bytes_accessed=2 * len(heads) * depth * (rows + 2 * width),
            transcendentals=0,
        ),
        name="project",
    )(*([keep] if last else []), *given)


def body(n_seq, n_head, queries, keys, values, cross_query, text_keys, text_values, out_weight, block_list, block_count):
    n_z, n_y = n_seq // 2, n_head // 2
    seq = lax.axis_index("seq").reshape(1)
    head = lax.axis_index("head").reshape(1)
    pair = lax.axis_index("pair").reshape(1)
    cross_heads = cross(cross_query, text_keys, text_values)
    swap = [(s, s ^ 1) for s in range(n_seq)]

    def to_other(array):
        return lax.ppermute(array, "seq", swap)

    def z_shift(step):
        return [(s, (s // 2 + step) % n_z * 2 + s % 2) for s in range(n_seq)]

    def y_shift(step):
        return [(g, (g // 2 + step) % n_y * 2 + g % 2) for g in range(n_head)]

    held = [{0: array} for array in pack(keys, values)]
    sent = {1: [], -1: []}

    def hop(way, group, step, after=None):
        done = sent[way]
        array = held[group][way * (step - 1) % n_z]
        if len(done) >= IN_FLIGHT:
            at, where = done[-IN_FLIGHT]
            array, held[at][where] = lax.optimization_barrier((array, held[at][where]))
        if after is not None:
            array, after[0] = lax.optimization_barrier((array, after[0]))
        place = way * step % n_z
        held[group][place] = lax.ppermute(array, "seq", z_shift(way))
        done.append((group, place))

    def partial(group, start, stop):
        pieces = [held[group][d] for d in range(n_z)]
        return list(attend(GROUPS[group][start:stop], start, queries, queries_other, pieces, seq, near, blocks, counts))

    def join(*parts):
        return merge(*(array for part in parts for array in (*part[:2], to_other(part[2]))))

    def along_y(array):
        return [array] + [lax.ppermute(array, "head", y_shift(-dy)) for dy in range(1, n_y)]

    for group in (0, 1):
        hop(1, group, 1)
        hop(-1, group, 1)
    queries_other = to_other(queries)
    early = list(plan(n_seq, seq, block_list, block_count))
    tiles = list(tile(lax.div(head, 2), pair, out_weight, n_y))
    early[0], tiles[0], queries_other = lax.optimization_barrier((early[0], tiles[0], queries_other))
    hop(1, 0, 2)
    hop(-1, 0, 2)
    arrived = [lax.ppermute(tiles[dy], "head", y_shift(dy)) for dy in (1, n_y - 1)]
    arrived[1], tiles[2] = lax.optimization_barrier((arrived[1], tiles[2]))
    tiles[1:n_y] = [arrived[1], lax.ppermute(tiles[2], "head", y_shift(2)), arrived[0]]
    hop(1, 1, 2)
    one_away = [(tiles[1], tiles[n_y - 1])]
    hop(1, 0, 3, one_away)
    tiles[1], tiles[n_y - 1] = one_away[0]
    hop(-1, 0, 3, early)
    blocks, counts, near = early
    hop(1, 0, 4)
    hop(-1, 1, 2)
    hop(-1, 1, 3)
    hop(1, 1, 3)
    hop(-1, 1, 4)
    near, tiles[2] = lax.optimization_barrier((near, tiles[2]))
    weights = [tiles[0], tiles[n_y]]
    for mine in tiles[1:n_y]:
        weights += [mine, lax.ppermute(mine, "pair", [(0, 1), (1, 0)])]
    most = partial(0, 0, 3)
    near, *weights = lax.optimization_barrier((near, *weights))
    rest = partial(1, 0, 2)
    most[0], rest[0] = lax.optimization_barrier((most[0], rest[0]))
    before = project(GROUPS[0][0], along_y(join(most)), weights)
    rest = join(rest)
    keep_block = (lax.rem(head, 2) != pair).astype(jnp.int32)
    keep, send = project(GROUPS[1][0], along_y(rest), weights, before, keep_block)
    got = lax.ppermute(send, "head", [(g, g ^ 1) for g in range(n_head)])
    return (keep + got.astype(jnp.float32)).astype(jnp.bfloat16), cross_heads


def solution(mesh):
    rows = P(("pair", "seq"), "head")
    text = P("pair", "head")
    return jax.shard_map(
        functools.partial(body, mesh.shape["seq"], mesh.shape["head"]),
        mesh=mesh,
        in_specs=(rows, rows, rows, rows, text, text, P("head", None), P(), P()),
        out_specs=(rows, rows),
        check_vma=False,
    )
```
